256 devices in a mesh: req: 8 (over z_lo, core), tile: 16 (over x, y), blk: 2 (over z_hi).
Axes of the slice: x: 4, y: 4, z: 8 (z_hi: 2, z_lo: 4; z = z_hi * 4 + z_lo), core: 2. Of those that a mesh axis runs over, the one named last changes fastest.
Arguments:
- image_tokens: bfloat16 [16, 1024, 1536], P(('req', 'blk'), 'tile'), may hold values from -6 to 6
- latent: float32 [16, 512, 128], P(('req', 'blk'), 'tile'), may hold values from -6 to 6
- modulation: float32 [16, 8, 1536], P(('req', 'blk')), may hold values from -3 to 3
- text_kv: bfloat16 [16, 154, 2, 1536], P(('req', 'blk')), as said below
- text_len: int32 [16], P(('req', 'blk')), may hold values from 38 to 154, as said below
- timestep: int32 [16], P(('req', 'blk')), may hold values from 0 to 7
- w_qkv: bfloat16 [1536, 3, 1536], P(None, None, 'tile'), may hold values from -0.15625 to 0.15625
- w_out: bfloat16 [1536, 1536], P('tile'), may hold values from -0.15625 to 0.15625
- w_up: bfloat16 [1536, 6144], P(None, 'tile'), may hold values from -0.15625 to 0.15625
- w_down: bfloat16 [6144, 1536], P('tile'), may hold values from -0.078125 to 0.078125
- w_final: bfloat16 [1536, 64], replicated, may hold values from -0.15625 to 0.15625
Outputs:
- image_state: bfloat16 [16, 1024, 1536], P(('req', 'blk'), 'tile')
- latent_next: float32 [16, 512, 128], P(('req', 'blk'), 'tile')
The draws below stay inside these ranges and needn't reach their ends.
Inputs may be any that keep to these rules, and one draw needn't show every extreme that they name: `text_len`: each request has 38 to 154 live text tokens; some request has 154 and some 154 // 4. `text_kv`: keys and values of text tokens, finite.
All inputs are finite; a program needn't handle non-finite values.
Results may differ from the reference program's by a relative error of at most 0.014.
Values may be sent and summed in bfloat16 or wider, within the bound.
No kernel may reach another device: no remote copies, remote signals or barrier semaphores. Data moves between devices by JAX's collectives and lax.ppermute only.
A program may use at most 64 MiB of HBM per device.

```python
import jax
import jax.numpy as jnp
from jax import lax

D = 1536
HEADS = 24
HEAD_DIM = 64
FF = 6144
PATCH = 64
TXT = 154
STEPS = 8
IMG = 1024
REQS = 16


def draw_text_kv(key, part):
    first = jax.random.fold_in(key, 0)
    base = jax.random.normal(first, (REQS, TXT, 2, D), jnp.float32)
    return jnp.clip(base, -200.0, 200.0).astype(jnp.bfloat16)


def draw_text_len(key, part):
    first, second = jax.random.split(key)
    lengths = jax.random.randint(first, (REQS,), TXT // 4, TXT + 1)
    order = jax.random.permutation(second, REQS)
    lengths = lengths.at[order[0]].set(TXT)
    lengths = lengths.at[order[1]].set(TXT // 4)
    return lengths.astype(jnp.int32)


def touch_ends(drawn, rng, low, largest):
    spot = [jax.random.randint(jax.random.fold_in(rng, axis), (), 0, length) for axis, length in enumerate(drawn.shape)]
    longest = drawn.shape.index(max(drawn.shape))
    next_to = spot[:longest] + [(spot[longest] + 1) % drawn.shape[longest]] + spot[longest + 1:]
    return drawn.at[tuple(spot)].set(low).at[tuple(next_to)].set(largest)


def shard_levels(own_key, shape, pieces, least, largest):
    def one(dim, parts):
        heights = jax.random.uniform(jax.random.fold_in(jax.random.fold_in(own_key, 6), dim), (parts,), jnp.float32, least / len(pieces), largest / len(pieces))
        return jnp.repeat(jnp.exp(heights), shape[dim] // parts).reshape((-1,) + (1,) * (len(shape) - dim - 1))

    level = one(*pieces[0])
    for cut in pieces[1:]:
        level = level * one(*cut)
    return level


def centred(key, extent, scale, reach, pieces=(), kind=jnp.bfloat16):
    values = scale * jax.random.normal(key, extent, jnp.float32)
    if pieces:
        values = values * shard_levels(key, extent, pieces, -0.22, 0.18)
    return jnp.clip(values, -reach, reach).astype(kind)


def setup_inputs(seed: int = 0) -> dict:
    seeds = jax.random.split(jax.random.key(seed), 12)
    return {
        "image_tokens": centred(seeds[0], (REQS, IMG, D), 1.0, 6.0, ((0, 16), (1, 16))),
        "latent": centred(seeds[1], (REQS, IMG // 2, 2 * PATCH), 1.0, 6.0, ((0, 16), (1, 16)), jnp.float32),
        "modulation": centred(seeds[2], (REQS, 8, D), 0.5, 3.0, ((0, 16),), jnp.float32),
        "text_kv": draw_text_kv(jax.random.fold_in(seeds[11], 71), 0),
        "text_len": draw_text_len(jax.random.fold_in(seeds[11], 71), 0),
        "timestep": touch_ends(jax.random.randint(seeds[5], (REQS,), 0, STEPS), jax.random.fold_in(seeds[5], 1), 0, STEPS - 1).astype(jnp.int32),
        "w_qkv": centred(seeds[6], (D, 3, D), D ** -0.5, 0.15625, ((2, 16),)),
        "w_out": centred(seeds[7], (D, D), D ** -0.5, 0.15625, ((0, 16),)),
        "w_up": centred(seeds[8], (D, FF), D ** -0.5, 0.15625, ((1, 16),)),
        "w_down": centred(seeds[9], (FF, D), FF ** -0.5, 0.078125, ((0, 16),)),
        "w_final": centred(seeds[10], (D, PATCH), D ** -0.5, 0.15625),
    }


def normed(value, shift, scale):
    full = value.astype(jnp.float32)
    mean = lax.optimization_barrier(jnp.mean(full, axis=-1, keepdims=True))
    spread = lax.optimization_barrier(jnp.mean(jnp.square(full - mean), axis=-1, keepdims=True))
    return (full - mean) * lax.rsqrt(spread + 1e-06) * (1.0 + scale) + shift

def sigma_at(index):
    frac = 1.0 - index.astype(jnp.float32) / STEPS
    return 3.0 * frac / (1.0 + 2.0 * frac)

def one_request(packed, w_qkv, w_out, w_up, w_down, w_final):
    tokens, latent_rows, mods, text_pair, length, step = packed
    h1 = normed(tokens, mods[0], mods[1]).astype(jnp.bfloat16)
    qkv = jnp.einsum('nd,dkc->nkc', h1.astype(jnp.float32), w_qkv.astype(jnp.float32)).astype(jnp.bfloat16)
    query = qkv[:, 0].reshape(IMG, HEADS, HEAD_DIM).astype(jnp.float32)
    keys = jnp.concatenate([qkv[:, 1], text_pair[:, 0]], axis=0).reshape(IMG + TXT, HEADS, HEAD_DIM).astype(jnp.float32)
    values = jnp.concatenate([qkv[:, 2], text_pair[:, 1]], axis=0).reshape(IMG + TXT, HEADS, HEAD_DIM).astype(jnp.float32)
    live = jnp.concatenate([jnp.ones((IMG,), bool), jnp.arange(TXT, dtype=jnp.int32) < length])
    scores = jnp.einsum('qhe,khe->hqk', query, keys) * HEAD_DIM ** (-0.5)
    scores = jnp.where(live[None, None, :], scores, -jnp.inf)
    top = lax.optimization_barrier(jnp.max(scores, axis=-1, keepdims=True))
    weights = jnp.exp(scores - top)
    total = lax.optimization_barrier(jnp.sum(weights, axis=-1))
    rounded = weights.astype(jnp.bfloat16).astype(jnp.float32)
    summed = jnp.einsum('hqk,khe->hqe', rounded, values) / total[:, :, None]
    attended = jnp.transpose(summed, (1, 0, 2)).reshape(IMG, D).astype(jnp.bfloat16)
    proj = jnp.dot(attended, w_out, preferred_element_type=jnp.float32)
    second = (tokens.astype(jnp.float32) + mods[2] * proj).astype(jnp.bfloat16)
    h2 = normed(second, mods[3], mods[4]).astype(jnp.bfloat16)
    hidden = jax.nn.gelu(jnp.dot(h2, w_up, preferred_element_type=jnp.float32), approximate=True).astype(jnp.bfloat16)
    ffn = jnp.dot(hidden, w_down, preferred_element_type=jnp.float32)
    state = (second.astype(jnp.float32) + mods[5] * ffn).astype(jnp.bfloat16)
    final_in = normed(state, mods[6], mods[7]).astype(jnp.bfloat16)
    velocity = jnp.dot(final_in, w_final, preferred_element_type=jnp.float32)
    delta = sigma_at(step + 1) - sigma_at(step)
    moved = latent_rows + delta * velocity.reshape(IMG // 2, 2 * PATCH)
    return (state, moved)

def reference(image_tokens, latent, modulation, text_kv, text_len, timestep, w_qkv, w_out, w_up, w_down, w_final):

    def apply_one(packed):
        return one_request(packed, w_qkv, w_out, w_up, w_down, w_final)
    state, moved = lax.map(apply_one, (image_tokens, latent, modulation, text_kv, text_len, timestep))
    return (state, moved)
```

```python
import functools

import jax
import jax.numpy as jnp
from jax import lax
from jax.experimental import pallas as pl
from jax.experimental.pallas import tpu as pltpu
from jax.sharding import Mesh, PartitionSpec as P

HEAD_DIM = 64
TXT = 154
STEPS = 8
BF = jnp.bfloat16
F32 = jnp.float32
NT = (((1,), (1,)), ((), ()))
NN = (((1,), (0,)), ((), ()))


def params():
    return pltpu.CompilerParams(vmem_limit_bytes=50 * 1024 * 1024)


def layer_norm(full, shift, scale):
    mean = jnp.mean(full, axis=-1, keepdims=True)
    cent = full - mean
    spread = jnp.mean(jnp.square(cent), axis=-1, keepdims=True)
    return cent * lax.rsqrt(spread + 1e-06) * (1.0 + scale) + shift


def sigma_at(index):
    frac = 1.0 - index.astype(F32) / STEPS
    return 3.0 * frac / (1.0 + 2.0 * frac)


def norm_kernel(copies, x_ref, mod_ref, out_ref):
    h = layer_norm(x_ref[...].astype(F32), mod_ref[0:1, :], mod_ref[1:2, :]).astype(BF)
    for i in range(copies):
        out_ref[i] = h


def first_norm(tokens, mods, copies):
    rows, width = tokens.shape
    return pl.pallas_call(
        functools.partial(norm_kernel, copies),
        out_shape=jax.ShapeDtypeStruct((copies, rows, width), BF),
        compiler_params=params(),
        name="first_norm",
    )(tokens, mods)


def qkv_kernel(pos_ref, h_ref, own_ref, near_ref, far_ref, out_ref, w_ref):
    side = pos_ref[0]
    core = pos_ref[1]
    for k in range(3):
        w_ref[k, side, 0] = own_ref[k, 0:48, :]
        w_ref[k, side, 1] = own_ref[k, 48:96, :]
        w_ref[k, 1 - side, core] = near_ref[k]
        w_ref[k, 1 - side, 1 - core] = far_ref[k]
    h = h_ref[...]
    for k in range(3):
        w = w_ref[k].reshape(192, h.shape[1])
        out_ref[k] = lax.dot_general(h, w, NT, preferred_element_type=F32).astype(BF)


def project_qkv(pos, h, own, near, far):
    rows, width = h.shape
    return pl.pallas_call(
        qkv_kernel,
        out_shape=jax.ShapeDtypeStruct((3, rows, 192), BF),
        in_specs=[pl.BlockSpec(memory_space=pltpu.SMEM)]
        + [pl.BlockSpec(memory_space=pltpu.VMEM)] * 4,
        scratch_shapes=[pltpu.VMEM((3, 2, 2, 48, width), BF)],
        compiler_params=params(),
        name="project_qkv",
    )(pos, h, own, near, far)


QB = 256


def own_attention_kernel(len_ref, q_ref, kv_ref, text_ref, acc_ref, top_ref, tot_ref):
    lane = lax.broadcasted_iota(jnp.int32, (QB, 192), 1) // HEAD_DIM
    live = lax.broadcasted_iota(jnp.int32, (QB, TXT), 1) < len_ref[0]
    keys = kv_ref[0]
    values = kv_ref[1]
    tkeys = text_ref[0]
    tvalues = text_ref[1]
    for b in range(q_ref.shape[0] // QB):
        rows = pl.ds(b * QB, QB)
        q = q_ref[rows, :]
        acc = jnp.zeros((QB, 192), F32)
        tops = jnp.zeros((QB, 192), F32)
        tots = jnp.zeros((QB, 192), F32)
        for h in range(3):
            here = lane == h
            qh = jnp.where(here, q, jnp.zeros_like(q))
            s = lax.dot_general(qh, keys, NT, preferred_element_type=F32) * 0.125
            st = lax.dot_general(qh, tkeys, NT, preferred_element_type=F32) * 0.125
            st = jnp.where(live, st, -jnp.inf)
            top = jnp.maximum(
                jnp.max(s, axis=1, keepdims=True), jnp.max(st, axis=1, keepdims=True)
            )
            p = jnp.exp(s - top)
            pt = jnp.exp(st - top)
            tot = jnp.sum(p, axis=1, keepdims=True) + jnp.sum(pt, axis=1, keepdims=True)
            part = lax.dot_general(p.astype(BF), values, NN, preferred_element_type=F32)
            part += lax.dot_general(pt.astype(BF), tvalues, NN, preferred_element_type=F32)
            acc = jnp.where(here, part, acc)
            tops = jnp.where(here, top, tops)
            tots = jnp.where(here, tot, tots)
        acc_ref[rows, :] = acc
        top_ref[rows, :] = tops
        tot_ref[rows, :] = tots


def own_attention(length, q, kv, text):
    rows = q.shape[0]
    return pl.pallas_call(
        own_attention_kernel,
        out_shape=[jax.ShapeDtypeStruct((rows, 192), F32)] * 3,
        in_specs=[pl.BlockSpec(memory_space=pltpu.SMEM)]
        + [pl.BlockSpec(memory_space=pltpu.VMEM)] * 3,
        compiler_params=params(),
        name="own_attention",
    )(length, q, kv, text)


def far_attention_kernel(q_ref, kv_ref, acc_ref, top_ref, tot_ref, out_ref):
    lane = lax.broadcasted_iota(jnp.int32, (QB, 192), 1) // HEAD_DIM
    keys = kv_ref[0]
    values = kv_ref[1]
    for b in range(q_ref.shape[0] // QB):
        rows = pl.ds(b * QB, QB)
        q = q_ref[rows, :]
        tops = top_ref[rows, :]
        acc = jnp.zeros((QB, 192), F32)
        new_tops = tops
        tots = jnp.zeros((QB, 192), F32)
        for h in range(3):
            here = lane == h
            qh = jnp.where(here, q, jnp.zeros_like(q))
            s = lax.dot_general(qh, keys, NT, preferred_element_type=F32) * 0.125
            old = tops[:, h * HEAD_DIM : h * HEAD_DIM + 1]
            top = jnp.maximum(jnp.max(s, axis=1, keepdims=True), old)
            p = jnp.exp(s - top)
            tot = jnp.sum(p, axis=1, keepdims=True)
            part = lax.dot_general(p.astype(BF), values, NN, preferred_element_type=F32)
            acc = jnp.where(here, part, acc)
            new_tops = jnp.where(here, top, new_tops)
            tots = jnp.where(here, tot, tots)
        factor = jnp.exp(tops - new_tops)
        total = tot_ref[rows, :] * factor + tots
        out_ref[rows, :] = ((acc_ref[rows, :] * factor + acc) / total).astype(BF)


def far_attention(q, kv, acc, top, tot):
    return pl.pallas_call(
        far_attention_kernel,
        out_shape=jax.ShapeDtypeStruct(q.shape, BF),
        compiler_params=params(),
        name="far_attention",
    )(q, kv, acc, top, tot)


def out_kernel(a_ref, w_ref, out_ref):
    out_ref[...] = lax.dot_general(
        a_ref[...], w_ref[...], NN, preferred_element_type=F32
    ).astype(BF)


def out_projection(a, w):
    return pl.pallas_call(
        out_kernel,
        out_shape=jax.ShapeDtypeStruct((a.shape[0], w.shape[1]), BF),
        compiler_params=params(),
        name="out_projection",
    )(a, w)


def second_norm_kernel(x_ref, part_ref, mod_ref, second_ref, out_ref):
    proj = part_ref[0].astype(F32)
    for i in range(1, part_ref.shape[0]):
        proj += part_ref[i].astype(F32)
    second = (x_ref[...].astype(F32) + mod_ref[2:3, :] * proj).astype(BF)
    second_ref[...] = second
    h = layer_norm(second.astype(F32), mod_ref[3:4, :], mod_ref[4:5, :]).astype(BF)
    for i in range(out_ref.shape[0]):
        out_ref[i] = h


def second_norm(tokens, parts, mods):
    return pl.pallas_call(
        second_norm_kernel,
        out_shape=[
            jax.ShapeDtypeStruct(tokens.shape, BF),
            jax.ShapeDtypeStruct(parts.shape, BF),
        ],
        compiler_params=params(),
        name="second_norm",
    )(tokens, parts, mods)


def ffn_kernel(h_ref, up_ref, down_ref, out_ref, acc_ref):
    step = pl.program_id(0)
    part = up_ref.shape[-1]
    hidden = jax.nn.gelu(
        lax.dot_general(h_ref[...], up_ref[0, 0], NN, preferred_element_type=F32),
        approximate=True,
    ).astype(BF)
    for s in range(4):
        value = lax.dot_general(
            hidden,
            down_ref[0, 0, s * part : (s + 1) * part, :],
            NN,
            preferred_element_type=F32,
        )
        cols = slice(s * part, (s + 1) * part)

        @pl.when(step == 0)
        def _():
            acc_ref[:, cols] = value

        @pl.when(step > 0)
        def _():
            acc_ref[:, cols] += value

    @pl.when(step == pl.num_programs(0) - 1)
    def _():
        out_ref[...] = acc_ref[...].astype(BF)


def feed_forward(h, weights):
    rows, width = h.shape
    part = weights.shape[3]
    return pl.pallas_call(
        ffn_kernel,
        grid=(4,),
        out_shape=jax.ShapeDtypeStruct((rows, width), BF),
        in_specs=[
            pl.BlockSpec((rows, width), lambda i: (0, 0)),
            pl.BlockSpec((1, 1, width, part), lambda i: (0, i, 0, 0)),
            pl.BlockSpec((1, 1, width, part), lambda i: (1, i, 0, 0)),
        ],
        out_specs=pl.BlockSpec((rows, width), lambda i: (0, 0)),
        scratch_shapes=[pltpu.VMEM((rows, width), F32)],
        compiler_params=params(),
        name="feed_forward",
    )(h, weights, weights)


def last_kernel(second_ref, part_ref, mod_ref, w_ref, state_ref, vel_ref):
    ffn = part_ref[0].astype(F32)
    for i in range(1, part_ref.shape[0]):
        ffn += part_ref[i].astype(F32)
    state = (second_ref[...].astype(F32) + mod_ref[5:6, :] * ffn).astype(BF)
    state_ref[...] = state
    h = layer_norm(state.astype(F32), mod_ref[6:7, :], mod_ref[7:8, :]).astype(BF)
    vel_ref[...] = lax.dot_general(h, w_ref[...], NN, preferred_element_type=F32)


def last_stage(second, parts, mods, w_final):
    return pl.pallas_call(
        last_kernel,
        out_shape=[
            jax.ShapeDtypeStruct(second.shape, BF),
            jax.ShapeDtypeStruct((second.shape[0], w_final.shape[1]), F32),
        ],
        compiler_params=params(),
        name="last_stage",
    )(second, parts, mods, w_final)


def on_device(
    image_tokens,
    latent,
    modulation,
    text_kv,
    text_len,
    timestep,
    w_qkv,
    w_out,
    w_up,
    w_down,
    w_final,
):
    tokens = image_tokens[0]
    mods = modulation[0]
    rows, width = tokens.shape
    core = lax.axis_index("core")
    side = lax.axis_index("yl")
    high = lax.axis_index("yh")
    swap2 = [(0, 1), (1, 0)]

    own_qkv = jnp.transpose(w_qkv, (1, 2, 0))
    half_qkv = lax.dynamic_slice_in_dim(own_qkv, core * 48, 48, 1)
    near_qkv = lax.ppermute(half_qkv, "yl", swap2)
    far_qkv = lax.ppermute(near_qkv, "core", swap2)

    half_out = lax.dynamic_slice_in_dim(w_out, core * 48, 48, 0)
    out_full = lax.all_gather(half_out, ("yh", "yl", "core"), axis=0, tiled=True)

    part = w_up.shape[1]
    slabs = jnp.transpose(w_down.reshape(part, 4, part), (1, 0, 2)).reshape(width, part)
    half_ffn = jnp.where(core == 0, w_up, slabs)
    ffn_full = lax.all_gather(half_ffn, ("core", "yh", "yl"), axis=0, tiled=False)
    ffn_full = ffn_full.reshape(2, 4, width, part)

    h1 = first_norm(tokens, mods, 8)
    h1 = lax.all_to_all(h1, ("tx", "yh"), split_axis=0, concat_axis=0, tiled=True)
    h1 = h1.reshape(8 * rows, width)
    pos = jnp.stack([side, core]).astype(jnp.int32)
    qkv = project_qkv(pos, h1, own_qkv, near_qkv, far_qkv)
    kv_far = lax.ppermute(qkv[1:], "yl", swap2)

    head_cols = (lax.axis_index("tx") * 2 + high) * 192
    text = lax.dynamic_slice_in_dim(text_kv[0], head_cols, 192, 2)
    text = jnp.transpose(text, (1, 0, 2))
    acc, top, tot = own_attention(text_len, qkv[0], qkv[1:], text)
    attended = far_attention(qkv[0], kv_far, acc, top, tot)

    lines = attended.reshape(4, 2, rows, 192)
    mine = lax.dynamic_index_in_dim(lines, high, 1, False)
    other = lax.dynamic_index_in_dim(lines, 1 - high, 1, False)
    got = lax.ppermute(other, "yh", swap2)
    low = jnp.where(high == 0, mine, got)
    upper = jnp.where(high == 0, got, mine)
    joined = jnp.concatenate([low, upper], axis=2).reshape(4 * rows, 384)

    partial = out_projection(joined, out_full).reshape(4, rows, width)
    partial = lax.all_to_all(partial, "tx", split_axis=0, concat_axis=0, tiled=True)
    second, h2 = second_norm(tokens, partial, mods)
    h2 = lax.all_to_all(h2, "tx", split_axis=0, concat_axis=0, tiled=True)
    partial = feed_forward(h2.reshape(4 * rows, width), ffn_full).reshape(4, rows, width)
    partial = lax.all_to_all(partial, "tx", split_axis=0, concat_axis=0, tiled=True)
    state, velocity = last_stage(second, partial, mods, w_final)

    step_index = timestep[0]
    delta = sigma_at(step_index + 1) - sigma_at(step_index)
    moved = latent[0] + delta * velocity.reshape(rows // 2, 2 * velocity.shape[1])
    return (state[None], moved[None])


def solution(mesh):
    fine = Mesh(
        mesh.devices.reshape(mesh.shape["req"] // 2, 2, 4, 2, 2, mesh.shape["blk"]),
        ("zl", "core", "tx", "yh", "yl", "blk"),
    )
    group = ("zl", "core", "blk")
    tile = ("tx", "yh", "yl")
    in_specs = (
        P(group, tile, None),
        P(group, tile, None),
        P(group, None, None),
        P(group, None, None, None),
        P(group),
        P(group),
        P(None, None, tile),
        P(tile, None),
        P(None, tile),
        P(tile, None),
        P(),
    )
    out_specs = (P(group, tile, None), P(group, tile, None))
    return jax.shard_map(
        on_device, mesh=fine, in_specs=in_specs, out_specs=out_specs, check_vma=False
    )
```

```python
import functools

import jax
import jax.numpy as jnp
from jax import lax
from jax.experimental import pallas as pl
from jax.experimental.pallas import tpu as pltpu
from jax.sharding import Mesh, PartitionSpec as P

HEAD_DIM = 64
TXT = 154
STEPS = 8
BF = jnp.bfloat16
F32 = jnp.float32
NT = (((1,), (1,)), ((), ()))
NN = (((1,), (0,)), ((), ()))
STRIDES = (1, 3, 2)


def params():
    return pltpu.CompilerParams(vmem_limit_bytes=50 * 1024 * 1024)


def layer_norm(full, shift, scale):
    mean = jnp.mean(full, axis=-1, keepdims=True)
    cent = full - mean
    spread = jnp.mean(jnp.square(cent), axis=-1, keepdims=True)
    return cent * lax.rsqrt(spread + 1e-06) * (1.0 + scale) + shift


def sigma_at(index):
    frac = 1.0 - index.astype(F32) / STEPS
    return 3.0 * frac / (1.0 + 2.0 * frac)


def norm_kernel(copies, x_ref, mod_ref, out_ref):
    h = layer_norm(x_ref[...].astype(F32), mod_ref[0:1, :], mod_ref[1:2, :]).astype(BF)
    for i in range(copies):
        out_ref[i] = h


def first_norm(tokens, mods, copies):
    rows, width = tokens.shape
    return pl.pallas_call(
        functools.partial(norm_kernel, copies),
        out_shape=jax.ShapeDtypeStruct((copies, rows, width), BF),
        compiler_params=params(),
        name="first_norm",
    )(tokens, mods)


def assemble(pos_ref, own_ref, near_refs, far_ref, store):
    core = pos_ref[0]
    row = pos_ref[1]
    store(row, 0, own_ref, 0)
    store(row, 1, own_ref, 1)
    for i, (near_ref, step) in enumerate(zip(near_refs, STRIDES)):
        source = lax.rem(row + 4 - step, 4)
        store(source, core, near_ref, None)
        store(source, 1 - core, far_ref, i)


def qkv_kernel(pos_ref, h_ref, own_ref, n0_ref, n1_ref, n2_ref, far_ref, q_ref, kv_ref, w_ref):
    def store(source, half, ref, index):
        for k in range(3):
            if ref is own_ref:
                value = ref[k, index * 48 : index * 48 + 48, :]
            elif index is None:
                value = ref[k]
            else:
                value = ref[index, k]
            w_ref[k, source, half] = value

    assemble(pos_ref, own_ref, (n0_ref, n1_ref, n2_ref), far_ref, store)
    h = h_ref[...]
    for k in range(3):
        w = w_ref[k].reshape(384, h.shape[1])
        value = lax.dot_general(h, w, NT, preferred_element_type=F32).astype(BF)
        if k == 0:
            q_ref[...] = value
        else:
            kv_ref[k - 1] = value


def project_qkv(pos, h, own, near, far):
    rows, width = h.shape
    return pl.pallas_call(
        qkv_kernel,
        out_shape=[
            jax.ShapeDtypeStruct((rows, 384), BF),
            jax.ShapeDtypeStruct((2, rows, 384), BF),
        ],
        in_specs=[pl.BlockSpec(memory_space=pltpu.SMEM)]
        + [pl.BlockSpec(memory_space=pltpu.VMEM)] * 6,
        scratch_shapes=[pltpu.VMEM((3, 4, 2, 48, width), BF)],
        compiler_params=params(),
        name="project_qkv",
    )(pos, h, own, *near, far)


def attention_kernel(chunks, has_text, has_state, last, *refs):
    refs = list(refs)
    len_ref = refs.pop(0) if has_text else None
    q_ref = refs.pop(0)
    kv_refs = [refs.pop(0) for _ in range(chunks)]
    text_ref = refs.pop(0) if has_text else None
    state_refs = [refs.pop(0) for _ in range(3)] if has_state else None
    rows = q_ref.shape[0]
    if has_text:
        live = lax.broadcasted_iota(jnp.int32, (rows, TXT), 1) < len_ref[0]
    first = lax.broadcasted_iota(jnp.int32, (rows, 128), 1) < HEAD_DIM
    for g in range(q_ref.shape[1] // 128):
        cols = slice(g * 128, g * 128 + 128)
        q = q_ref[:, cols]
        sides = []
        for side in range(2):
            here = first if side == 0 else jnp.logical_not(first)
            qh = jnp.where(here, q, jnp.zeros_like(q))
            parts = []
            for ref in kv_refs:
                s = lax.dot_general(qh, ref[0, :, cols], NT, preferred_element_type=F32) * 0.125
                parts.append((s, ref[1, :, cols]))
            if has_text:
                s = (
                    lax.dot_general(qh, text_ref[0, :, cols], NT, preferred_element_type=F32)
                    * 0.125
                )
                parts.append((jnp.where(live, s, -jnp.inf), text_ref[1, :, cols]))
            top = None
            for s, _ in parts:
                peak = jnp.max(s, axis=1, keepdims=True)
                top = peak if top is None else jnp.maximum(top, peak)
            if has_state:
                lane = g * 128 + side * HEAD_DIM
                top = jnp.maximum(top, state_refs[1][:, lane : lane + 1])
            total = None
            acc = None
            for s, values in parts:
                p = jnp.exp(s - top)
                amount = jnp.sum(p, axis=1, keepdims=True)
                part = lax.dot_general(p.astype(BF), values, NN, preferred_element_type=F32)
                total = amount if total is None else total + amount
                acc = part if acc is None else acc + part
            sides.append((acc, top, total))
        acc = jnp.where(first, sides[0][0], sides[1][0])
        top = jnp.where(first, sides[0][1], sides[1][1])
        total = jnp.where(first, sides[0][2], sides[1][2])
        if has_state:
            factor = jnp.exp(state_refs[1][:, cols] - top)
            acc = acc + state_refs[0][:, cols] * factor
            total = total + state_refs[2][:, cols] * factor
        if last:
            refs[0][:, cols] = (acc / total).astype(BF)
        else:
            refs[0][:, cols] = acc
            refs[1][:, cols] = top
            refs[2][:, cols] = total


def attention(q, kvs, text=None, length=None, state=None, last=False):
    args = []
    specs = []
    if text is not None:
        args.append(length)
        specs.append(pl.BlockSpec(memory_space=pltpu.SMEM))
    rest = [q, *kvs] + ([text] if text is not None else []) + list(state or [])
    args += rest
    specs += [pl.BlockSpec(memory_space=pltpu.VMEM)] * len(rest)
    if last:
        out = jax.ShapeDtypeStruct(q.shape, BF)
    else:
        out = [jax.ShapeDtypeStruct(q.shape, F32)] * 3
    return pl.pallas_call(
        functools.partial(
            attention_kernel, len(kvs), text is not None, state is not None, last
        ),
        out_shape=out,
        in_specs=specs,
        compiler_params=params(),
        name="attention",
    )(*args)


def out_kernel(pos_ref, a_ref, own_ref, n0_ref, n1_ref, n2_ref, far_ref, out_ref, w_ref):
    def store(source, half, ref, index):
        if ref is own_ref:
            value = ref[index * 48 : index * 48 + 48, :]
        elif index is None:
            value = ref[...]
        else:
            value = ref[index]
        w_ref[source, half] = value

    assemble(pos_ref, own_ref, (n0_ref, n1_ref, n2_ref), far_ref, store)
    w = w_ref[...].reshape(384, out_ref.shape[1])
    out_ref[...] = lax.dot_general(
        a_ref[...], w, NN, preferred_element_type=F32
    ).astype(BF)


def out_projection(pos, a, own, near, far):
    width = own.shape[1]
    return pl.pallas_call(
        out_kernel,
        out_shape=jax.ShapeDtypeStruct((a.shape[0], width), BF),
        in_specs=[pl.BlockSpec(memory_space=pltpu.SMEM)]
        + [pl.BlockSpec(memory_space=pltpu.VMEM)] * 6,
        scratch_shapes=[pltpu.VMEM((4, 2, 48, width), BF)],
        compiler_params=params(),
        name="out_projection",
    )(pos, a, own, *near, far)


def pack_kernel(pos_ref, up_ref, down_ref, out_ref, sem):
    @pl.when(pos_ref[0] == 0)
    def _():
        copy = pltpu.make_async_copy(up_ref, out_ref, sem.at[0])
        copy.start()
        copy.wait()

    @pl.when(pos_ref[0] == 1)
    def _():
        part = down_ref.shape[0]
        copies = []
        for s in range(4):
            copies.append(
                pltpu.make_async_copy(
                    down_ref.at[:, pl.ds(s * part, part)],
                    out_ref.at[pl.ds(s * part, part), :],
                    sem.at[s],
                )
            )
        for copy in copies:
            copy.start()
        for copy in copies:
            copy.wait()


def pack_ffn(pos, w_up, w_down):
    return pl.pallas_call(
        pack_kernel,
        out_shape=jax.ShapeDtypeStruct(w_up.shape, BF),
        in_specs=[
            pl.BlockSpec(memory_space=pltpu.SMEM),
            pl.BlockSpec(memory_space=pl.ANY),
            pl.BlockSpec(memory_space=pl.ANY),
        ],
        out_specs=pl.BlockSpec(memory_space=pl.ANY),
        scratch_shapes=[pltpu.SemaphoreType.DMA((4,))],
        compiler_params=params(),
        name="pack_ffn",
    )(pos, w_up, w_down)


def second_norm_kernel(x_ref, part_ref, mod_ref, second_ref, out_ref):
    proj = part_ref[0].astype(F32)
    for i in range(1, part_ref.shape[0]):
        proj += part_ref[i].astype(F32)
    second = (x_ref[...].astype(F32) + mod_ref[2:3, :] * proj).astype(BF)
    second_ref[...] = second
    h = layer_norm(second.astype(F32), mod_ref[3:4, :], mod_ref[4:5, :]).astype(BF)
    for i in range(out_ref.shape[0]):
        out_ref[i] = h


def second_norm(tokens, parts, mods):
    return pl.pallas_call(
        second_norm_kernel,
        out_shape=[
            jax.ShapeDtypeStruct(tokens.shape, BF),
            jax.ShapeDtypeStruct(parts.shape, BF),
        ],
        compiler_params=params(),
        name="second_norm",
    )(tokens, parts, mods)


def ffn_kernel(h_ref, up_ref, down_ref, out_ref, acc_ref):
    step = pl.program_id(0)
    part = up_ref.shape[-1]
    hidden = jax.nn.gelu(
        lax.dot_general(h_ref[...], up_ref[0, 0], NN, preferred_element_type=F32),
        approximate=True,
    ).astype(BF)
    for s in range(4):
        value = lax.dot_general(
            hidden,
            down_ref[0, 0, s * part : (s + 1) * part, :],
            NN,
            preferred_element_type=F32,
        )
        cols = slice(s * part, (s + 1) * part)

        @pl.when(step == 0)
        def _():
            acc_ref[:, cols] = value

        @pl.when(step > 0)
        def _():
            acc_ref[:, cols] += value

    @pl.when(step == pl.num_programs(0) - 1)
    def _():
        out_ref[...] = acc_ref[...].astype(BF)


def feed_forward(h, weights):
    rows, width = h.shape
    part = weights.shape[3]
    return pl.pallas_call(
        ffn_kernel,
        grid=(4,),
        out_shape=jax.ShapeDtypeStruct((rows, width), BF),
        in_specs=[
            pl.BlockSpec((rows, width), lambda i: (0, 0)),
            pl.BlockSpec((1, 1, width, part), lambda i: (0, i, 0, 0)),
            pl.BlockSpec((1, 1, width, part), lambda i: (1, i, 0, 0)),
        ],
        out_specs=pl.BlockSpec((rows, width), lambda i: (0, 0)),
        scratch_shapes=[pltpu.VMEM((rows, width), F32)],
        compiler_params=params(),
        name="feed_forward",
    )(h, weights, weights)


def last_kernel(second_ref, part_ref, mod_ref, w_ref, state_ref, vel_ref):
    ffn = part_ref[0].astype(F32)
    for i in range(1, part_ref.shape[0]):
        ffn += part_ref[i].astype(F32)
    state = (second_ref[...].astype(F32) + mod_ref[5:6, :] * ffn).astype(BF)
    state_ref[...] = state
    h = layer_norm(state.astype(F32), mod_ref[6:7, :], mod_ref[7:8, :]).astype(BF)
    vel_ref[...] = lax.dot_general(h, w_ref[...], NN, preferred_element_type=F32)


def last_stage(second, parts, mods, w_final):
    return pl.pallas_call(
        last_kernel,
        out_shape=[
            jax.ShapeDtypeStruct(second.shape, BF),
            jax.ShapeDtypeStruct((second.shape[0], w_final.shape[1]), F32),
        ],
        compiler_params=params(),
        name="last_stage",
    )(second, parts, mods, w_final)


def on_device(
    image_tokens,
    latent,
    modulation,
    text_kv,
    text_len,
    timestep,
    w_qkv,
    w_out,
    w_up,
    w_down,
    w_final,
):
    tokens = image_tokens[0]
    mods = modulation[0]
    rows, width = tokens.shape
    core = lax.axis_index("core")
    pos = jnp.stack([core, lax.axis_index("ty")]).astype(jnp.int32)
    swap2 = [(0, 1), (1, 0)]

    def to_lines(value, step):
        return lax.ppermute(value, "ty", [(i, (i + step) % 4) for i in range(4)])

    half_ffn = pack_ffn(pos, w_up, w_down)
    ffn_full = lax.all_gather(half_ffn, ("core", "tx"), axis=0, tiled=False)
    ffn_full = ffn_full.reshape(2, 4, width, w_up.shape[1])

    own_qkv = jnp.transpose(w_qkv, (1, 2, 0))
    half_qkv = lax.dynamic_slice_in_dim(own_qkv, core * 48, 48, 1)
    h1 = first_norm(tokens, mods, 4)
    h1, half_qkv = lax.optimization_barrier((h1, half_qkv))
    near_qkv = [to_lines(half_qkv, step) for step in STRIDES]
    h1 = lax.all_to_all(h1, "tx", split_axis=0, concat_axis=0, tiled=True)
    *near_qkv, h1 = lax.optimization_barrier((*near_qkv, h1))
    far_qkv = lax.ppermute(jnp.stack(near_qkv), "core", swap2)
    h1 = h1.reshape(4 * rows, width)
    query, keyval = project_qkv(pos, h1, own_qkv, near_qkv, far_qkv)

    half_out = lax.dynamic_slice_in_dim(w_out, core * 48, 48, 0)
    half_out, keyval = lax.optimization_barrier((half_out, keyval))
    chunks = [to_lines(keyval, step) for step in STRIDES]
    near_out = [to_lines(half_out, step) for step in STRIDES]
    text = lax.dynamic_slice_in_dim(text_kv[0], lax.axis_index("tx") * 384, 384, 2)
    text = jnp.transpose(text, (1, 0, 2))
    state = attention(query, [keyval], text=text, length=text_len)
    state = attention(query, chunks[:2], state=state)
    *near_out, across, totals = lax.optimization_barrier((*near_out, chunks[2], state[2]))
    state = (state[0], state[1], totals)
    far_out = lax.ppermute(jnp.stack(near_out), "core", swap2)
    attended = attention(query, [across], state=state, last=True)

    partial = out_projection(pos, attended, w_out, near_out, far_out)
    partial = partial.reshape(4, rows, width)
    partial = lax.all_to_all(partial, "tx", split_axis=0, concat_axis=0, tiled=True)
    second, h2 = second_norm(tokens, partial, mods)
    h2 = lax.all_to_all(h2, "ty", split_axis=0, concat_axis=0, tiled=True)
    partial = feed_forward(h2.reshape(4 * rows, width), ffn_full).reshape(4, rows, width)
    partial = lax.all_to_all(partial, "ty", split_axis=0, concat_axis=0, tiled=True)
    state, velocity = last_stage(second, partial, mods, w_final)

    step_index = timestep[0]
    delta = sigma_at(step_index + 1) - sigma_at(step_index)
    moved = latent[0] + delta * velocity.reshape(rows // 2, 2 * velocity.shape[1])
    return (state[None], moved[None])


def solution(mesh):
    fine = Mesh(
        mesh.devices.reshape(mesh.shape["req"] // 2, 2, 4, 4, mesh.shape["blk"]),
        ("zl", "core", "tx", "ty", "blk"),
    )
    group = ("zl", "core", "blk")
    tile = ("tx", "ty")
    in_specs = (
        P(group, tile, None),
        P(group, tile, None),
        P(group, None, None),
        P(group, None, None, None),
        P(group),
        P(group),
        P(None, None, tile),
        P(tile, None),
        P(None, tile),
        P(tile, None),
        P(),
    )
    out_specs = (P(group, tile, None), P(group, tile, None))
    return jax.shard_map(
        on_device, mesh=fine, in_specs=in_specs, out_specs=out_specs, check_vma=False
    )
```

```python
import functools

import jax
import jax.numpy as jnp
from jax import lax
from jax.experimental import pallas as pl
from jax.experimental.pallas import tpu as pltpu
from jax.sharding import Mesh, PartitionSpec as P

HEAD_DIM = 64
TXT = 154
STEPS = 8
BF = jnp.bfloat16
F32 = jnp.float32
NT = (((1,), (1,)), ((), ()))
NN = (((1,), (0,)), ((), ()))
STRIDES = (1, 3, 2)


def params():
    return pltpu.CompilerParams(vmem_limit_bytes=50 * 1024 * 1024)


def layer_norm(full, shift, scale):
    mean = jnp.mean(full, axis=-1, keepdims=True)
    cent = full - mean
    spread = jnp.mean(jnp.square(cent), axis=-1, keepdims=True)
    return cent * lax.rsqrt(spread + 1e-06) * (1.0 + scale) + shift


def sigma_at(index):
    frac = 1.0 - index.astype(F32) / STEPS
    return 3.0 * frac / (1.0 + 2.0 * frac)


def norm_kernel(copies, x_ref, mod_ref, out_ref):
    h = layer_norm(x_ref[...].astype(F32), mod_ref[0:1, :], mod_ref[1:2, :]).astype(BF)
    for i in range(copies):
        out_ref[i] = h


def first_norm(tokens, mods, copies):
    rows, width = tokens.shape
    return pl.pallas_call(
        functools.partial(norm_kernel, copies),
        out_shape=jax.ShapeDtypeStruct((copies, rows, width), BF),
        compiler_params=params(),
        name="first_norm",
    )(tokens, mods)


def assemble(pos_ref, own_ref, near_refs, far_ref, store):
    core = pos_ref[0]
    row = pos_ref[1]
    store(row, 0, own_ref, 0)
    store(row, 1, own_ref, 1)
    for i, (near_ref, step) in enumerate(zip(near_refs, STRIDES)):
        source = lax.rem(row + 4 - step, 4)
        store(source, core, near_ref, None)
        store(source, 1 - core, far_ref, i)


def project_kernel(first, pos_ref, h_ref, own_ref, n0_ref, n1_ref, n2_ref, far_ref, out_ref, w_ref):
    count = out_ref.shape[0]

    def store(source, half, ref, index):
        for k in range(count):
            if ref is own_ref:
                value = ref[first + k, index * 48 : index * 48 + 48, :]
            elif index is None:
                value = ref[k]
            else:
                value = ref[index, k]
            w_ref[k, source, half] = value

    assemble(pos_ref, own_ref, (n0_ref, n1_ref, n2_ref), far_ref, store)
    h = h_ref[...]
    for k in range(count):
        w = w_ref[k].reshape(384, h.shape[1])
        out_ref[k] = lax.dot_general(h, w, NT, preferred_element_type=F32).astype(BF)


def project(pos, h, own, first, near, far):
    rows, width = h.shape
    count = near[0].shape[0]
    return pl.pallas_call(
        functools.partial(project_kernel, first),
        out_shape=jax.ShapeDtypeStruct((count, rows, 384), BF),
        in_specs=[pl.BlockSpec(memory_space=pltpu.SMEM)]
        + [pl.BlockSpec(memory_space=pltpu.VMEM)] * 6,
        scratch_shapes=[pltpu.VMEM((count, 4, 2, 48, width), BF)],
        compiler_params=params(),
        name="project",
    )(pos, h, own, *near, far)


def attention_kernel(chunks, has_text, has_state, last, *refs):
    refs = list(refs)
    len_ref = refs.pop(0) if has_text else None
    q_ref = refs.pop(0)
    kv_refs = [refs.pop(0) for _ in range(chunks)]
    text_ref = refs.pop(0) if has_text else None
    state_refs = [refs.pop(0) for _ in range(3)] if has_state else None
    rows = q_ref.shape[0]
    if has_text:
        live = lax.broadcasted_iota(jnp.int32, (rows, TXT), 1) < len_ref[0]
    first = lax.broadcasted_iota(jnp.int32, (rows, 128), 1) < HEAD_DIM
    for g in range(q_ref.shape[1] // 128):
        cols = slice(g * 128, g * 128 + 128)
        q = q_ref[:, cols]
        sides = []
        for side in range(2):
            here = first if side == 0 else jnp.logical_not(first)
            qh = jnp.where(here, q, jnp.zeros_like(q))
            parts = []
            for ref in kv_refs:
                s = lax.dot_general(qh, ref[0, :, cols], NT, preferred_element_type=F32) * 0.125
                parts.append((s, ref[1, :, cols]))
            if has_text:
                s = (
                    lax.dot_general(qh, text_ref[0, :, cols], NT, preferred_element_type=F32)
                    * 0.125
                )
                parts.append((jnp.where(live, s, -jnp.inf), text_ref[1, :, cols]))
            top = None
            for s, _ in parts:
                peak = jnp.max(s, axis=1, keepdims=True)
                top = peak if top is None else jnp.maximum(top, peak)
            if has_state:
                lane = g * 128 + side * HEAD_DIM
                top = jnp.maximum(top, state_refs[1][:, lane : lane + 1])
            total = None
            acc = None
            for s, values in parts:
                p = jnp.exp(s - top)
                amount = jnp.sum(p, axis=1, keepdims=True)
                part = lax.dot_general(p.astype(BF), values, NN, preferred_element_type=F32)
                total = amount if total is None else total + amount
                acc = part if acc is None else acc + part
            sides.append((acc, top, total))
        acc = jnp.where(first, sides[0][0], sides[1][0])
        top = jnp.where(first, sides[0][1], sides[1][1])
        total = jnp.where(first, sides[0][2], sides[1][2])
        if has_state:
            factor = jnp.exp(state_refs[1][:, cols] - top)
            acc = acc + state_refs[0][:, cols] * factor
            total = total + state_refs[2][:, cols] * factor
        if last:
            refs[0][:, cols] = (acc / total).astype(BF)
        else:
            refs[0][:, cols] = acc
            refs[1][:, cols] = top
            refs[2][:, cols] = total


def attention(q, kvs, text=None, length=None, state=None, last=False):
    args = []
    specs = []
    if text is not None:
        args.append(length)
        specs.append(pl.BlockSpec(memory_space=pltpu.SMEM))
    rest = [q, *kvs] + ([text] if text is not None else []) + list(state or [])
    args += rest
    specs += [pl.BlockSpec(memory_space=pltpu.VMEM)] * len(rest)
    if last:
        out = jax.ShapeDtypeStruct(q.shape, BF)
    else:
        out = [jax.ShapeDtypeStruct(q.shape, F32)] * 3
    return pl.pallas_call(
        functools.partial(
            attention_kernel, len(kvs), text is not None, state is not None, last
        ),
        out_shape=out,
        in_specs=specs,
        compiler_params=params(),
        name="attention",
    )(*args)


def out_kernel(a_ref, w_ref, out_ref):
    out_ref[...] = lax.dot_general(
        a_ref[...], w_ref[...], NN, preferred_element_type=F32
    ).astype(BF)


def out_projection(a, w):
    return pl.pallas_call(
        out_kernel,
        out_shape=jax.ShapeDtypeStruct((a.shape[0], w.shape[1]), BF),
        compiler_params=params(),
        name="out_projection",
    )(a, w)


def pack_kernel(pos_ref, up_ref, down_ref, out_ref, sem):
    @pl.when(pos_ref[0] == 0)
    def _():
        copy = pltpu.make_async_copy(up_ref, out_ref, sem.at[0])
        copy.start()
        copy.wait()

    @pl.when(pos_ref[0] == 1)
    def _():
        part = down_ref.shape[0]
        copies = []
        for s in range(4):
            copies.append(
                pltpu.make_async_copy(
                    down_ref.at[:, pl.ds(s * part, part)],
                    out_ref.at[pl.ds(s * part, part), :],
                    sem.at[s],
                )
            )
        for copy in copies:
            copy.start()
        for copy in copies:
            copy.wait()


def pack_ffn(pos, w_up, w_down):
    return pl.pallas_call(
        pack_kernel,
        out_shape=jax.ShapeDtypeStruct(w_up.shape, BF),
        in_specs=[
            pl.BlockSpec(memory_space=pltpu.SMEM),
            pl.BlockSpec(memory_space=pltpu.HBM),
            pl.BlockSpec(memory_space=pltpu.HBM),
        ],
        out_specs=pl.BlockSpec(memory_space=pltpu.HBM),
        scratch_shapes=[pltpu.SemaphoreType.DMA((4,))],
        compiler_params=params(),
        name="pack_ffn",
    )(pos, w_up, w_down)


def second_norm_kernel(x_ref, part_ref, mod_ref, second_ref, out_ref):
    proj = part_ref[0].astype(F32)
    for i in range(1, part_ref.shape[0]):
        proj += part_ref[i].astype(F32)
    second = (x_ref[...].astype(F32) + mod_ref[2:3, :] * proj).astype(BF)
    second_ref[...] = second
    h = layer_norm(second.astype(F32), mod_ref[3:4, :], mod_ref[4:5, :]).astype(BF)
    for i in range(out_ref.shape[0]):
        out_ref[i] = h


def second_norm(tokens, parts, mods):
    return pl.pallas_call(
        second_norm_kernel,
        out_shape=[
            jax.ShapeDtypeStruct(tokens.shape, BF),
            jax.ShapeDtypeStruct(parts.shape, BF),
        ],
        compiler_params=params(),
        name="second_norm",
    )(tokens, parts, mods)


def ffn_kernel(h_ref, up_ref, down_ref, out_ref, hidden_ref):
    step = pl.program_id(0)
    part = up_ref.shape[-1]

    @pl.when(step < 2)
    def _():
        up = jnp.concatenate([up_ref[0, 0], up_ref[0, 1]], axis=1)
        hidden_ref[lax.rem(step, 2)] = jax.nn.gelu(
            lax.dot_general(h_ref[...], up, NN, preferred_element_type=F32),
            approximate=True,
        ).astype(BF)

    @pl.when(step >= 2)
    def _():
        hidden = jnp.concatenate([hidden_ref[0], hidden_ref[1]], axis=1)
        down = jnp.concatenate(
            [
                jnp.concatenate([down_ref[0, y, :part], down_ref[0, y, part:]], axis=1)
                for y in range(4)
            ],
            axis=0,
        )
        out_ref[...] = lax.dot_general(
            hidden, down, NN, preferred_element_type=F32
        ).astype(BF)


def feed_forward(h, weights):
    rows, width = h.shape
    part = weights.shape[3]
    return pl.pallas_call(
        ffn_kernel,
        grid=(4,),
        out_shape=jax.ShapeDtypeStruct((rows, width), BF),
        in_specs=[
            pl.BlockSpec((rows, width), lambda i: (0, 0)),
            pl.BlockSpec((1, 2, width, part), lambda i: (0, jnp.minimum(i, 1), 0, 0)),
            pl.BlockSpec((1, 4, 2 * part, part), lambda i: (1, 0, jnp.maximum(i - 2, 0), 0)),
        ],
        out_specs=pl.BlockSpec((rows, 2 * part), lambda i: (0, jnp.maximum(i - 2, 0))),
        scratch_shapes=[pltpu.VMEM((2, rows, 2 * part), BF)],
        compiler_params=params(),
        name="feed_forward",
    )(h, weights, weights)


def last_kernel(second_ref, part_ref, mod_ref, w_ref, state_ref, vel_ref):
    ffn = part_ref[0].astype(F32)
    for i in range(1, part_ref.shape[0]):
        ffn += part_ref[i].astype(F32)
    state = (second_ref[...].astype(F32) + mod_ref[5:6, :] * ffn).astype(BF)
    state_ref[...] = state
    h = layer_norm(state.astype(F32), mod_ref[6:7, :], mod_ref[7:8, :]).astype(BF)
    vel_ref[...] = lax.dot_general(h, w_ref[...], NN, preferred_element_type=F32)


def last_stage(second, parts, mods, w_final):
    return pl.pallas_call(
        last_kernel,
        out_shape=[
            jax.ShapeDtypeStruct(second.shape, BF),
            jax.ShapeDtypeStruct((second.shape[0], w_final.shape[1]), F32),
        ],
        compiler_params=params(),
        name="last_stage",
    )(second, parts, mods, w_final)


def on_device(
    image_tokens,
    latent,
    modulation,
    text_kv,
    text_len,
    timestep,
    w_qkv,
    w_out,
    w_up,
    w_down,
    w_final,
):
    tokens = image_tokens[0]
    mods = modulation[0]
    rows, width = tokens.shape
    core = lax.axis_index("core")
    pos = jnp.stack([core, lax.axis_index("ty")]).astype(jnp.int32)
    swap2 = [(0, 1), (1, 0)]

    def to_lines(value, step):
        return lax.ppermute(value, "ty", [(i, (i + step) % 4) for i in range(4)])

    half_out = lax.dynamic_slice_in_dim(w_out, core * 48, 48, 0)
    out_full = lax.all_gather(half_out, ("ty", "core"), axis=0, tiled=True)

    own_qkv = jnp.transpose(w_qkv, (1, 2, 0))
    half_qkv = lax.dynamic_slice_in_dim(own_qkv, core * 48, 48, 1)
    h1 = first_norm(tokens, mods, 4)
    h1, half_qkv, pos = lax.optimization_barrier((h1, half_qkv, pos))
    near_kv = [to_lines(half_qkv[1:], step) for step in STRIDES]
    half_ffn = pack_ffn(pos, w_up, w_down)
    ffn_full = lax.all_gather(half_ffn, ("core", "tx"), axis=0, tiled=False)
    ffn_full = ffn_full.reshape(2, 4, width, w_up.shape[1])
    h1 = lax.all_to_all(h1, "tx", split_axis=0, concat_axis=0, tiled=True)

    *near_kv, h1, half_q = lax.optimization_barrier((*near_kv, h1, half_qkv[:1]))
    far_kv = lax.ppermute(jnp.stack(near_kv), "core", swap2)
    near_q = [to_lines(half_q, step) for step in STRIDES]
    h1 = h1.reshape(4 * rows, width)
    keyval = project(pos, h1, own_qkv, 1, near_kv, far_kv)
    chunks = [to_lines(keyval, step) for step in STRIDES]
    *near_q, keyval = lax.optimization_barrier((*near_q, keyval))
    far_q = lax.ppermute(jnp.stack(near_q), "core", swap2)
    query = project(pos, h1, own_qkv, 0, near_q, far_q)[0]

    text = lax.dynamic_slice_in_dim(text_kv[0], lax.axis_index("tx") * 384, 384, 2)
    text = jnp.transpose(text, (1, 0, 2))
    state = attention(query, [keyval], text=text, length=text_len)
    state = attention(query, chunks[:2], state=state)
    attended = attention(query, chunks[2:], state=state, last=True)

    partial = out_projection(attended, out_full)
    partial = partial.reshape(4, rows, width)
    partial = lax.all_to_all(partial, "tx", split_axis=0, concat_axis=0, tiled=True)
    second, h2 = second_norm(tokens, partial, mods)
    h2 = lax.all_to_all(h2, "ty", split_axis=0, concat_axis=0, tiled=True)
    partial = feed_forward(h2.reshape(4 * rows, width), ffn_full).reshape(4, rows, width)
    partial = lax.all_to_all(partial, "ty", split_axis=0, concat_axis=0, tiled=True)
    state, velocity = last_stage(second, partial, mods, w_final)

    step_index = timestep[0]
    delta = sigma_at(step_index + 1) - sigma_at(step_index)
    moved = latent[0] + delta * velocity.reshape(rows // 2, 2 * velocity.shape[1])
    return (state[None], moved[None])


def solution(mesh):
    fine = Mesh(
        mesh.devices.reshape(mesh.shape["req"] // 2, 2, 4, 4, mesh.shape["blk"]),
        ("zl", "core", "tx", "ty", "blk"),
    )
    group = ("zl", "core", "blk")
    tile = ("tx", "ty")
    in_specs = (
        P(group, tile, None),
        P(group, tile, None),
        P(group, None, None),
        P(group, None, None, None),
        P(group),
        P(group),
        P(None, None, tile),
        P(tile, None),
        P(None, tile),
        P(tile, None),
        P(),
    )
    out_specs = (P(group, tile, None), P(group, tile, None))
    return jax.shard_map(
        on_device, mesh=fine, in_specs=in_specs, out_specs=out_specs, check_vma=False
    )
```

```python
import functools

import jax
import jax.numpy as jnp
from jax import lax
from jax.experimental import pallas as pl
from jax.experimental.pallas import tpu as pltpu
from jax.sharding import Mesh, PartitionSpec as P

HEAD_DIM = 64
TXT = 154
STEPS = 8
BF = jnp.bfloat16
F32 = jnp.float32
NT = (((1,), (1,)), ((), ()))
NN = (((1,), (0,)), ((), ()))
STRIDES = (1, 3, 2)


def params():
    return pltpu.CompilerParams(vmem_limit_bytes=50 * 1024 * 1024)


def layer_norm(full, shift, scale):
    mean = jnp.mean(full, axis=-1, keepdims=True)
    cent = full - mean
    spread = jnp.mean(jnp.square(cent), axis=-1, keepdims=True)
    return cent * lax.rsqrt(spread + 1e-06) * (1.0 + scale) + shift


def sigma_at(index):
    frac = 1.0 - index.astype(F32) / STEPS
    return 3.0 * frac / (1.0 + 2.0 * frac)


def norm_kernel(copies, x_ref, mod_ref, out_ref):
    h = layer_norm(x_ref[...].astype(F32), mod_ref[0:1, :], mod_ref[1:2, :]).astype(BF)
    for i in range(copies):
        out_ref[i] = h


def first_norm(tokens, mods, copies):
    rows, width = tokens.shape
    return pl.pallas_call(
        functools.partial(norm_kernel, copies),
        out_shape=jax.ShapeDtypeStruct((copies, rows, width), BF),
        compiler_params=params(),
        name="first_norm",
    )(tokens, mods)


def assemble(pos_ref, own_ref, near_refs, far_ref, store):
    core = pos_ref[0]
    row = pos_ref[1]
    store(row, 0, own_ref, 0)
    store(row, 1, own_ref, 1)
    for i, (near_ref, step) in enumerate(zip(near_refs, STRIDES)):
        source = lax.rem(row + 4 - step, 4)
        store(source, core, near_ref, None)
        store(source, 1 - core, far_ref, i)


def project_kernel(first, pos_ref, h_ref, own_ref, n0_ref, n1_ref, n2_ref, far_ref, out_ref, w_ref):
    count = out_ref.shape[1]

    def store(source, half, ref, index):
        for k in range(count):
            if ref is own_ref:
                value = ref[first + k, index * 48 : index * 48 + 48, :]
            elif index is None:
                value = ref[k]
            else:
                value = ref[index, k]
            w_ref[k, source, half] = value

    assemble(pos_ref, own_ref, (n0_ref, n1_ref, n2_ref), far_ref, store)
    h = h_ref[...]
    for k in range(count):
        w = w_ref[k].reshape(384, h.shape[1])
        value = lax.dot_general(h, w, NT, preferred_element_type=F32).astype(BF)
        for i in range(out_ref.shape[0]):
            out_ref[i, k] = value


def project(pos, h, own, first, count, copies, near, far):
    rows, width = h.shape
    return pl.pallas_call(
        functools.partial(project_kernel, first),
        out_shape=jax.ShapeDtypeStruct((copies, count, rows, 384), BF),
        in_specs=[pl.BlockSpec(memory_space=pltpu.SMEM)]
        + [pl.BlockSpec(memory_space=pltpu.VMEM)] * 6,
        scratch_shapes=[pltpu.VMEM((count, 4, 2, 48, width), BF)],
        compiler_params=params(),
        name="project",
    )(pos, h, own, *near, far)


def attention_kernel(own, *refs):
    refs = list(refs)
    pos_ref, q_ref, kv_ref = refs[:3]
    if own:
        text_ref = refs[3]
        state_refs = None
        outs = refs[4:]
    else:
        state_refs = refs[3:6]
        outs = refs[6:]
    rows = q_ref.shape[0]
    if own:
        live = lax.broadcasted_iota(jnp.int32, (rows, TXT), 1) < pos_ref[2]
    first = lax.broadcasted_iota(jnp.int32, (rows, 128), 1) < HEAD_DIM
    where = [0] if own else [lax.rem(pos_ref[1] + i, 4) for i in (1, 2, 3)]
    for g in range(q_ref.shape[1] // 128):
        cols = slice(g * 128, g * 128 + 128)
        q = q_ref[:, cols]
        sides = []
        for side in range(2):
            here = first if side == 0 else jnp.logical_not(first)
            qh = jnp.where(here, q, jnp.zeros_like(q))
            parts = []
            for i in where:
                s = (
                    lax.dot_general(qh, kv_ref[i, 0, :, cols], NT, preferred_element_type=F32)
                    * 0.125
                )
                parts.append((s, kv_ref[i, 1, :, cols]))
            if own:
                s = (
                    lax.dot_general(qh, text_ref[0, :, cols], NT, preferred_element_type=F32)
                    * 0.125
                )
                parts.append((jnp.where(live, s, -jnp.inf), text_ref[1, :, cols]))
            top = None
            for s, _ in parts:
                peak = jnp.max(s, axis=1, keepdims=True)
                top = peak if top is None else jnp.maximum(top, peak)
            if not own:
                lane = g * 128 + side * HEAD_DIM
                top = jnp.maximum(top, state_refs[1][:, lane : lane + 1])
            total = None
            acc = None
            for s, values in parts:
                p = jnp.exp(s - top)
                amount = jnp.sum(p, axis=1, keepdims=True)
                part = lax.dot_general(p.astype(BF), values, NN, preferred_element_type=F32)
                total = amount if total is None else total + amount
                acc = part if acc is None else acc + part
            sides.append((acc, top, total))
        acc = jnp.where(first, sides[0][0], sides[1][0])
        top = jnp.where(first, sides[0][1], sides[1][1])
        total = jnp.where(first, sides[0][2], sides[1][2])
        if own:
            outs[0][:, cols] = acc
            outs[1][:, cols] = top
            outs[2][:, cols] = total
        else:
            factor = jnp.exp(state_refs[1][:, cols] - top)
            acc = acc + state_refs[0][:, cols] * factor
            total = total + state_refs[2][:, cols] * factor
            outs[0][:, cols] = (acc / total).astype(BF)


def attention(pos, q, kv, text=None, state=None):
    own = text is not None
    args = [q, kv] + ([text] if own else list(state))
    if own:
        out = [jax.ShapeDtypeStruct(q.shape, F32)] * 3
    else:
        out = jax.ShapeDtypeStruct(q.shape, BF)
    return pl.pallas_call(
        functools.partial(attention_kernel, own),
        out_shape=out,
        in_specs=[pl.BlockSpec(memory_space=pltpu.SMEM)]
        + [pl.BlockSpec(memory_space=pltpu.VMEM)] * len(args),
        compiler_params=params(),
        name="attention",
    )(pos, *args)


def out_kernel(pos_ref, a_ref, own_ref, n0_ref, n1_ref, n2_ref, far_ref, out_ref, w_ref):
    def store(source, half, ref, index):
        if ref is own_ref:
            value = ref[index * 48 : index * 48 + 48, :]
        elif index is None:
            value = ref[1]
        else:
            value = ref[index, 1]
        w_ref[source, half] = value

    assemble(pos_ref, own_ref, (n0_ref, n1_ref, n2_ref), far_ref, store)
    w = w_ref[...].reshape(384, out_ref.shape[1])
    out_ref[...] = lax.dot_general(
        a_ref[...], w, NN, preferred_element_type=F32
    ).astype(BF)


def out_projection(pos, a, own, near, far):
    width = own.shape[1]
    return pl.pallas_call(
        out_kernel,
        out_shape=jax.ShapeDtypeStruct((a.shape[0], width), BF),
        in_specs=[pl.BlockSpec(memory_space=pltpu.SMEM)]
        + [pl.BlockSpec(memory_space=pltpu.VMEM)] * 6,
        scratch_shapes=[pltpu.VMEM((4, 2, 48, width), BF)],
        compiler_params=params(),
        name="out_projection",
    )(pos, a, own, *near, far)


def pack_kernel(pos_ref, up_ref, down_ref, out_ref, sem):
    @pl.when(pos_ref[0] == 0)
    def _():
        copy = pltpu.make_async_copy(up_ref, out_ref, sem.at[0])
        copy.start()
        copy.wait()

    @pl.when(pos_ref[0] == 1)
    def _():
        part = down_ref.shape[0]
        copies = []
        for s in range(4):
            copies.append(
                pltpu.make_async_copy(
                    down_ref.at[:, pl.ds(s * part, part)],
                    out_ref.at[pl.ds(s * part, part), :],
                    sem.at[s],
                )
            )
        for copy in copies:
            copy.start()
        for copy in copies:
            copy.wait()


def pack_ffn(pos, w_up, w_down):
    return pl.pallas_call(
        pack_kernel,
        out_shape=jax.ShapeDtypeStruct(w_up.shape, BF),
        in_specs=[
            pl.BlockSpec(memory_space=pltpu.SMEM),
            pl.BlockSpec(memory_space=pltpu.HBM),
            pl.BlockSpec(memory_space=pltpu.HBM),
        ],
        out_specs=pl.BlockSpec(memory_space=pltpu.HBM),
        scratch_shapes=[pltpu.SemaphoreType.DMA((4,))],
        compiler_params=params(),
        name="pack_ffn",
    )(pos, w_up, w_down)


def second_norm_kernel(x_ref, part_ref, mod_ref, second_ref, out_ref):
    proj = part_ref[0].astype(F32)
    for i in range(1, part_ref.shape[0]):
        proj += part_ref[i].astype(F32)
    second = (x_ref[...].astype(F32) + mod_ref[2:3, :] * proj).astype(BF)
    second_ref[...] = second
    h = layer_norm(second.astype(F32), mod_ref[3:4, :], mod_ref[4:5, :]).astype(BF)
    for i in range(out_ref.shape[0]):
        out_ref[i] = h


def second_norm(tokens, parts, mods):
    return pl.pallas_call(
        second_norm_kernel,
        out_shape=[
            jax.ShapeDtypeStruct(tokens.shape, BF),
            jax.ShapeDtypeStruct(parts.shape, BF),
        ],
        compiler_params=params(),
        name="second_norm",
    )(tokens, parts, mods)


def ffn_kernel(h_ref, up_ref, down_ref, out_ref, hidden_ref):
    step = pl.program_id(0)
    part = up_ref.shape[-1]

    @pl.when(step < 2)
    def _():
        up = jnp.concatenate([up_ref[0, 0], up_ref[0, 1]], axis=1)
        hidden_ref[lax.rem(step, 2)] = jax.nn.gelu(
            lax.dot_general(h_ref[...], up, NN, preferred_element_type=F32),
            approximate=True,
        ).astype(BF)

    @pl.when(step >= 2)
    def _():
        hidden = jnp.concatenate([hidden_ref[0], hidden_ref[1]], axis=1)
        down = jnp.concatenate(
            [
                jnp.concatenate([down_ref[0, y, :part], down_ref[0, y, part:]], axis=1)
                for y in range(4)
            ],
            axis=0,
        )
        out_ref[...] = lax.dot_general(
            hidden, down, NN, preferred_element_type=F32
        ).astype(BF)


def feed_forward(h, weights):
    rows, width = h.shape
    part = weights.shape[3]
    return pl.pallas_call(
        ffn_kernel,
        grid=(4,),
        out_shape=jax.ShapeDtypeStruct((rows, width), BF),
        in_specs=[
            pl.BlockSpec((rows, width), lambda i: (0, 0)),
            pl.BlockSpec((1, 2, width, part), lambda i: (0, jnp.minimum(i, 1), 0, 0)),
            pl.BlockSpec((1, 4, 2 * part, part), lambda i: (1, 0, jnp.maximum(i - 2, 0), 0)),
        ],
        out_specs=pl.BlockSpec((rows, 2 * part), lambda i: (0, jnp.maximum(i - 2, 0))),
        scratch_shapes=[pltpu.VMEM((2, rows, 2 * part), BF)],
        compiler_params=params(),
        name="feed_forward",
    )(h, weights, weights)


def last_kernel(second_ref, part_ref, mod_ref, w_ref, state_ref, vel_ref):
    ffn = part_ref[0].astype(F32)
    for i in range(1, part_ref.shape[0]):
        ffn += part_ref[i].astype(F32)
    state = (second_ref[...].astype(F32) + mod_ref[5:6, :] * ffn).astype(BF)
    state_ref[...] = state
    h = layer_norm(state.astype(F32), mod_ref[6:7, :], mod_ref[7:8, :]).astype(BF)
    vel_ref[...] = lax.dot_general(h, w_ref[...], NN, preferred_element_type=F32)


def last_stage(second, parts, mods, w_final):
    return pl.pallas_call(
        last_kernel,
        out_shape=[
            jax.ShapeDtypeStruct(second.shape, BF),
            jax.ShapeDtypeStruct((second.shape[0], w_final.shape[1]), F32),
        ],
        compiler_params=params(),
        name="last_stage",
    )(second, parts, mods, w_final)


def on_device(
    image_tokens,
    latent,
    modulation,
    text_kv,
    text_len,
    timestep,
    w_qkv,
    w_out,
    w_up,
    w_down,
    w_final,
):
    tokens = image_tokens[0]
    mods = modulation[0]
    rows, width = tokens.shape
    core = lax.axis_index("core")
    pos = jnp.concatenate([jnp.stack([core, lax.axis_index("ty")]).astype(jnp.int32), text_len])
    swap2 = [(0, 1), (1, 0)]

    def to_lines(value, step):
        return lax.ppermute(value, "ty", [(i, (i + step) % 4) for i in range(4)])

    own_qkv = jnp.transpose(w_qkv, (1, 2, 0))
    half_kv = lax.dynamic_slice(own_qkv, (1, core * 48, 0), (2, 48, width))
    near_kv = [to_lines(half_kv, step) for step in STRIDES]

    h1 = first_norm(tokens, mods, 4)
    h1 = lax.all_to_all(h1, "tx", split_axis=0, concat_axis=0, tiled=True)

    half_q = lax.dynamic_slice(own_qkv, (0, core * 48, 0), (1, 48, width))
    half_out = lax.dynamic_slice(w_out, (core * 48, 0), (48, width))
    half_qo = jnp.concatenate([half_q, half_out[None]])
    text = lax.dynamic_slice_in_dim(text_kv[0], lax.axis_index("tx") * 384, 384, 2)
    text = jnp.transpose(text, (1, 0, 2))
    half_ffn = pack_ffn(core[None].astype(jnp.int32), w_up, w_down)
    ffn_full = lax.all_gather(half_ffn, ("core", "tx"), axis=0, tiled=False)
    ffn_full = ffn_full.reshape(2, 4, width, w_up.shape[1])

    *near_kv, h1, half_qo, text = lax.optimization_barrier((*near_kv, h1, half_qo, text))
    far_kv = lax.ppermute(jnp.stack(near_kv), "core", swap2)
    near_qo = [to_lines(half_qo, step) for step in STRIDES]
    h1 = h1.reshape(4 * rows, width)
    own_kv = project(pos, h1, own_qkv, 1, 2, 4, near_kv, far_kv)
    all_kv = lax.all_to_all(own_kv, "ty", split_axis=0, concat_axis=0, tiled=True)
    *near_qo, own_kv = lax.optimization_barrier((*near_qo, own_kv))
    far_qo = lax.ppermute(jnp.stack(near_qo), "core", swap2)
    query = project(pos, h1, own_qkv, 0, 1, 1, near_qo, far_qo)[0, 0]

    state = attention(pos, query, own_kv, text=text)
    attended = attention(pos, query, all_kv, state=state)

    partial = out_projection(pos, attended, w_out, near_qo, far_qo)
    partial = partial.reshape(4, rows, width)
    partial = lax.all_to_all(partial, "tx", split_axis=0, concat_axis=0, tiled=True)
    second, h2 = second_norm(tokens, partial, mods)
    h2 = lax.all_to_all(h2, "ty", split_axis=0, concat_axis=0, tiled=True)
    partial = feed_forward(h2.reshape(4 * rows, width), ffn_full).reshape(4, rows, width)
    partial = lax.all_to_all(partial, "ty", split_axis=0, concat_axis=0, tiled=True)
    state, velocity = last_stage(second, partial, mods, w_final)

    step_index = timestep[0]
    delta = sigma_at(step_index + 1) - sigma_at(step_index)
    moved = latent[0] + delta * velocity.reshape(rows // 2, 2 * velocity.shape[1])
    return (state[None], moved[None])


def solution(mesh):
    fine = Mesh(
        mesh.devices.reshape(mesh.shape["req"] // 2, 2, 4, 4, mesh.shape["blk"]),
        ("zl", "core", "tx", "ty", "blk"),
    )
    group = ("zl", "core", "blk")
    tile = ("tx", "ty")
    in_specs = (
        P(group, tile, None),
        P(group, tile, None),
        P(group, None, None),
        P(group, None, None, None),
        P(group),
        P(group),
        P(None, None, tile),
        P(tile, None),
        P(None, tile),
        P(tile, None),
        P(),
    )
    out_specs = (P(group, tile, None), P(group, tile, None))
    return jax.shard_map(
        on_device, mesh=fine, in_specs=in_specs, out_specs=out_specs, check_vma=False
    )
```

```python
import functools

import jax
import jax.numpy as jnp
from jax import lax
from jax.experimental import pallas as pl
from jax.experimental.pallas import tpu as pltpu
from jax.sharding import Mesh, PartitionSpec as P

HEAD_DIM = 64
TXT = 154
STEPS = 8
BF = jnp.bfloat16
F32 = jnp.float32
NT = (((1,), (1,)), ((), ()))
NN = (((1,), (0,)), ((), ()))
STRIDES = (1, 3, 2)


def params(mebibytes):
    return pltpu.CompilerParams(vmem_limit_bytes=mebibytes * 1024 * 1024)


def layer_norm(full, shift, scale):
    mean = jnp.mean(full, axis=-1, keepdims=True)
    cent = full - mean
    spread = jnp.mean(jnp.square(cent), axis=-1, keepdims=True)
    return cent * lax.rsqrt(spread + 1e-06) * (1.0 + scale) + shift


def sigma_at(index):
    frac = 1.0 - index.astype(F32) / STEPS
    return 3.0 * frac / (1.0 + 2.0 * frac)


def norm_kernel(copies, x_ref, mod_ref, out_ref):
    h = layer_norm(x_ref[...].astype(F32), mod_ref[0:1, :], mod_ref[1:2, :]).astype(BF)
    for i in range(copies):
        out_ref[i] = h


def first_norm(tokens, mods, copies):
    rows, width = tokens.shape
    return pl.pallas_call(
        functools.partial(norm_kernel, copies),
        out_shape=jax.ShapeDtypeStruct((copies, rows, width), BF),
        compiler_params=params(6),
        name="first_norm",
    )(tokens, mods)


def assemble(pos_ref, own_ref, near_refs, far_ref, store):
    core = pos_ref[0]
    row = pos_ref[1]
    store(row, 0, own_ref, 0)
    store(row, 1, own_ref, 1)
    for i, (near_ref, step) in enumerate(zip(near_refs, STRIDES)):
        source = lax.rem(row + 4 - step, 4)
        store(source, core, near_ref, None)
        store(source, 1 - core, far_ref, i)


def project_kernel(first, pos_ref, h_ref, own_ref, n0_ref, n1_ref, n2_ref, far_ref, out_ref, w_ref):
    count = out_ref.shape[1]

    def store(source, half, ref, index):
        for k in range(count):
            if ref is own_ref:
                value = ref[first + k, index * 48 : index * 48 + 48, :]
            elif index is None:
                value = ref[k]
            else:
                value = ref[index, k]
            w_ref[k, source, half] = value

    assemble(pos_ref, own_ref, (n0_ref, n1_ref, n2_ref), far_ref, store)
    h = h_ref[...]
    for k in range(count):
        w = w_ref[k].reshape(384, h.shape[1])
        value = lax.dot_general(h, w, NT, preferred_element_type=F32).astype(BF)
        for i in range(out_ref.shape[0]):
            out_ref[i, k] = value


def project(pos, h, own, first, count, copies, near, far):
    rows, width = h.shape
    return pl.pallas_call(
        functools.partial(project_kernel, first),
        out_shape=jax.ShapeDtypeStruct((copies, count, rows, 384), BF),
        in_specs=[pl.BlockSpec(memory_space=pltpu.SMEM)]
        + [pl.BlockSpec(memory_space=pltpu.VMEM)] * 6,
        scratch_shapes=[pltpu.VMEM((count, 4, 2, 48, width), BF)],
        compiler_params=params(14),
        name="project",
    )(pos, h, own, *near, far)


def attention_kernel(own, *refs):
    refs = list(refs)
    pos_ref, q_ref, kv_ref = refs[:3]
    if own:
        text_ref = refs[3]
        outs = refs[4:]
    else:
        acc_ref, stat_ref = refs[3:5]
        outs = refs[5:]
    rows = q_ref.shape[0]
    if own:
        live = lax.broadcasted_iota(jnp.int32, (rows, TXT), 1) < pos_ref[2]
    first = lax.broadcasted_iota(jnp.int32, (rows, 128), 1) < HEAD_DIM
    where = [0] if own else [lax.rem(pos_ref[1] + i, 4) for i in (1, 2, 3)]
    lane = lax.broadcasted_iota(jnp.int32, (rows, 128), 1)
    tops = jnp.zeros((rows, 128), F32)
    totals = jnp.zeros((rows, 128), F32)
    for g in range(q_ref.shape[1] // 128):
        cols = slice(g * 128, g * 128 + 128)
        q = q_ref[:, cols]
        accs = []
        scales = []
        for side in range(2):
            head = 2 * g + side
            here = first if side == 0 else jnp.logical_not(first)
            qh = jnp.where(here, q, jnp.zeros_like(q))
            parts = []
            for i in where:
                s = (
                    lax.dot_general(qh, kv_ref[i, 0, :, cols], NT, preferred_element_type=F32)
                    * 0.125
                )
                parts.append((s, kv_ref[i, 1, :, cols]))
            if own:
                s = (
                    lax.dot_general(qh, text_ref[0, :, cols], NT, preferred_element_type=F32)
                    * 0.125
                )
                parts.append((jnp.where(live, s, -jnp.inf), text_ref[1, :, cols]))
            top = None
            for s, _ in parts:
                peak = jnp.max(s, axis=1, keepdims=True)
                top = peak if top is None else jnp.maximum(top, peak)
            if not own:
                old = stat_ref[0, :, head : head + 1]
                top = jnp.maximum(top, old)
            total = None
            acc = None
            for s, values in parts:
                p = jnp.exp(s - top)
                amount = jnp.sum(p, axis=1, keepdims=True)
                part = lax.dot_general(p.astype(BF), values, NN, preferred_element_type=F32)
                total = amount if total is None else total + amount
                acc = part if acc is None else acc + part
            if own:
                tops = jnp.where(lane == head, top, tops)
                totals = jnp.where(lane == head, total, totals)
            else:
                factor = jnp.exp(old - top)
                total = total + stat_ref[1, :, head : head + 1] * factor
                scales.append((factor, total))
            accs.append(acc)
        acc = jnp.where(first, accs[0], accs[1])
        if own:
            outs[0][:, cols] = acc
        else:
            factor = jnp.where(first, scales[0][0], scales[1][0])
            total = jnp.where(first, scales[0][1], scales[1][1])
            outs[0][:, cols] = ((acc + acc_ref[:, cols] * factor) / total).astype(BF)
    if own:
        outs[1][0] = tops
        outs[1][1] = totals


def attention(pos, q, kv, text=None, state=None):
    own = text is not None
    args = [q, kv] + ([text] if own else list(state))
    if own:
        out = [
            jax.ShapeDtypeStruct(q.shape, F32),
            jax.ShapeDtypeStruct((2, q.shape[0], 128), F32),
        ]
    else:
        out = jax.ShapeDtypeStruct(q.shape, BF)
    return pl.pallas_call(
        functools.partial(attention_kernel, own),
        out_shape=out,
        in_specs=[pl.BlockSpec(memory_space=pltpu.SMEM)]
        + [pl.BlockSpec(memory_space=pltpu.VMEM)] * len(args),
        compiler_params=params(16),
        name="attention",
    )(pos, *args)


def out_kernel(pos_ref, a_ref, own_ref, n0_ref, n1_ref, n2_ref, far_ref, out_ref, w_ref):
    def store(source, half, ref, index):
        if ref is own_ref:
            value = ref[index * 48 : index * 48 + 48, :]
        elif index is None:
            value = ref[1]
        else:
            value = ref[index, 1]
        w_ref[source, half] = value

    assemble(pos_ref, own_ref, (n0_ref, n1_ref, n2_ref), far_ref, store)
    w = w_ref[...].reshape(384, out_ref.shape[1])
    out_ref[...] = lax.dot_general(
        a_ref[...], w, NN, preferred_element_type=F32
    ).astype(BF)


def out_projection(pos, a, own, near, far):
    width = own.shape[1]
    return pl.pallas_call(
        out_kernel,
        out_shape=jax.ShapeDtypeStruct((a.shape[0], width), BF),
        in_specs=[pl.BlockSpec(memory_space=pltpu.SMEM)]
        + [pl.BlockSpec(memory_space=pltpu.VMEM)] * 6,
        scratch_shapes=[pltpu.VMEM((4, 2, 48, width), BF)],
        compiler_params=params(8),
        name="out_projection",
    )(pos, a, own, *near, far)


def pack_kernel(pos_ref, up_ref, down_ref, out_ref, sem):
    @pl.when(pos_ref[0] == 0)
    def _():
        copy = pltpu.make_async_copy(up_ref, out_ref, sem.at[0])
        copy.start()
        copy.wait()

    @pl.when(pos_ref[0] == 1)
    def _():
        part = down_ref.shape[0]
        copies = []
        for s in range(4):
            copies.append(
                pltpu.make_async_copy(
                    down_ref.at[:, pl.ds(s * part, part)],
                    out_ref.at[pl.ds(s * part, part), :],
                    sem.at[s],
                )
            )
        for copy in copies:
            copy.start()
        for copy in copies:
            copy.wait()


def pack_ffn(pos, w_up, w_down):
    return pl.pallas_call(
        pack_kernel,
        out_shape=jax.ShapeDtypeStruct(w_up.shape, BF),
        in_specs=[
            pl.BlockSpec(memory_space=pltpu.SMEM),
            pl.BlockSpec(memory_space=pltpu.HBM),
            pl.BlockSpec(memory_space=pltpu.HBM),
        ],
        out_specs=pl.BlockSpec(memory_space=pltpu.HBM),
        scratch_shapes=[pltpu.SemaphoreType.DMA((4,))],
        compiler_params=params(60),
        name="pack_ffn",
    )(pos, w_up, w_down)


def second_norm_kernel(x_ref, part_ref, mod_ref, second_ref, out_ref):
    proj = part_ref[0].astype(F32)
    for i in range(1, part_ref.shape[0]):
        proj += part_ref[i].astype(F32)
    second = (x_ref[...].astype(F32) + mod_ref[2:3, :] * proj).astype(BF)
    second_ref[...] = second
    h = layer_norm(second.astype(F32), mod_ref[3:4, :], mod_ref[4:5, :]).astype(BF)
    for i in range(out_ref.shape[0]):
        out_ref[i] = h


def second_norm(tokens, parts, mods):
    return pl.pallas_call(
        second_norm_kernel,
        out_shape=[
            jax.ShapeDtypeStruct(tokens.shape, BF),
            jax.ShapeDtypeStruct(parts.shape, BF),
        ],
        compiler_params=params(6),
        name="second_norm",
    )(tokens, parts, mods)


def ffn_kernel(h_ref, up_ref, down_ref, out_ref, hidden_ref):
    step = pl.program_id(0)
    part = up_ref.shape[-1]

    @pl.when(step < 2)
    def _():
        up = jnp.concatenate([up_ref[0, 0], up_ref[0, 1]], axis=1)
        hidden_ref[lax.rem(step, 2)] = jax.nn.gelu(
            lax.dot_general(h_ref[...], up, NN, preferred_element_type=F32),
            approximate=True,
        ).astype(BF)

    @pl.when(step >= 2)
    def _():
        hidden = jnp.concatenate([hidden_ref[0], hidden_ref[1]], axis=1)
        down = jnp.concatenate(
            [
                jnp.concatenate([down_ref[0, y, :part], down_ref[0, y, part:]], axis=1)
                for y in range(4)
            ],
            axis=0,
        )
        out_ref[...] = lax.dot_general(
            hidden, down, NN, preferred_element_type=F32
        ).astype(BF)


def feed_forward(h, weights):
    rows, width = h.shape
    part = weights.shape[3]
    return pl.pallas_call(
        ffn_kernel,
        grid=(4,),
        out_shape=jax.ShapeDtypeStruct((rows, width), BF),
        in_specs=[
            pl.BlockSpec((rows, width), lambda i: (0, 0)),
            pl.BlockSpec((1, 2, width, part), lambda i: (0, jnp.minimum(i, 1), 0, 0)),
            pl.BlockSpec((1, 4, 2 * part, part), lambda i: (1, 0, jnp.maximum(i - 2, 0), 0)),
        ],
        out_specs=pl.BlockSpec((rows, 2 * part), lambda i: (0, jnp.maximum(i - 2, 0))),
        scratch_shapes=[pltpu.VMEM((2, rows, 2 * part), BF)],
        compiler_params=params(58),
        name="feed_forward",
    )(h, weights, weights)


def last_kernel(second_ref, part_ref, mod_ref, w_ref, state_ref, vel_ref):
    ffn = part_ref[0].astype(F32)
    for i in range(1, part_ref.shape[0]):
        ffn += part_ref[i].astype(F32)
    state = (second_ref[...].astype(F32) + mod_ref[5:6, :] * ffn).astype(BF)
    state_ref[...] = state
    h = layer_norm(state.astype(F32), mod_ref[6:7, :], mod_ref[7:8, :]).astype(BF)
    vel_ref[...] = lax.dot_general(h, w_ref[...], NN, preferred_element_type=F32)


def last_stage(second, parts, mods, w_final):
    return pl.pallas_call(
        last_kernel,
        out_shape=[
            jax.ShapeDtypeStruct(second.shape, BF),
            jax.ShapeDtypeStruct((second.shape[0], w_final.shape[1]), F32),
        ],
        compiler_params=params(6),
        name="last_stage",
    )(second, parts, mods, w_final)


def on_device(
    image_tokens,
    latent,
    modulation,
    text_kv,
    text_len,
    timestep,
    w_qkv,
    w_out,
    w_up,
    w_down,
    w_final,
):
    tokens = image_tokens[0]
    mods = modulation[0]
    rows, width = tokens.shape
    core = lax.axis_index("core")
    pos = jnp.concatenate([jnp.stack([core, lax.axis_index("ty")]).astype(jnp.int32), text_len])
    swap2 = [(0, 1), (1, 0)]

    def to_lines(value, step):
        return lax.ppermute(value, "ty", [(i, (i + step) % 4) for i in range(4)])

    own_qkv = jnp.transpose(w_qkv, (1, 2, 0))
    half_kv = lax.dynamic_slice(own_qkv, (1, core * 48, 0), (2, 48, width))
    h1 = first_norm(tokens, mods, 4)
    h1, half_kv = lax.optimization_barrier((h1, half_kv))
    h1 = lax.all_to_all(h1, "tx", split_axis=0, concat_axis=0, tiled=True)
    near_kv = [to_lines(half_kv, step) for step in STRIDES]

    half_q = lax.dynamic_slice(own_qkv, (0, core * 48, 0), (1, 48, width))
    half_out = lax.dynamic_slice(w_out, (core * 48, 0), (48, width))
    half_qo = jnp.concatenate([half_q, half_out[None]])
    text = lax.dynamic_slice_in_dim(text_kv[0], lax.axis_index("tx") * 384, 384, 2)
    text = jnp.transpose(text, (1, 0, 2))
    half_ffn = pack_ffn(core[None].astype(jnp.int32), w_up, w_down)
    ffn_full = lax.all_gather(half_ffn, ("core", "tx"), axis=0, tiled=False)
    ffn_full = ffn_full.reshape(2, 4, width, w_up.shape[1])

    far_kv = lax.ppermute(jnp.stack(near_kv), "core", swap2)
    h1, half_qo, text = lax.optimization_barrier((h1, half_qo, text))
    near_qo = [to_lines(half_qo, step) for step in STRIDES]
    h1 = h1.reshape(4 * rows, width)
    own_kv = project(pos, h1, own_qkv, 1, 2, 4, near_kv, far_kv)
    all_kv = lax.all_to_all(own_kv, "ty", split_axis=0, concat_axis=0, tiled=True)
    *near_qo, own_kv = lax.optimization_barrier((*near_qo, own_kv))
    far_qo = lax.ppermute(jnp.stack(near_qo), "core", swap2)
    query = project(pos, h1, own_qkv, 0, 1, 1, near_qo, far_qo)[0, 0]

    state = attention(pos, query, own_kv, text=text)
    attended = attention(pos, query, all_kv, state=state)

    partial = out_projection(pos, attended, w_out, near_qo, far_qo)
    partial = partial.reshape(4, rows, width)
    partial = lax.all_to_all(partial, "tx", split_axis=0, concat_axis=0, tiled=True)
    second, h2 = second_norm(tokens, partial, mods)
    h2 = lax.all_to_all(h2, "ty", split_axis=0, concat_axis=0, tiled=True)
    partial = feed_forward(h2.reshape(4 * rows, width), ffn_full).reshape(4, rows, width)
    partial = lax.all_to_all(partial, "ty", split_axis=0, concat_axis=0, tiled=True)
    state, velocity = last_stage(second, partial, mods, w_final)

    step_index = timestep[0]
    delta = sigma_at(step_index + 1) - sigma_at(step_index)
    moved = latent[0] + delta * velocity.reshape(rows // 2, 2 * velocity.shape[1])
    return (state[None], moved[None])


def solution(mesh):
    fine = Mesh(
        mesh.devices.reshape(mesh.shape["req"] // 2, 2, 4, 4, mesh.shape["blk"]),
        ("zl", "core", "tx", "ty", "blk"),
    )
    group = ("zl", "core", "blk")
    tile = ("tx", "ty")
    in_specs = (
        P(group, tile, None),
        P(group, tile, None),
        P(group, None, None),
        P(group, None, None, None),
        P(group),
        P(group),
        P(None, None, tile),
        P(tile, None),
        P(None, tile),
        P(tile, None),
        P(),
    )
    out_specs = (P(group, tile, None), P(group, tile, None))
    return jax.shard_map(
        on_device, mesh=fine, in_specs=in_specs, out_specs=out_specs, check_vma=False
    )
```

```python
import functools

import jax
import jax.numpy as jnp
from jax import lax
from jax.experimental import pallas as pl
from jax.experimental.pallas import tpu as pltpu
from jax.sharding import Mesh, PartitionSpec as P

HEAD_DIM = 64
TXT = 154
STEPS = 8
BF = jnp.bfloat16
F32 = jnp.float32
NT = (((1,), (1,)), ((), ()))
NN = (((1,), (0,)), ((), ()))
STRIDES = (1, 3, 2)


def params(mebibytes):
    return pltpu.CompilerParams(vmem_limit_bytes=mebibytes * 1024 * 1024)


def layer_norm(full, shift, scale):
    mean = jnp.mean(full, axis=-1, keepdims=True)
    cent = full - mean
    spread = jnp.mean(jnp.square(cent), axis=-1, keepdims=True)
    return cent * lax.rsqrt(spread + 1e-06) * (1.0 + scale) + shift


def sigma_at(index):
    frac = 1.0 - index.astype(F32) / STEPS
    return 3.0 * frac / (1.0 + 2.0 * frac)


def norm_kernel(copies, x_ref, mod_ref, out_ref):
    h = layer_norm(x_ref[...].astype(F32), mod_ref[0:1, :], mod_ref[1:2, :]).astype(BF)
    for i in range(copies):
        out_ref[i] = h


def first_norm(tokens, mods, copies):
    rows, width = tokens.shape
    return pl.pallas_call(
        functools.partial(norm_kernel, copies),
        out_shape=jax.ShapeDtypeStruct((copies, rows, width), BF),
        compiler_params=params(6),
        name="first_norm",
    )(tokens, mods)


def assemble(pos_ref, own_ref, near_refs, far_ref, store):
    core = pos_ref[0]
    row = pos_ref[1]
    store(row, 0, own_ref, 0)
    store(row, 1, own_ref, 1)
    for i, (near_ref, step) in enumerate(zip(near_refs, STRIDES)):
        source = lax.rem(row + 4 - step, 4)
        store(source, core, near_ref, None)
        store(source, 1 - core, far_ref, i)


def project_kernel(first, pos_ref, h_ref, own_ref, n0_ref, n1_ref, n2_ref, far_ref, out_ref, w_ref):
    count = out_ref.shape[1]

    def store(source, half, ref, index):
        for k in range(count):
            if ref is own_ref:
                value = ref[first + k, index * 48 : index * 48 + 48, :]
            elif index is None:
                value = ref[k]
            else:
                value = ref[index, k]
            w_ref[k, source, half] = value

    assemble(pos_ref, own_ref, (n0_ref, n1_ref, n2_ref), far_ref, store)
    h = h_ref[...]
    for k in range(count):
        w = w_ref[k].reshape(384, h.shape[1])
        value = lax.dot_general(h, w, NT, preferred_element_type=F32).astype(BF)
        for i in range(out_ref.shape[0]):
            out_ref[i, k] = value


def project(pos, h, own, first, count, copies, near, far):
    rows, width = h.shape
    return pl.pallas_call(
        functools.partial(project_kernel, first),
        out_shape=jax.ShapeDtypeStruct((copies, count, rows, 384), BF),
        in_specs=[pl.BlockSpec(memory_space=pltpu.SMEM)]
        + [pl.BlockSpec(memory_space=pltpu.VMEM)] * 6,
        scratch_shapes=[pltpu.VMEM((count, 4, 2, 48, width), BF)],
        compiler_params=params(14),
        name="project",
    )(pos, h, own, *near, far)


def attention_kernel(own, *refs):
    refs = list(refs)
    pos_ref, q_ref, kv_ref = refs[:3]
    if own:
        text_ref = refs[3]
        outs = refs[4:]
    else:
        acc_ref, stat_ref = refs[3:5]
        outs = refs[5:]
    rows = q_ref.shape[0]
    if own:
        live = lax.broadcasted_iota(jnp.int32, (rows, TXT), 1) < pos_ref[2]
    first = lax.broadcasted_iota(jnp.int32, (rows, 128), 1) < HEAD_DIM
    where = [0] if own else [lax.rem(pos_ref[1] + i, 4) for i in (1, 2, 3)]
    lane = lax.broadcasted_iota(jnp.int32, (rows, 128), 1)
    tops = jnp.zeros((rows, 128), F32)
    totals = jnp.zeros((rows, 128), F32)
    for g in range(q_ref.shape[1] // 128):
        cols = slice(g * 128, g * 128 + 128)
        q = q_ref[:, cols]
        accs = []
        scales = []
        for side in range(2):
            head = 2 * g + side
            here = first if side == 0 else jnp.logical_not(first)
            qh = jnp.where(here, q, jnp.zeros_like(q))
            parts = []
            for i in where:
                s = (
                    lax.dot_general(qh, kv_ref[i, 0, :, cols], NT, preferred_element_type=F32)
                    * 0.125
                )
                parts.append((s, kv_ref[i, 1, :, cols]))
            if own:
                s = (
                    lax.dot_general(qh, text_ref[0, :, cols], NT, preferred_element_type=F32)
                    * 0.125
                )
                parts.append((jnp.where(live, s, -jnp.inf), text_ref[1, :, cols]))
            top = None
            for s, _ in parts:
                peak = jnp.max(s, axis=1, keepdims=True)
                top = peak if top is None else jnp.maximum(top, peak)
            if not own:
                old = stat_ref[0, :, head : head + 1]
                top = jnp.maximum(top, old)
            total = None
            acc = None
            for s, values in parts:
                p = jnp.exp(s - top)
                amount = jnp.sum(p, axis=1, keepdims=True)
                part = lax.dot_general(p.astype(BF), values, NN, preferred_element_type=F32)
                total = amount if total is None else total + amount
                acc = part if acc is None else acc + part
            if own:
                tops = jnp.where(lane == head, top, tops)
                totals = jnp.where(lane == head, total, totals)
            else:
                factor = jnp.exp(old - top)
                total = total + stat_ref[1, :, head : head + 1] * factor
                scales.append((factor, total))
            accs.append(acc)
        acc = jnp.where(first, accs[0], accs[1])
        if own:
            outs[0][:, cols] = acc
        else:
            factor = jnp.where(first, scales[0][0], scales[1][0])
            total = jnp.where(first, scales[0][1], scales[1][1])
            outs[0][:, cols] = ((acc + acc_ref[:, cols] * factor) / total).astype(BF)
    if own:
        outs[1][0] = tops
        outs[1][1] = totals


def attention(pos, q, kv, text=None, state=None):
    own = text is not None
    args = [q, kv] + ([text] if own else list(state))
    if own:
        out = [
            jax.ShapeDtypeStruct(q.shape, F32),
            jax.ShapeDtypeStruct((2, q.shape[0], 128), F32),
        ]
    else:
        out = jax.ShapeDtypeStruct(q.shape, BF)
    return pl.pallas_call(
        functools.partial(attention_kernel, own),
        out_shape=out,
        in_specs=[pl.BlockSpec(memory_space=pltpu.SMEM)]
        + [pl.BlockSpec(memory_space=pltpu.VMEM)] * len(args),
        compiler_params=params(16),
        name="attention",
    )(pos, *args)


def out_kernel(pos_ref, a_ref, own_ref, n0_ref, n1_ref, n2_ref, far_ref, out_ref, w_ref):
    def store(source, half, ref, index):
        if ref is own_ref:
            value = ref[index * 48 : index * 48 + 48, :]
        elif index is None:
            value = ref[1]
        else:
            value = ref[index, 1]
        w_ref[source, half] = value

    assemble(pos_ref, own_ref, (n0_ref, n1_ref, n2_ref), far_ref, store)
    w = w_ref[...].reshape(384, out_ref.shape[1])
    out_ref[...] = lax.dot_general(
        a_ref[...], w, NN, preferred_element_type=F32
    ).astype(BF)


def out_projection(pos, a, own, near, far):
    width = own.shape[1]
    return pl.pallas_call(
        out_kernel,
        out_shape=jax.ShapeDtypeStruct((a.shape[0], width), BF),
        in_specs=[pl.BlockSpec(memory_space=pltpu.SMEM)]
        + [pl.BlockSpec(memory_space=pltpu.VMEM)] * 6,
        scratch_shapes=[pltpu.VMEM((4, 2, 48, width), BF)],
        compiler_params=params(8),
        name="out_projection",
    )(pos, a, own, *near, far)


def pack_kernel(pos_ref, up_ref, down_ref, out_ref, held, load_sem, store_sem):
    core = pos_ref[0]
    zone = pos_ref[1]
    part = down_ref.shape[0]

    def move(sources):
        loads = []
        stores = []
        for i, source in enumerate(sources):
            rows = pl.ds(i * part, part)
            loads.append(pltpu.make_async_copy(source, held.at[rows, :], load_sem.at[i]))
            stores.append(
                pltpu.make_async_copy(held.at[rows, :], out_ref.at[rows, :], store_sem.at[i])
            )
        for load in loads:
            load.start()
        for load, store in zip(loads, stores):
            load.wait()
            store.start()
        for store in stores:
            store.wait()

    for half in range(2):

        @pl.when(jnp.logical_and(core == 0, zone == half))
        def _():
            move([up_ref.at[pl.ds((2 * half + i) * part, part), :] for i in range(2)])

        @pl.when(jnp.logical_and(core == 1, zone == half))
        def _():
            move([down_ref.at[:, pl.ds((2 * half + i) * part, part)] for i in range(2)])


def pack_ffn(pos, w_up, w_down):
    part = w_down.shape[0]
    return pl.pallas_call(
        pack_kernel,
        out_shape=jax.ShapeDtypeStruct((2 * part, part), BF),
        in_specs=[
            pl.BlockSpec(memory_space=pltpu.SMEM),
            pl.BlockSpec(memory_space=pltpu.HBM),
            pl.BlockSpec(memory_space=pltpu.HBM),
        ],
        out_specs=pl.BlockSpec(memory_space=pltpu.HBM),
        scratch_shapes=[
            pltpu.VMEM((2 * part, part), BF),
            pltpu.SemaphoreType.DMA((2,)),
            pltpu.SemaphoreType.DMA((2,)),
        ],
        compiler_params=params(58),
        name="pack_ffn",
    )(pos, w_up, w_down)


def second_norm_kernel(x_ref, part_ref, mod_ref, second_ref, out_ref):
    proj = part_ref[0].astype(F32)
    for i in range(1, part_ref.shape[0]):
        proj += part_ref[i].astype(F32)
    second = (x_ref[...].astype(F32) + mod_ref[2:3, :] * proj).astype(BF)
    second_ref[...] = second
    h = layer_norm(second.astype(F32), mod_ref[3:4, :], mod_ref[4:5, :]).astype(BF)
    for i in range(out_ref.shape[0]):
        out_ref[i] = h


def second_norm(tokens, parts, mods):
    return pl.pallas_call(
        second_norm_kernel,
        out_shape=[
            jax.ShapeDtypeStruct(tokens.shape, BF),
            jax.ShapeDtypeStruct(parts.shape, BF),
        ],
        compiler_params=params(6),
        name="second_norm",
    )(tokens, parts, mods)


def ffn_kernel(h_ref, up_ref, down_ref, out_ref, hidden_ref):
    step = pl.program_id(0)
    part = up_ref.shape[-1]

    @pl.when(step < 2)
    def _():
        up = jnp.concatenate([up_ref[0, 0], up_ref[0, 1]], axis=1)
        hidden_ref[lax.rem(step, 2)] = jax.nn.gelu(
            lax.dot_general(h_ref[...], up, NN, preferred_element_type=F32),
            approximate=True,
        ).astype(BF)

    @pl.when(step >= 2)
    def _():
        hidden = jnp.concatenate([hidden_ref[0], hidden_ref[1]], axis=1)
        down = jnp.concatenate(
            [
                jnp.concatenate([down_ref[0, y, :part], down_ref[0, y, part:]], axis=1)
                for y in range(4)
            ],
            axis=0,
        )
        out_ref[...] = lax.dot_general(
            hidden, down, NN, preferred_element_type=F32
        ).astype(BF)


def feed_forward(h, weights):
    rows, width = h.shape
    part = weights.shape[3]
    return pl.pallas_call(
        ffn_kernel,
        grid=(4,),
        out_shape=jax.ShapeDtypeStruct((rows, width), BF),
        in_specs=[
            pl.BlockSpec((rows, width), lambda i: (0, 0)),
            pl.BlockSpec((1, 2, width, part), lambda i: (0, jnp.minimum(i, 1), 0, 0)),
            pl.BlockSpec((1, 4, 2 * part, part), lambda i: (1, 0, jnp.maximum(i - 2, 0), 0)),
        ],
        out_specs=pl.BlockSpec((rows, 2 * part), lambda i: (0, jnp.maximum(i - 2, 0))),
        scratch_shapes=[pltpu.VMEM((2, rows, 2 * part), BF)],
        compiler_params=params(58),
        name="feed_forward",
    )(h, weights, weights)


def last_kernel(second_ref, part_ref, mod_ref, w_ref, state_ref, vel_ref):
    ffn = part_ref[0].astype(F32)
    for i in range(1, part_ref.shape[0]):
        ffn += part_ref[i].astype(F32)
    state = (second_ref[...].astype(F32) + mod_ref[5:6, :] * ffn).astype(BF)
    state_ref[...] = state
    h = layer_norm(state.astype(F32), mod_ref[6:7, :], mod_ref[7:8, :]).astype(BF)
    vel_ref[...] = lax.dot_general(h, w_ref[...], NN, preferred_element_type=F32)


def last_stage(second, parts, mods, w_final):
    return pl.pallas_call(
        last_kernel,
        out_shape=[
            jax.ShapeDtypeStruct(second.shape, BF),
            jax.ShapeDtypeStruct((second.shape[0], w_final.shape[1]), F32),
        ],
        compiler_params=params(6),
        name="last_stage",
    )(second, parts, mods, w_final)


def on_device(
    image_tokens,
    latent,
    modulation,
    text_kv,
    text_len,
    timestep,
    w_qkv,
    w_out,
    w_up,
    w_down,
    w_final,
):
    tokens = image_tokens[0]
    mods = modulation[0]
    rows, width = tokens.shape
    core = lax.axis_index("core")
    pos = jnp.concatenate([jnp.stack([core, lax.axis_index("ty")]).astype(jnp.int32), text_len])
    swap2 = [(0, 1), (1, 0)]

    def to_lines(value, step):
        return lax.ppermute(value, "ty", [(i, (i + step) % 4) for i in range(4)])

    own_qkv = jnp.transpose(w_qkv, (1, 2, 0))
    half_kv = lax.dynamic_slice(own_qkv, (1, core * 48, 0), (2, 48, width))
    h1 = first_norm(tokens, mods, 4)
    h1, half_kv = lax.optimization_barrier((h1, half_kv))
    h1 = lax.all_to_all(h1, "tx", split_axis=0, concat_axis=0, tiled=True)
    near_kv = [to_lines(half_kv, step) for step in STRIDES]

    half_q = lax.dynamic_slice(own_qkv, (0, core * 48, 0), (1, 48, width))
    half_out = lax.dynamic_slice(w_out, (core * 48, 0), (48, width))
    half_qo = jnp.concatenate([half_q, half_out[None]])
    text = lax.dynamic_slice_in_dim(text_kv[0], lax.axis_index("tx") * 384, 384, 2)
    text = jnp.transpose(text, (1, 0, 2))
    place = jnp.stack([core, lax.axis_index("zp")]).astype(jnp.int32)
    quarter = pack_ffn(place, w_up, w_down)
    ffn_full = lax.all_gather(quarter, ("core", "tx", "zp"), axis=0, tiled=False)
    ffn_full = ffn_full.reshape(2, 4, width, w_up.shape[1])

    far_kv = lax.ppermute(jnp.stack(near_kv), "core", swap2)
    h1, half_qo, text = lax.optimization_barrier((h1, half_qo, text))
    near_qo = [to_lines(half_qo, step) for step in STRIDES]
    h1 = h1.reshape(4 * rows, width)
    own_kv = project(pos, h1, own_qkv, 1, 2, 4, near_kv, far_kv)
    all_kv = lax.all_to_all(own_kv, "ty", split_axis=0, concat_axis=0, tiled=True)
    *near_qo, own_kv = lax.optimization_barrier((*near_qo, own_kv))
    far_qo = lax.ppermute(jnp.stack(near_qo), "core", swap2)
    query = project(pos, h1, own_qkv, 0, 1, 1, near_qo, far_qo)[0, 0]

    state = attention(pos, query, own_kv, text=text)
    attended = attention(pos, query, all_kv, state=state)

    partial = out_projection(pos, attended, w_out, near_qo, far_qo)
    partial = partial.reshape(4, rows, width)
    partial = lax.all_to_all(partial, "tx", split_axis=0, concat_axis=0, tiled=True)
    second, h2 = second_norm(tokens, partial, mods)
    h2 = lax.all_to_all(h2, "ty", split_axis=0, concat_axis=0, tiled=True)
    partial = feed_forward(h2.reshape(4 * rows, width), ffn_full).reshape(4, rows, width)
    partial = lax.all_to_all(partial, "ty", split_axis=0, concat_axis=0, tiled=True)
    state, velocity = last_stage(second, partial, mods, w_final)

    step_index = timestep[0]
    delta = sigma_at(step_index + 1) - sigma_at(step_index)
    moved = latent[0] + delta * velocity.reshape(rows // 2, 2 * velocity.shape[1])
    return (state[None], moved[None])


def solution(mesh):
    fine = Mesh(
        mesh.devices.reshape(mesh.shape["req"] // 4, 2, 2, 4, 4, mesh.shape["blk"]),
        ("zl", "zp", "core", "tx", "ty", "blk"),
    )
    group = ("zl", "zp", "core", "blk")
    tile = ("tx", "ty")
    in_specs = (
        P(group, tile, None),
        P(group, tile, None),
        P(group, None, None),
        P(group, None, None, None),
        P(group),
        P(group),
        P(None, None, tile),
        P(tile, None),
        P(None, tile),
        P(tile, None),
        P(),
    )
    out_specs = (P(group, tile, None), P(group, tile, None))
    return jax.shard_map(
        on_device, mesh=fine, in_specs=in_specs, out_specs=out_specs, check_vma=False
    )
```

```python
import functools

import jax
import jax.numpy as jnp
from jax import lax
from jax.experimental import pallas as pl
from jax.experimental.pallas import tpu as pltpu
from jax.sharding import Mesh, PartitionSpec as P

HEAD_DIM = 64
TXT = 154
STEPS = 8
BF = jnp.bfloat16
F32 = jnp.float32
NT = (((1,), (1,)), ((), ()))
NN = (((1,), (0,)), ((), ()))
STRIDES = (1, 3, 2)


def params(mebibytes):
    return pltpu.CompilerParams(vmem_limit_bytes=mebibytes * 1024 * 1024)


def layer_norm(full, shift, scale):
    mean = jnp.mean(full, axis=-1, keepdims=True)
    cent = full - mean
    spread = jnp.mean(jnp.square(cent), axis=-1, keepdims=True)
    return cent * lax.rsqrt(spread + 1e-06) * (1.0 + scale) + shift


def sigma_at(index):
    frac = 1.0 - index.astype(F32) / STEPS
    return 3.0 * frac / (1.0 + 2.0 * frac)


def norm_kernel(copies, x_ref, mod_ref, out_ref):
    h = layer_norm(x_ref[...].astype(F32), mod_ref[0:1, :], mod_ref[1:2, :]).astype(BF)
    for i in range(copies):
        out_ref[i] = h


def first_norm(tokens, mods, copies):
    rows, width = tokens.shape
    return pl.pallas_call(
        functools.partial(norm_kernel, copies),
        out_shape=jax.ShapeDtypeStruct((copies, rows, width), BF),
        compiler_params=params(6),
        name="first_norm",
    )(tokens, mods)


def assemble(pos_ref, own_ref, near_refs, far_ref, store):
    core = pos_ref[0]
    row = pos_ref[1]
    store(row, 0, own_ref, 0)
    store(row, 1, own_ref, 1)
    for i, (near_ref, step) in enumerate(zip(near_refs, STRIDES)):
        source = lax.rem(row + 4 - step, 4)
        store(source, core, near_ref, None)
        store(source, 1 - core, far_ref, i)


def project_kernel(first, pos_ref, h_ref, own_ref, n0_ref, n1_ref, n2_ref, far_ref, out_ref, w_ref):
    count = out_ref.shape[1]

    def store(source, half, ref, index):
        for k in range(count):
            if ref is own_ref:
                value = ref[first + k, index * 48 : index * 48 + 48, :]
            elif index is None:
                value = ref[k]
            else:
                value = ref[index, k]
            w_ref[k, source, half] = value

    assemble(pos_ref, own_ref, (n0_ref, n1_ref, n2_ref), far_ref, store)
    h = h_ref[...]
    for k in range(count):
        w = w_ref[k].reshape(384, h.shape[1])
        value = lax.dot_general(h, w, NT, preferred_element_type=F32).astype(BF)
        for i in range(out_ref.shape[0]):
            out_ref[i, k] = value


def project(pos, h, own, first, count, copies, near, far):
    rows, width = h.shape
    return pl.pallas_call(
        functools.partial(project_kernel, first),
        out_shape=jax.ShapeDtypeStruct((copies, count, rows, 384), BF),
        in_specs=[pl.BlockSpec(memory_space=pltpu.SMEM)]
        + [pl.BlockSpec(memory_space=pltpu.VMEM)] * 6,
        scratch_shapes=[pltpu.VMEM((count, 4, 2, 48, width), BF)],
        compiler_params=params(14),
        name="project",
    )(pos, h, own, *near, far)


def attention_kernel(own, *refs):
    refs = list(refs)
    pos_ref, q_ref, kv_ref = refs[:3]
    if own:
        text_ref = refs[3]
        outs = refs[4:]
    else:
        state_ref = refs[3]
        outs = refs[4:]
    rows = q_ref.shape[0]
    if own:
        live = lax.broadcasted_iota(jnp.int32, (rows, TXT), 1) < pos_ref[2]
    first = lax.broadcasted_iota(jnp.int32, (rows, 128), 1) < HEAD_DIM
    where = [0] if own else [lax.rem(pos_ref[1] + i, 4) for i in (1, 2, 3)]
    lane = lax.broadcasted_iota(jnp.int32, (rows, 128), 1)
    stats = jnp.zeros((rows, 128), F32)
    for g in range(q_ref.shape[1] // 128):
        cols = slice(g * 128, g * 128 + 128)
        q = q_ref[:, cols]
        accs = []
        scales = []
        for side in range(2):
            head = 2 * g + side
            here = first if side == 0 else jnp.logical_not(first)
            qh = jnp.where(here, q, jnp.zeros_like(q))
            parts = []
            for i in where:
                s = (
                    lax.dot_general(qh, kv_ref[i, 0, :, cols], NT, preferred_element_type=F32)
                    * 0.125
                )
                parts.append((s, kv_ref[i, 1, :, cols]))
            if own:
                s = (
                    lax.dot_general(qh, text_ref[0, :, cols], NT, preferred_element_type=F32)
                    * 0.125
                )
                parts.append((jnp.where(live, s, -jnp.inf), text_ref[1, :, cols]))
            top = None
            for s, _ in parts:
                peak = jnp.max(s, axis=1, keepdims=True)
                top = peak if top is None else jnp.maximum(top, peak)
            if not own:
                old = state_ref[:, 384 + head : 385 + head]
                top = jnp.maximum(top, old)
            total = None
            acc = None
            for s, values in parts:
                p = jnp.exp(s - top)
                amount = jnp.sum(p, axis=1, keepdims=True)
                part = lax.dot_general(p.astype(BF), values, NN, preferred_element_type=F32)
                total = amount if total is None else total + amount
                acc = part if acc is None else acc + part
            if own:
                stats = jnp.where(lane == head, top, stats)
                stats = jnp.where(lane == HEAD_DIM + head, total, stats)
            else:
                factor = jnp.exp(old - top)
                total = total + state_ref[:, 448 + head : 449 + head] * factor
                scales.append((factor, total))
            accs.append(acc)
        acc = jnp.where(first, accs[0], accs[1])
        if own:
            outs[0][:, cols] = acc
        else:
            factor = jnp.where(first, scales[0][0], scales[1][0])
            total = jnp.where(first, scales[0][1], scales[1][1])
            outs[0][:, cols] = ((acc + state_ref[:, cols] * factor) / total).astype(BF)
    if own:
        outs[0][:, 384:] = stats


def attention(pos, q, kv, text=None, state=None):
    own = text is not None
    args = [q, kv, text if own else state]
    if own:
        out = jax.ShapeDtypeStruct((q.shape[0], 512), F32)
    else:
        out = jax.ShapeDtypeStruct(q.shape, BF)
    return pl.pallas_call(
        functools.partial(attention_kernel, own),
        out_shape=out,
        in_specs=[pl.BlockSpec(memory_space=pltpu.SMEM)]
        + [pl.BlockSpec(memory_space=pltpu.VMEM)] * len(args),
        compiler_params=params(16),
        name="attention",
    )(pos, *args)


def out_kernel(pos_ref, a_ref, own_ref, n0_ref, n1_ref, n2_ref, far_ref, out_ref, w_ref):
    def store(source, half, ref, index):
        if ref is own_ref:
            value = ref[index * 48 : index * 48 + 48, :]
        elif index is None:
            value = ref[1]
        else:
            value = ref[index, 1]
        w_ref[source, half] = value

    assemble(pos_ref, own_ref, (n0_ref, n1_ref, n2_ref), far_ref, store)
    w = w_ref[...].reshape(384, out_ref.shape[1])
    out_ref[...] = lax.dot_general(
        a_ref[...], w, NN, preferred_element_type=F32
    ).astype(BF)


def out_projection(pos, a, own, near, far):
    width = own.shape[1]
    return pl.pallas_call(
        out_kernel,
        out_shape=jax.ShapeDtypeStruct((a.shape[0], width), BF),
        in_specs=[pl.BlockSpec(memory_space=pltpu.SMEM)]
        + [pl.BlockSpec(memory_space=pltpu.VMEM)] * 6,
        scratch_shapes=[pltpu.VMEM((4, 2, 48, width), BF)],
        compiler_params=params(8),
        name="out_projection",
    )(pos, a, own, *near, far)


def pack_kernel(
    pos_ref, n0_ref, n1_ref, n2_ref, up_ref, down_ref, stack_ref, out_ref, held, load_sem, store_sem
):
    core = pos_ref[0]
    zone = pos_ref[1]
    part = down_ref.shape[0]

    def move(sources):
        loads = []
        stores = []
        for i, source in enumerate(sources):
            rows = pl.ds(i * part, part)
            loads.append(pltpu.make_async_copy(source, held.at[rows, :], load_sem.at[i]))
            stores.append(
                pltpu.make_async_copy(held.at[rows, :], out_ref.at[rows, :], store_sem.at[i])
            )
        for load in loads:
            load.start()
        for i, ref in enumerate((n0_ref, n1_ref, n2_ref)):
            stack_ref[i] = ref[...]
        for load, store in zip(loads, stores):
            load.wait()
            store.start()
        for store in stores:
            store.wait()

    for half in range(2):

        @pl.when(jnp.logical_and(core == 0, zone == half))
        def _():
            move([up_ref.at[pl.ds((2 * half + i) * part, part), :] for i in range(2)])

        @pl.when(jnp.logical_and(core == 1, zone == half))
        def _():
            move([down_ref.at[:, pl.ds((2 * half + i) * part, part)] for i in range(2)])


def stack_and_pack(pos, near, w_up, w_down):
    part = w_down.shape[0]
    return pl.pallas_call(
        pack_kernel,
        out_shape=[
            jax.ShapeDtypeStruct((3, *near[0].shape), BF),
            jax.ShapeDtypeStruct((2 * part, part), BF),
        ],
        in_specs=[pl.BlockSpec(memory_space=pltpu.SMEM)]
        + [pl.BlockSpec(memory_space=pltpu.VMEM)] * 3
        + [pl.BlockSpec(memory_space=pltpu.HBM)] * 2,
        out_specs=[
            pl.BlockSpec(memory_space=pltpu.VMEM),
            pl.BlockSpec(memory_space=pltpu.HBM),
        ],
        scratch_shapes=[
            pltpu.VMEM((2 * part, part), BF),
            pltpu.SemaphoreType.DMA((2,)),
            pltpu.SemaphoreType.DMA((2,)),
        ],
        compiler_params=params(58),
        name="stack_and_pack",
    )(pos, *near, w_up, w_down)


def second_norm_kernel(x_ref, part_ref, mod_ref, second_ref, out_ref):
    proj = part_ref[0].astype(F32)
    for i in range(1, part_ref.shape[0]):
        proj += part_ref[i].astype(F32)
    second = (x_ref[...].astype(F32) + mod_ref[2:3, :] * proj).astype(BF)
    second_ref[...] = second
    h = layer_norm(second.astype(F32), mod_ref[3:4, :], mod_ref[4:5, :]).astype(BF)
    for i in range(out_ref.shape[0]):
        out_ref[i] = h


def second_norm(tokens, parts, mods):
    return pl.pallas_call(
        second_norm_kernel,
        out_shape=[
            jax.ShapeDtypeStruct(tokens.shape, BF),
            jax.ShapeDtypeStruct(parts.shape, BF),
        ],
        compiler_params=params(6),
        name="second_norm",
    )(tokens, parts, mods)


def ffn_kernel(h_ref, up_ref, down_ref, out_ref, hidden_ref):
    step = pl.program_id(0)
    part = up_ref.shape[-1]

    @pl.when(step < 2)
    def _():
        up = jnp.concatenate([up_ref[0, 0], up_ref[0, 1]], axis=1)
        hidden_ref[lax.rem(step, 2)] = jax.nn.gelu(
            lax.dot_general(h_ref[...], up, NN, preferred_element_type=F32),
            approximate=True,
        ).astype(BF)

    @pl.when(step >= 2)
    def _():
        hidden = jnp.concatenate([hidden_ref[0], hidden_ref[1]], axis=1)
        down = jnp.concatenate(
            [
                jnp.concatenate([down_ref[0, y, :part], down_ref[0, y, part:]], axis=1)
                for y in range(4)
            ],
            axis=0,
        )
        out_ref[...] = lax.dot_general(
            hidden, down, NN, preferred_element_type=F32
        ).astype(BF)


def feed_forward(h, weights):
    rows, width = h.shape
    part = weights.shape[3]
    return pl.pallas_call(
        ffn_kernel,
        grid=(4,),
        out_shape=jax.ShapeDtypeStruct((rows, width), BF),
        in_specs=[
            pl.BlockSpec((rows, width), lambda i: (0, 0)),
            pl.BlockSpec((1, 2, width, part), lambda i: (0, jnp.minimum(i, 1), 0, 0)),
            pl.BlockSpec((1, 4, 2 * part, part), lambda i: (1, 0, jnp.maximum(i - 2, 0), 0)),
        ],
        out_specs=pl.BlockSpec((rows, 2 * part), lambda i: (0, jnp.maximum(i - 2, 0))),
        scratch_shapes=[pltpu.VMEM((2, rows, 2 * part), BF)],
        compiler_params=params(58),
        name="feed_forward",
    )(h, weights, weights)


def last_kernel(second_ref, part_ref, mod_ref, w_ref, state_ref, vel_ref):
    ffn = part_ref[0].astype(F32)
    for i in range(1, part_ref.shape[0]):
        ffn += part_ref[i].astype(F32)
    state = (second_ref[...].astype(F32) + mod_ref[5:6, :] * ffn).astype(BF)
    state_ref[...] = state
    h = layer_norm(state.astype(F32), mod_ref[6:7, :], mod_ref[7:8, :]).astype(BF)
    vel_ref[...] = lax.dot_general(h, w_ref[...], NN, preferred_element_type=F32)


def last_stage(second, parts, mods, w_final):
    return pl.pallas_call(
        last_kernel,
        out_shape=[
            jax.ShapeDtypeStruct(second.shape, BF),
            jax.ShapeDtypeStruct((second.shape[0], w_final.shape[1]), F32),
        ],
        compiler_params=params(6),
        name="last_stage",
    )(second, parts, mods, w_final)


def on_device(
    image_tokens,
    latent,
    modulation,
    text_kv,
    text_len,
    timestep,
    w_qkv,
    w_out,
    w_up,
    w_down,
    w_final,
):
    tokens = image_tokens[0]
    mods = modulation[0]
    rows, width = tokens.shape
    core = lax.axis_index("core")
    pos = jnp.concatenate([jnp.stack([core, lax.axis_index("ty")]).astype(jnp.int32), text_len])
    swap2 = [(0, 1), (1, 0)]

    def to_lines(value, step):
        return lax.ppermute(value, "ty", [(i, (i + step) % 4) for i in range(4)])

    own_qkv = jnp.transpose(w_qkv, (1, 2, 0))
    half_kv = lax.dynamic_slice(own_qkv, (1, core * 48, 0), (2, 48, width))
    h1 = first_norm(tokens, mods, 4)
    h1, half_kv = lax.optimization_barrier((h1, half_kv))
    h1 = lax.all_to_all(h1, "tx", split_axis=0, concat_axis=0, tiled=True)
    near_kv = [to_lines(half_kv, step) for step in STRIDES]

    half_q = lax.dynamic_slice(own_qkv, (0, core * 48, 0), (1, 48, width))
    half_out = lax.dynamic_slice(w_out, (core * 48, 0), (48, width))
    half_qo = jnp.concatenate([half_q, half_out[None]])
    text = lax.dynamic_slice_in_dim(text_kv[0], lax.axis_index("tx") * 384, 384, 2)
    text = jnp.transpose(text, (1, 0, 2))
    place = jnp.stack([core, lax.axis_index("zp")]).astype(jnp.int32)
    *near_kv, h1, half_qo, text = lax.optimization_barrier((*near_kv, h1, half_qo, text))
    stacked, quarter = stack_and_pack(place, near_kv, w_up, w_down)
    ffn_full = lax.all_gather(quarter, ("core", "tx", "zp"), axis=0, tiled=False)
    ffn_full = ffn_full.reshape(2, 4, width, w_up.shape[1])

    stacked, half_qo = lax.optimization_barrier((stacked, half_qo))
    far_kv = lax.ppermute(stacked, "core", swap2)
    near_qo = [to_lines(half_qo, step) for step in STRIDES]
    h1 = h1.reshape(4 * rows, width)
    own_kv = project(pos, h1, own_qkv, 1, 2, 4, near_kv, far_kv)
    all_kv = lax.all_to_all(own_kv, "ty", split_axis=0, concat_axis=0, tiled=True)
    *near_qo, own_kv = lax.optimization_barrier((*near_qo, own_kv))
    far_qo = lax.ppermute(jnp.stack(near_qo), "core", swap2)
    query = project(pos, h1, own_qkv, 0, 1, 1, near_qo, far_qo)[0, 0]

    state = attention(pos, query, own_kv, text=text)
    attended = attention(pos, query, all_kv, state=state)

    partial = out_projection(pos, attended, w_out, near_qo, far_qo)
    partial = partial.reshape(4, rows, width)
    partial = lax.all_to_all(partial, "tx", split_axis=0, concat_axis=0, tiled=True)
    second, h2 = second_norm(tokens, partial, mods)
    h2 = lax.all_to_all(h2, "ty", split_axis=0, concat_axis=0, tiled=True)
    partial = feed_forward(h2.reshape(4 * rows, width), ffn_full).reshape(4, rows, width)
    partial = lax.all_to_all(partial, "ty", split_axis=0, concat_axis=0, tiled=True)
    state, velocity = last_stage(second, partial, mods, w_final)

    step_index = timestep[0]
    delta = sigma_at(step_index + 1) - sigma_at(step_index)
    moved = latent[0] + delta * velocity.reshape(rows // 2, 2 * velocity.shape[1])
    return (state[None], moved[None])


def solution(mesh):
    fine = Mesh(
        mesh.devices.reshape(mesh.shape["req"] // 4, 2, 2, 4, 4, mesh.shape["blk"]),
        ("zl", "zp", "core", "tx", "ty", "blk"),
    )
    group = ("zl", "zp", "core", "blk")
    tile = ("tx", "ty")
    in_specs = (
        P(group, tile, None),
        P(group, tile, None),
        P(group, None, None),
        P(group, None, None, None),
        P(group),
        P(group),
        P(None, None, tile),
        P(tile, None),
        P(None, tile),
        P(tile, None),
        P(),
    )
    out_specs = (P(group, tile, None), P(group, tile, None))
    return jax.shard_map(
        on_device, mesh=fine, in_specs=in_specs, out_specs=out_specs, check_vma=False
    )
```

```python
import functools

import jax
import jax.numpy as jnp
from jax import lax
from jax.experimental import pallas as pl
from jax.experimental.pallas import tpu as pltpu
from jax.sharding import Mesh, PartitionSpec as P

HEAD_DIM = 64
TXT = 154
STEPS = 8
BF = jnp.bfloat16
F32 = jnp.float32
NT = (((1,), (1,)), ((), ()))
NN = (((1,), (0,)), ((), ()))
STRIDES = (1, 3, 2)


def params(mebibytes):
    return pltpu.CompilerParams(vmem_limit_bytes=mebibytes * 1024 * 1024)


def layer_norm(full, shift, scale):
    mean = jnp.mean(full, axis=-1, keepdims=True)
    cent = full - mean
    spread = jnp.mean(jnp.square(cent), axis=-1, keepdims=True)
    return cent * lax.rsqrt(spread + 1e-06) * (1.0 + scale) + shift


def sigma_at(index):
    frac = 1.0 - index.astype(F32) / STEPS
    return 3.0 * frac / (1.0 + 2.0 * frac)


def first_kernel(
    pos_ref,
    x_ref,
    mod_ref,
    up_ref,
    down_ref,
    qkv_ref,
    wout_ref,
    h_ref,
    kv_ref,
    qo_ref,
    pack_ref,
    held,
    load_sem,
    store_sem,
    half_sem,
):
    core = pos_ref[0]
    zone = pos_ref[1]
    part = down_ref.shape[0]

    def move(core_here, sources):
        mine = pl.ds(core_here * 48, 48)
        halves = [
            pltpu.make_async_copy(qkv_ref.at[pl.ds(1, 2), mine, :], kv_ref, half_sem.at[0]),
            pltpu.make_async_copy(qkv_ref.at[0, mine, :], qo_ref.at[0], half_sem.at[1]),
            pltpu.make_async_copy(wout_ref.at[mine, :], qo_ref.at[1], half_sem.at[2]),
        ]
        loads = []
        stores = []
        for i, source in enumerate(sources):
            rows = pl.ds(i * part, part)
            loads.append(pltpu.make_async_copy(source, held.at[rows, :], load_sem.at[i]))
            stores.append(
                pltpu.make_async_copy(held.at[rows, :], pack_ref.at[rows, :], store_sem.at[i])
            )
        for copy in loads + halves:
            copy.start()
        h = layer_norm(x_ref[...].astype(F32), mod_ref[0:1, :], mod_ref[1:2, :]).astype(BF)
        for i in range(h_ref.shape[0]):
            h_ref[i] = h
        for load, store in zip(loads, stores):
            load.wait()
            store.start()
        for copy in halves + stores:
            copy.wait()

    for half in range(2):

        @pl.when(jnp.logical_and(core == 0, zone == half))
        def _():
            move(0, [up_ref.at[pl.ds((2 * half + i) * part, part), :] for i in range(2)])

        @pl.when(jnp.logical_and(core == 1, zone == half))
        def _():
            move(1, [down_ref.at[:, pl.ds((2 * half + i) * part, part)] for i in range(2)])


def first_stage(pos, tokens, mods, w_up, w_down, own_qkv, w_out, copies):
    rows, width = tokens.shape
    part = w_down.shape[0]
    return pl.pallas_call(
        first_kernel,
        out_shape=[
            jax.ShapeDtypeStruct((copies, rows, width), BF),
            jax.ShapeDtypeStruct((2, 48, width), BF),
            jax.ShapeDtypeStruct((2, 48, width), BF),
            jax.ShapeDtypeStruct((2 * part, part), BF),
        ],
        in_specs=[pl.BlockSpec(memory_space=pltpu.SMEM)]
        + [pl.BlockSpec(memory_space=pltpu.VMEM)] * 2
        + [pl.BlockSpec(memory_space=pltpu.HBM)] * 4,
        out_specs=[pl.BlockSpec(memory_space=pltpu.VMEM)] * 3
        + [pl.BlockSpec(memory_space=pltpu.HBM)],
        scratch_shapes=[
            pltpu.VMEM((2 * part, part), BF),
            pltpu.SemaphoreType.DMA((2,)),
            pltpu.SemaphoreType.DMA((2,)),
            pltpu.SemaphoreType.DMA((3,)),
        ],
        compiler_params=params(58),
        name="first_stage",
    )(pos, tokens, mods, w_up, w_down, own_qkv, w_out)


def assemble(pos_ref, own_ref, near_refs, far_ref, store):
    core = pos_ref[0]
    row = pos_ref[1]
    store(row, 0, own_ref, 0)
    store(row, 1, own_ref, 1)
    for i, (near_ref, step) in enumerate(zip(near_refs, STRIDES)):
        source = lax.rem(row + 4 - step, 4)
        store(source, core, near_ref, None)
        store(source, 1 - core, far_ref, i)


def project_kernel(first, pos_ref, h_ref, own_ref, n0_ref, n1_ref, n2_ref, far_ref, out_ref, w_ref):
    count = out_ref.shape[1]

    def store(source, half, ref, index):
        for k in range(count):
            if ref is own_ref:
                value = ref[first + k, index * 48 : index * 48 + 48, :]
            elif index is None:
                value = ref[k]
            else:
                value = ref[index, k]
            w_ref[k, source, half] = value

    assemble(pos_ref, own_ref, (n0_ref, n1_ref, n2_ref), far_ref, store)
    h = h_ref[...]
    for k in range(count):
        w = w_ref[k].reshape(384, h.shape[1])
        value = lax.dot_general(h, w, NT, preferred_element_type=F32).astype(BF)
        for i in range(out_ref.shape[0]):
            out_ref[i, k] = value


def project(pos, h, own, first, count, copies, near, far):
    rows, width = h.shape
    return pl.pallas_call(
        functools.partial(project_kernel, first),
        out_shape=jax.ShapeDtypeStruct((copies, count, rows, 384), BF),
        in_specs=[pl.BlockSpec(memory_space=pltpu.SMEM)]
        + [pl.BlockSpec(memory_space=pltpu.VMEM)] * 6,
        scratch_shapes=[pltpu.VMEM((count, 4, 2, 48, width), BF)],
        compiler_params=params(14),
        name="project",
    )(pos, h, own, *near, far)


def attention_kernel(own, *refs):
    refs = list(refs)
    pos_ref, q_ref, kv_ref = refs[:3]
    if own:
        text_ref = refs[3]
        outs = refs[4:]
    else:
        state_ref = refs[3]
        outs = refs[4:]
    rows = q_ref.shape[0]
    if own:
        live = lax.broadcasted_iota(jnp.int32, (rows, TXT), 1) < pos_ref[2]
    first = lax.broadcasted_iota(jnp.int32, (rows, 128), 1) < HEAD_DIM
    where = [0] if own else [lax.rem(pos_ref[1] + i, 4) for i in (1, 2, 3)]
    lane = lax.broadcasted_iota(jnp.int32, (rows, 128), 1)
    stats = jnp.zeros((rows, 128), F32)
    for g in range(q_ref.shape[1] // 128):
        cols = slice(g * 128, g * 128 + 128)
        q = q_ref[:, cols]
        accs = []
        scales = []
        for side in range(2):
            head = 2 * g + side
            here = first if side == 0 else jnp.logical_not(first)
            qh = jnp.where(here, q, jnp.zeros_like(q))
            parts = []
            for i in where:
                s = (
                    lax.dot_general(qh, kv_ref[i, 0, :, cols], NT, preferred_element_type=F32)
                    * 0.125
                )
                parts.append((s, kv_ref[i, 1, :, cols]))
            if own:
                s = (
                    lax.dot_general(qh, text_ref[0, :, cols], NT, preferred_element_type=F32)
                    * 0.125
                )
                parts.append((jnp.where(live, s, -jnp.inf), text_ref[1, :, cols]))
            top = None
            for s, _ in parts:
                peak = jnp.max(s, axis=1, keepdims=True)
                top = peak if top is None else jnp.maximum(top, peak)
            if not own:
                old = state_ref[:, 384 + head : 385 + head]
                top = jnp.maximum(top, old)
            total = None
            acc = None
            for s, values in parts:
                p = jnp.exp(s - top)
                amount = jnp.sum(p, axis=1, keepdims=True)
                part = lax.dot_general(p.astype(BF), values, NN, preferred_element_type=F32)
                total = amount if total is None else total + amount
                acc = part if acc is None else acc + part
            if own:
                stats = jnp.where(lane == head, top, stats)
                stats = jnp.where(lane == HEAD_DIM + head, total, stats)
            else:
                factor = jnp.exp(old - top)
                total = total + state_ref[:, 448 + head : 449 + head] * factor
                scales.append((factor, total))
            accs.append(acc)
        acc = jnp.where(first, accs[0], accs[1])
        if own:
            outs[0][:, cols] = acc
        else:
            factor = jnp.where(first, scales[0][0], scales[1][0])
            total = jnp.where(first, scales[0][1], scales[1][1])
            outs[0][:, cols] = ((acc + state_ref[:, cols] * factor) / total).astype(BF)
    if own:
        outs[0][:, 384:] = stats


def attention(pos, q, kv, text=None, state=None):
    own = text is not None
    args = [q, kv, text if own else state]
    if own:
        out = jax.ShapeDtypeStruct((q.shape[0], 512), F32)
    else:
        out = jax.ShapeDtypeStruct(q.shape, BF)
    return pl.pallas_call(
        functools.partial(attention_kernel, own),
        out_shape=out,
        in_specs=[pl.BlockSpec(memory_space=pltpu.SMEM)]
        + [pl.BlockSpec(memory_space=pltpu.VMEM)] * len(args),
        compiler_params=params(16),
        name="attention",
    )(pos, *args)


def out_kernel(pos_ref, a_ref, own_ref, n0_ref, n1_ref, n2_ref, far_ref, out_ref, w_ref):
    def store(source, half, ref, index):
        if ref is own_ref:
            value = ref[index * 48 : index * 48 + 48, :]
        elif index is None:
            value = ref[1]
        else:
            value = ref[index, 1]
        w_ref[source, half] = value

    assemble(pos_ref, own_ref, (n0_ref, n1_ref, n2_ref), far_ref, store)
    w = w_ref[...].reshape(384, out_ref.shape[1])
    out_ref[...] = lax.dot_general(
        a_ref[...], w, NN, preferred_element_type=F32
    ).astype(BF)


def out_projection(pos, a, own, near, far):
    width = own.shape[1]
    return pl.pallas_call(
        out_kernel,
        out_shape=jax.ShapeDtypeStruct((a.shape[0], width), BF),
        in_specs=[pl.BlockSpec(memory_space=pltpu.SMEM)]
        + [pl.BlockSpec(memory_space=pltpu.VMEM)] * 6,
        scratch_shapes=[pltpu.VMEM((4, 2, 48, width), BF)],
        compiler_params=params(8),
        name="out_projection",
    )(pos, a, own, *near, far)


def second_norm_kernel(x_ref, part_ref, mod_ref, second_ref, out_ref):
    proj = part_ref[0].astype(F32)
    for i in range(1, part_ref.shape[0]):
        proj += part_ref[i].astype(F32)
    second = (x_ref[...].astype(F32) + mod_ref[2:3, :] * proj).astype(BF)
    second_ref[...] = second
    h = layer_norm(second.astype(F32), mod_ref[3:4, :], mod_ref[4:5, :]).astype(BF)
    for i in range(out_ref.shape[0]):
        out_ref[i] = h


def second_norm(tokens, parts, mods):
    return pl.pallas_call(
        second_norm_kernel,
        out_shape=[
            jax.ShapeDtypeStruct(tokens.shape, BF),
            jax.ShapeDtypeStruct(parts.shape, BF),
        ],
        compiler_params=params(6),
        name="second_norm",
    )(tokens, parts, mods)


def ffn_kernel(h_ref, up_ref, down_ref, out_ref, hidden_ref):
    step = pl.program_id(0)
    part = up_ref.shape[-1]

    @pl.when(step < 2)
    def _():
        up = jnp.concatenate([up_ref[0, 0], up_ref[0, 1]], axis=1)
        hidden_ref[lax.rem(step, 2)] = jax.nn.gelu(
            lax.dot_general(h_ref[...], up, NN, preferred_element_type=F32),
            approximate=True,
        ).astype(BF)

    @pl.when(step >= 2)
    def _():
        hidden = jnp.concatenate([hidden_ref[0], hidden_ref[1]], axis=1)
        down = jnp.concatenate(
            [
                jnp.concatenate([down_ref[0, y, :part], down_ref[0, y, part:]], axis=1)
                for y in range(4)
            ],
            axis=0,
        )
        out_ref[...] = lax.dot_general(
            hidden, down, NN, preferred_element_type=F32
        ).astype(BF)


def feed_forward(h, weights):
    rows, width = h.shape
    part = weights.shape[3]
    return pl.pallas_call(
        ffn_kernel,
        grid=(4,),
        out_shape=jax.ShapeDtypeStruct((rows, width), BF),
        in_specs=[
            pl.BlockSpec((rows, width), lambda i: (0, 0)),
            pl.BlockSpec((1, 2, width, part), lambda i: (0, jnp.minimum(i, 1), 0, 0)),
            pl.BlockSpec((1, 4, 2 * part, part), lambda i: (1, 0, jnp.maximum(i - 2, 0), 0)),
        ],
        out_specs=pl.BlockSpec((rows, 2 * part), lambda i: (0, jnp.maximum(i - 2, 0))),
        scratch_shapes=[pltpu.VMEM((2, rows, 2 * part), BF)],
        compiler_params=params(58),
        name="feed_forward",
    )(h, weights, weights)


def last_kernel(second_ref, part_ref, mod_ref, w_ref, state_ref, vel_ref):
    ffn = part_ref[0].astype(F32)
    for i in range(1, part_ref.shape[0]):
        ffn += part_ref[i].astype(F32)
    state = (second_ref[...].astype(F32) + mod_ref[5:6, :] * ffn).astype(BF)
    state_ref[...] = state
    h = layer_norm(state.astype(F32), mod_ref[6:7, :], mod_ref[7:8, :]).astype(BF)
    vel_ref[...] = lax.dot_general(h, w_ref[...], NN, preferred_element_type=F32)


def last_stage(second, parts, mods, w_final):
    return pl.pallas_call(
        last_kernel,
        out_shape=[
            jax.ShapeDtypeStruct(second.shape, BF),
            jax.ShapeDtypeStruct((second.shape[0], w_final.shape[1]), F32),
        ],
        compiler_params=params(6),
        name="last_stage",
    )(second, parts, mods, w_final)


def on_device(
    image_tokens,
    latent,
    modulation,
    text_kv,
    text_len,
    timestep,
    w_qkv,
    w_out,
    w_up,
    w_down,
    w_final,
):
    tokens = image_tokens[0]
    mods = modulation[0]
    rows, width = tokens.shape
    core = lax.axis_index("core")
    pos = jnp.concatenate([jnp.stack([core, lax.axis_index("ty")]).astype(jnp.int32), text_len])
    swap2 = [(0, 1), (1, 0)]

    def to_lines(value, step):
        return lax.ppermute(value, "ty", [(i, (i + step) % 4) for i in range(4)])

    own_qkv = jnp.transpose(w_qkv, (1, 2, 0))
    place = jnp.stack([core, lax.axis_index("zp")]).astype(jnp.int32)
    h1, half_kv, half_qo, quarter = first_stage(
        place, tokens, mods, w_up, w_down, own_qkv, w_out, 4
    )
    ffn_full = lax.all_gather(quarter, ("core", "tx", "zp"), axis=0, tiled=False)
    ffn_full = ffn_full.reshape(2, 4, width, w_up.shape[1])
    h1 = lax.all_to_all(h1, "tx", split_axis=0, concat_axis=0, tiled=True)
    near_kv = [to_lines(half_kv, step) for step in STRIDES]
    *near_kv, h1 = lax.optimization_barrier((*near_kv, h1))
    stacked, half_qo = lax.optimization_barrier((jnp.stack(near_kv), half_qo))
    far_kv = lax.ppermute(stacked, "core", swap2)
    near_qo = [to_lines(half_qo, step) for step in STRIDES]
    h1 = h1.reshape(4 * rows, width)
    own_kv = project(pos, h1, own_qkv, 1, 2, 4, near_kv, far_kv)
    all_kv = lax.all_to_all(own_kv, "ty", split_axis=0, concat_axis=0, tiled=True)
    *near_qo, own_kv, text_kv = lax.optimization_barrier((*near_qo, own_kv, text_kv))
    text = lax.dynamic_slice_in_dim(text_kv[0], lax.axis_index("tx") * 384, 384, 2)
    text = jnp.transpose(text, (1, 0, 2))
    far_qo = lax.ppermute(jnp.stack(near_qo), "core", swap2)
    query = project(pos, h1, own_qkv, 0, 1, 1, near_qo, far_qo)[0, 0]

    state = attention(pos, query, own_kv, text=text)
    attended = attention(pos, query, all_kv, state=state)

    partial = out_projection(pos, attended, w_out, near_qo, far_qo)
    partial = partial.reshape(4, rows, width)
    partial = lax.all_to_all(partial, "tx", split_axis=0, concat_axis=0, tiled=True)
    second, h2 = second_norm(tokens, partial, mods)
    h2 = lax.all_to_all(h2, "ty", split_axis=0, concat_axis=0, tiled=True)
    partial = feed_forward(h2.reshape(4 * rows, width), ffn_full).reshape(4, rows, width)
    partial = lax.all_to_all(partial, "ty", split_axis=0, concat_axis=0, tiled=True)
    state, velocity = last_stage(second, partial, mods, w_final)

    step_index = timestep[0]
    delta = sigma_at(step_index + 1) - sigma_at(step_index)
    moved = latent[0] + delta * velocity.reshape(rows // 2, 2 * velocity.shape[1])
    return (state[None], moved[None])


def solution(mesh):
    fine = Mesh(
        mesh.devices.reshape(mesh.shape["req"] // 4, 2, 2, 4, 4, mesh.shape["blk"]),
        ("zl", "zp", "core", "tx", "ty", "blk"),
    )
    group = ("zl", "zp", "core", "blk")
    tile = ("tx", "ty")
    in_specs = (
        P(group, tile, None),
        P(group, tile, None),
        P(group, None, None),
        P(group, None, None, None),
        P(group),
        P(group),
        P(None, None, tile),
        P(tile, None),
        P(None, tile),
        P(tile, None),
        P(),
    )
    out_specs = (P(group, tile, None), P(group, tile, None))
    return jax.shard_map(
        on_device, mesh=fine, in_specs=in_specs, out_specs=out_specs, check_vma=False
    )
```

```python
import functools

import jax
import jax.numpy as jnp
from jax import lax
from jax.experimental import pallas as pl
from jax.experimental.pallas import tpu as pltpu
from jax.sharding import Mesh, PartitionSpec as P

HEAD_DIM = 64
TXT = 154
STEPS = 8
BF = jnp.bfloat16
F32 = jnp.float32
NT = (((1,), (1,)), ((), ()))
NN = (((1,), (0,)), ((), ()))
STRIDES = (1, 3, 2)


def params(mebibytes):
    return pltpu.CompilerParams(vmem_limit_bytes=mebibytes * 1024 * 1024)


def layer_norm(full, shift, scale):
    mean = jnp.mean(full, axis=-1, keepdims=True)
    cent = full - mean
    spread = jnp.mean(jnp.square(cent), axis=-1, keepdims=True)
    return cent * lax.rsqrt(spread + 1e-06) * (1.0 + scale) + shift


def sigma_at(index):
    frac = 1.0 - index.astype(F32) / STEPS
    return 3.0 * frac / (1.0 + 2.0 * frac)


def first_kernel(
    pos_ref,
    x_ref,
    mod_ref,
    up_ref,
    down_ref,
    qkv_ref,
    wout_ref,
    h_ref,
    kv_ref,
    qo_ref,
    pack_ref,
    held,
    load_sem,
    store_sem,
    half_sem,
):
    core = pos_ref[0]
    zone = pos_ref[1]
    part = down_ref.shape[0]

    def move(core_here, sources):
        mine = pl.ds(core_here * 48, 48)
        halves = [
            pltpu.make_async_copy(qkv_ref.at[pl.ds(1, 2), mine, :], kv_ref, half_sem.at[0]),
            pltpu.make_async_copy(qkv_ref.at[0, mine, :], qo_ref.at[0], half_sem.at[1]),
            pltpu.make_async_copy(wout_ref.at[mine, :], qo_ref.at[1], half_sem.at[2]),
        ]
        loads = []
        stores = []
        for i, source in enumerate(sources):
            rows = pl.ds(i * part, part)
            loads.append(pltpu.make_async_copy(source, held.at[rows, :], load_sem.at[i]))
            stores.append(
                pltpu.make_async_copy(held.at[rows, :], pack_ref.at[rows, :], store_sem.at[i])
            )
        for copy in loads + halves:
            copy.start()
        h = layer_norm(x_ref[...].astype(F32), mod_ref[0:1, :], mod_ref[1:2, :]).astype(BF)
        for i in range(h_ref.shape[0]):
            h_ref[i] = h
        for load, store in zip(loads, stores):
            load.wait()
            store.start()
        for copy in halves + stores:
            copy.wait()

    for half in range(2):

        @pl.when(jnp.logical_and(core == 0, zone == half))
        def _():
            move(0, [up_ref.at[pl.ds((2 * half + i) * part, part), :] for i in range(2)])

        @pl.when(jnp.logical_and(core == 1, zone == half))
        def _():
            move(1, [down_ref.at[:, pl.ds((2 * half + i) * part, part)] for i in range(2)])


def first_stage(pos, tokens, mods, w_up, w_down, own_qkv, w_out, copies):
    rows, width = tokens.shape
    part = w_down.shape[0]
    return pl.pallas_call(
        first_kernel,
        out_shape=[
            jax.ShapeDtypeStruct((copies, rows, width), BF),
            jax.ShapeDtypeStruct((2, 48, width), BF),
            jax.ShapeDtypeStruct((2, 48, width), BF),
            jax.ShapeDtypeStruct((2 * part, part), BF),
        ],
        in_specs=[pl.BlockSpec(memory_space=pltpu.SMEM)]
        + [pl.BlockSpec(memory_space=pltpu.VMEM)] * 2
        + [pl.BlockSpec(memory_space=pltpu.HBM)] * 4,
        out_specs=[pl.BlockSpec(memory_space=pltpu.VMEM)] * 3
        + [pl.BlockSpec(memory_space=pltpu.HBM)],
        scratch_shapes=[
            pltpu.VMEM((2 * part, part), BF),
            pltpu.SemaphoreType.DMA((2,)),
            pltpu.SemaphoreType.DMA((2,)),
            pltpu.SemaphoreType.DMA((3,)),
        ],
        compiler_params=params(58),
        name="first_stage",
    )(pos, tokens, mods, w_up, w_down, own_qkv, w_out)


def assemble(pos_ref, own_ref, near_ref, far_ref, store):
    core = pos_ref[0]
    row = pos_ref[1]
    store(row, 0, own_ref, 0)
    store(row, 1, own_ref, 1)
    for i, step in enumerate(STRIDES):
        source = lax.rem(row + 4 - step, 4)
        store(source, core, near_ref, i)
        store(source, 1 - core, far_ref, i)


def project_kernel(first, pos_ref, h_ref, own_ref, near_ref, far_ref, out_ref, w_ref):
    count = out_ref.shape[1]

    def store(source, half, ref, index):
        for k in range(count):
            if ref is own_ref:
                value = ref[first + k, index * 48 : index * 48 + 48, :]
            else:
                value = ref[index, k]
            w_ref[k, source, half] = value

    assemble(pos_ref, own_ref, near_ref, far_ref, store)
    h = h_ref[...]
    for k in range(count):
        w = w_ref[k].reshape(384, h.shape[1])
        value = lax.dot_general(h, w, NT, preferred_element_type=F32).astype(BF)
        for i in range(out_ref.shape[0]):
            out_ref[i, k] = value


def project(pos, h, own, first, count, copies, near, far):
    rows, width = h.shape
    return pl.pallas_call(
        functools.partial(project_kernel, first),
        out_shape=jax.ShapeDtypeStruct((copies, count, rows, 384), BF),
        in_specs=[pl.BlockSpec(memory_space=pltpu.SMEM)]
        + [pl.BlockSpec(memory_space=pltpu.VMEM)] * 4,
        scratch_shapes=[pltpu.VMEM((count, 4, 2, 48, width), BF)],
        compiler_params=params(14),
        name="project",
    )(pos, h, own, near, far)


def attention_kernel(own, *refs):
    refs = list(refs)
    pos_ref, kv_ref = refs[:2]
    if own:
        q_ref, text_ref = refs[2:4]
        outs = refs[4:]
        outs[0][:, 512:] = q_ref[...].astype(F32)
    else:
        state_ref = refs[2]
        outs = refs[3:]
    rows = outs[0].shape[0]
    if own:
        live = lax.broadcasted_iota(jnp.int32, (rows, TXT), 1) < pos_ref[2]
    first = lax.broadcasted_iota(jnp.int32, (rows, 128), 1) < HEAD_DIM
    where = [0] if own else [lax.rem(pos_ref[1] + i, 4) for i in (1, 2, 3)]
    lane = lax.broadcasted_iota(jnp.int32, (rows, 128), 1)
    stats = jnp.zeros((rows, 128), F32)
    for g in range(3):
        cols = slice(g * 128, g * 128 + 128)
        if own:
            q = q_ref[:, cols]
        else:
            q = state_ref[:, 512 + g * 128 : 640 + g * 128].astype(BF)
        accs = []
        scales = []
        for side in range(2):
            head = 2 * g + side
            here = first if side == 0 else jnp.logical_not(first)
            qh = jnp.where(here, q, jnp.zeros_like(q))
            parts = []
            for i in where:
                s = (
                    lax.dot_general(qh, kv_ref[i, 0, :, cols], NT, preferred_element_type=F32)
                    * 0.125
                )
                parts.append((s, kv_ref[i, 1, :, cols]))
            if own:
                s = (
                    lax.dot_general(qh, text_ref[0, :, cols], NT, preferred_element_type=F32)
                    * 0.125
                )
                parts.append((jnp.where(live, s, -jnp.inf), text_ref[1, :, cols]))
            top = None
            for s, _ in parts:
                peak = jnp.max(s, axis=1, keepdims=True)
                top = peak if top is None else jnp.maximum(top, peak)
            if not own:
                old = state_ref[:, 384 + head : 385 + head]
                top = jnp.maximum(top, old)
            total = None
            acc = None
            for s, values in parts:
                p = jnp.exp(s - top)
                amount = jnp.sum(p, axis=1, keepdims=True)
                part = lax.dot_general(p.astype(BF), values, NN, preferred_element_type=F32)
                total = amount if total is None else total + amount
                acc = part if acc is None else acc + part
            if own:
                stats = jnp.where(lane == head, top, stats)
                stats = jnp.where(lane == HEAD_DIM + head, total, stats)
            else:
                factor = jnp.exp(old - top)
                total = total + state_ref[:, 448 + head : 449 + head] * factor
                scales.append((factor, total))
            accs.append(acc)
        acc = jnp.where(first, accs[0], accs[1])
        if own:
            outs[0][:, cols] = acc
        else:
            factor = jnp.where(first, scales[0][0], scales[1][0])
            total = jnp.where(first, scales[0][1], scales[1][1])
            outs[0][:, cols] = ((acc + state_ref[:, cols] * factor) / total).astype(BF)
    if own:
        outs[0][:, 384:512] = stats


def attention(pos, kv, query=None, text=None, state=None):
    own = state is None
    args = [kv, query, text] if own else [kv, state]
    rows = kv.shape[2]
    if own:
        out = jax.ShapeDtypeStruct((rows, 896), F32)
    else:
        out = jax.ShapeDtypeStruct((rows, 384), BF)
    return pl.pallas_call(
        functools.partial(attention_kernel, own),
        out_shape=out,
        in_specs=[pl.BlockSpec(memory_space=pltpu.SMEM)]
        + [pl.BlockSpec(memory_space=pltpu.VMEM)] * len(args),
        compiler_params=params(16),
        name="attention",
    )(pos, *args)


def out_kernel(pos_ref, a_ref, own_ref, near_ref, far_ref, out_ref, w_ref):
    def store(source, half, ref, index):
        if ref is own_ref:
            value = ref[index * 48 : index * 48 + 48, :]
        else:
            value = ref[index, 1]
        w_ref[source, half] = value

    assemble(pos_ref, own_ref, near_ref, far_ref, store)
    w = w_ref[...].reshape(384, out_ref.shape[1])
    out_ref[...] = lax.dot_general(
        a_ref[...], w, NN, preferred_element_type=F32
    ).astype(BF)


def out_projection(pos, a, own, near, far):
    width = own.shape[1]
    return pl.pallas_call(
        out_kernel,
        out_shape=jax.ShapeDtypeStruct((a.shape[0], width), BF),
        in_specs=[pl.BlockSpec(memory_space=pltpu.SMEM)]
        + [pl.BlockSpec(memory_space=pltpu.VMEM)] * 4,
        scratch_shapes=[pltpu.VMEM((4, 2, 48, width), BF)],
        compiler_params=params(8),
        name="out_projection",
    )(pos, a, own, near, far)


def second_norm_kernel(x_ref, part_ref, mod_ref, second_ref, out_ref):
    proj = part_ref[0].astype(F32)
    for i in range(1, part_ref.shape[0]):
        proj += part_ref[i].astype(F32)
    second = (x_ref[...].astype(F32) + mod_ref[2:3, :] * proj).astype(BF)
    second_ref[...] = second
    h = layer_norm(second.astype(F32), mod_ref[3:4, :], mod_ref[4:5, :]).astype(BF)
    for i in range(out_ref.shape[0]):
        out_ref[i] = h


def second_norm(tokens, parts, mods):
    return pl.pallas_call(
        second_norm_kernel,
        out_shape=[
            jax.ShapeDtypeStruct(tokens.shape, BF),
            jax.ShapeDtypeStruct(parts.shape, BF),
        ],
        compiler_params=params(6),
        name="second_norm",
    )(tokens, parts, mods)


def ffn_kernel(h_ref, up_ref, down_ref, out_ref, hidden_ref):
    step = pl.program_id(0)
    part = up_ref.shape[-1]

    @pl.when(step < 2)
    def _():
        up = jnp.concatenate([up_ref[0, 0], up_ref[0, 1]], axis=1)
        hidden_ref[lax.rem(step, 2)] = jax.nn.gelu(
            lax.dot_general(h_ref[...], up, NN, preferred_element_type=F32),
            approximate=True,
        ).astype(BF)

    @pl.when(step >= 2)
    def _():
        hidden = jnp.concatenate([hidden_ref[0], hidden_ref[1]], axis=1)
        down = jnp.concatenate(
            [
                jnp.concatenate([down_ref[0, y, :part], down_ref[0, y, part:]], axis=1)
                for y in range(4)
            ],
            axis=0,
        )
        out_ref[...] = lax.dot_general(
            hidden, down, NN, preferred_element_type=F32
        ).astype(BF)


def feed_forward(h, weights):
    rows, width = h.shape
    part = weights.shape[3]
    return pl.pallas_call(
        ffn_kernel,
        grid=(4,),
        out_shape=jax.ShapeDtypeStruct((rows, width), BF),
        in_specs=[
            pl.BlockSpec((rows, width), lambda i: (0, 0)),
            pl.BlockSpec((1, 2, width, part), lambda i: (0, jnp.minimum(i, 1), 0, 0)),
            pl.BlockSpec((1, 4, 2 * part, part), lambda i: (1, 0, jnp.maximum(i - 2, 0), 0)),
        ],
        out_specs=pl.BlockSpec((rows, 2 * part), lambda i: (0, jnp.maximum(i - 2, 0))),
        scratch_shapes=[pltpu.VMEM((2, rows, 2 * part), BF)],
        compiler_params=params(58),
        name="feed_forward",
    )(h, weights, weights)


def last_kernel(second_ref, part_ref, mod_ref, w_ref, state_ref, vel_ref):
    ffn = part_ref[0].astype(F32)
    for i in range(1, part_ref.shape[0]):
        ffn += part_ref[i].astype(F32)
    state = (second_ref[...].astype(F32) + mod_ref[5:6, :] * ffn).astype(BF)
    state_ref[...] = state
    h = layer_norm(state.astype(F32), mod_ref[6:7, :], mod_ref[7:8, :]).astype(BF)
    vel_ref[...] = lax.dot_general(h, w_ref[...], NN, preferred_element_type=F32)


def last_stage(second, parts, mods, w_final):
    return pl.pallas_call(
        last_kernel,
        out_shape=[
            jax.ShapeDtypeStruct(second.shape, BF),
            jax.ShapeDtypeStruct((second.shape[0], w_final.shape[1]), F32),
        ],
        compiler_params=params(6),
        name="last_stage",
    )(second, parts, mods, w_final)


def on_device(
    image_tokens,
    latent,
    modulation,
    text_kv,
    text_len,
    timestep,
    w_qkv,
    w_out,
    w_up,
    w_down,
    w_final,
):
    tokens = image_tokens[0]
    mods = modulation[0]
    rows, width = tokens.shape
    core = lax.axis_index("core")
    pos = jnp.concatenate([jnp.stack([core, lax.axis_index("ty")]).astype(jnp.int32), text_len])
    swap2 = [(0, 1), (1, 0)]

    def to_lines(value, step):
        return lax.ppermute(value, "ty", [(i, (i + step) % 4) for i in range(4)])

    own_qkv = jnp.transpose(w_qkv, (1, 2, 0))
    place = jnp.stack([core, lax.axis_index("zp")]).astype(jnp.int32)
    h1, half_kv, half_qo, quarter = first_stage(
        place, tokens, mods, w_up, w_down, own_qkv, w_out, 4
    )
    ffn_full = lax.all_gather(quarter, ("core", "tx", "zp"), axis=0, tiled=False)
    ffn_full = ffn_full.reshape(2, 4, width, w_up.shape[1])
    h1 = lax.all_to_all(h1, "tx", split_axis=0, concat_axis=0, tiled=True)
    near_kv = [to_lines(half_kv, step) for step in STRIDES]
    *near_kv, h1 = lax.optimization_barrier((*near_kv, h1))
    stacked, half_qo = lax.optimization_barrier((jnp.stack(near_kv), half_qo))
    far_kv = lax.ppermute(stacked, "core", swap2)
    near_qo = [to_lines(half_qo, step) for step in STRIDES]
    h1 = h1.reshape(4 * rows, width)
    own_kv = project(pos, h1, own_qkv, 1, 2, 4, stacked, far_kv)
    all_kv = lax.all_to_all(own_kv, "ty", split_axis=0, concat_axis=0, tiled=True)
    *near_qo, own_kv, text_kv = lax.optimization_barrier((*near_qo, own_kv, text_kv))
    text = lax.dynamic_slice_in_dim(text_kv[0], lax.axis_index("tx") * 384, 384, 2)
    text = jnp.transpose(text, (1, 0, 2))
    near_qo = jnp.stack(near_qo)
    far_qo = lax.ppermute(near_qo, "core", swap2)
    query = project(pos, h1, own_qkv, 0, 1, 1, near_qo, far_qo)[0, 0]

    state = attention(pos, own_kv, query=query, text=text)
    attended = attention(pos, all_kv, state=state)

    partial = out_projection(pos, attended, w_out, near_qo, far_qo)
    partial = partial.reshape(4, rows, width)
    partial = lax.all_to_all(partial, "tx", split_axis=0, concat_axis=0, tiled=True)
    second, h2 = second_norm(tokens, partial, mods)
    h2 = lax.all_to_all(h2, "ty", split_axis=0, concat_axis=0, tiled=True)
    partial = feed_forward(h2.reshape(4 * rows, width), ffn_full).reshape(4, rows, width)
    partial = lax.all_to_all(partial, "ty", split_axis=0, concat_axis=0, tiled=True)
    state, velocity = last_stage(second, partial, mods, w_final)

    step_index = timestep[0]
    delta = sigma_at(step_index + 1) - sigma_at(step_index)
    moved = latent[0] + delta * velocity.reshape(rows // 2, 2 * velocity.shape[1])
    return (state[None], moved[None])


def solution(mesh):
    fine = Mesh(
        mesh.devices.reshape(mesh.shape["req"] // 4, 2, 2, 4, 4, mesh.shape["blk"]),
        ("zl", "zp", "core", "tx", "ty", "blk"),
    )
    group = ("zl", "zp", "core", "blk")
    tile = ("tx", "ty")
    in_specs = (
        P(group, tile, None),
        P(group, tile, None),
        P(group, None, None),
        P(group, None, None, None),
        P(group),
        P(group),
        P(None, None, tile),
        P(tile, None),
        P(None, tile),
        P(tile, None),
        P(),
    )
    out_specs = (P(group, tile, None), P(group, tile, None))
    return jax.shard_map(
        on_device, mesh=fine, in_specs=in_specs, out_specs=out_specs, check_vma=False
    )
```

```python
import functools

import jax
import jax.numpy as jnp
from jax import lax
from jax.experimental import pallas as pl
from jax.experimental.pallas import tpu as pltpu
from jax.sharding import Mesh, PartitionSpec as P

HEAD_DIM = 64
TXT = 154
STEPS = 8
BF = jnp.bfloat16
F32 = jnp.float32
NT = (((1,), (1,)), ((), ()))
NN = (((1,), (0,)), ((), ()))
STRIDES = (1, 3, 2)


def params(mebibytes):
    return pltpu.CompilerParams(vmem_limit_bytes=mebibytes * 1024 * 1024)


def layer_norm(full, shift, scale):
    mean = jnp.mean(full, axis=-1, keepdims=True)
    cent = full - mean
    spread = jnp.mean(jnp.square(cent), axis=-1, keepdims=True)
    return cent * lax.rsqrt(spread + 1e-06) * (1.0 + scale) + shift


def sigma_at(index):
    frac = 1.0 - index.astype(F32) / STEPS
    return 3.0 * frac / (1.0 + 2.0 * frac)


def first_kernel(
    copies, pos_ref, x_ref, mod_ref, up_ref, down_ref, out_ref, pack_ref, held, load_sem, store_sem
):
    core = pos_ref[0]
    zone = pos_ref[1]
    part = down_ref.shape[0]

    def move(sources):
        loads = []
        stores = []
        for i, source in enumerate(sources):
            rows = pl.ds(i * part, part)
            loads.append(pltpu.make_async_copy(source, held.at[rows, :], load_sem.at[i]))
            stores.append(
                pltpu.make_async_copy(held.at[rows, :], pack_ref.at[rows, :], store_sem.at[i])
            )
        for load in loads:
            load.start()
        h = layer_norm(x_ref[...].astype(F32), mod_ref[0:1, :], mod_ref[1:2, :]).astype(BF)
        for i in range(copies):
            out_ref[i] = h
        for load, store in zip(loads, stores):
            load.wait()
            store.start()
        for store in stores:
            store.wait()

    for half in range(2):

        @pl.when(jnp.logical_and(core == 0, zone == half))
        def _():
            move([up_ref.at[pl.ds((2 * half + i) * part, part), :] for i in range(2)])

        @pl.when(jnp.logical_and(core == 1, zone == half))
        def _():
            move([down_ref.at[:, pl.ds((2 * half + i) * part, part)] for i in range(2)])


def first_norm_and_pack(pos, tokens, mods, w_up, w_down, copies):
    rows, width = tokens.shape
    part = w_down.shape[0]
    return pl.pallas_call(
        functools.partial(first_kernel, copies),
        out_shape=[
            jax.ShapeDtypeStruct((copies, rows, width), BF),
            jax.ShapeDtypeStruct((2 * part, part), BF),
        ],
        in_specs=[pl.BlockSpec(memory_space=pltpu.SMEM)]
        + [pl.BlockSpec(memory_space=pltpu.VMEM)] * 2
        + [pl.BlockSpec(memory_space=pltpu.HBM)] * 2,
        out_specs=[
            pl.BlockSpec(memory_space=pltpu.VMEM),
            pl.BlockSpec(memory_space=pltpu.HBM),
        ],
        scratch_shapes=[
            pltpu.VMEM((2 * part, part), BF),
            pltpu.SemaphoreType.DMA((2,)),
            pltpu.SemaphoreType.DMA((2,)),
        ],
        compiler_params=params(58),
        name="first_norm_and_pack",
    )(pos, tokens, mods, w_up, w_down)


def assemble(pos_ref, own_ref, near_ref, far_ref, store):
    core = pos_ref[0]
    row = pos_ref[1]
    store(row, 0, own_ref, 0)
    store(row, 1, own_ref, 1)
    for i, step in enumerate(STRIDES):
        source = lax.rem(row + 4 - step, 4)
        store(source, core, near_ref, i)
        store(source, 1 - core, far_ref, i)


def project_kernel(first, pos_ref, h_ref, own_ref, near_ref, far_ref, out_ref, w_ref):
    count = out_ref.shape[1]

    def store(source, half, ref, index):
        for k in range(count):
            if ref is own_ref:
                value = ref[first + k, index * 48 : index * 48 + 48, :]
            else:
                value = ref[index, k]
            w_ref[k, source, half] = value

    assemble(pos_ref, own_ref, near_ref, far_ref, store)
    h = h_ref[...]
    for k in range(count):
        w = w_ref[k].reshape(384, h.shape[1])
        value = lax.dot_general(h, w, NT, preferred_element_type=F32).astype(BF)
        for i in range(out_ref.shape[0]):
            out_ref[i, k] = value


def project(pos, h, own, first, count, copies, near, far):
    rows, width = h.shape
    return pl.pallas_call(
        functools.partial(project_kernel, first),
        out_shape=jax.ShapeDtypeStruct((copies, count, rows, 384), BF),
        in_specs=[pl.BlockSpec(memory_space=pltpu.SMEM)]
        + [pl.BlockSpec(memory_space=pltpu.VMEM)] * 4,
        scratch_shapes=[pltpu.VMEM((count, 4, 2, 48, width), BF)],
        compiler_params=params(14),
        name="project",
    )(pos, h, own, near, far)


def attention_kernel(own, *refs):
    refs = list(refs)
    pos_ref, kv_ref = refs[:2]
    if own:
        q_ref, text_ref = refs[2:4]
        outs = refs[4:]
        outs[0][:, 512:] = q_ref[...].astype(F32)
    else:
        state_ref = refs[2]
        outs = refs[3:]
    rows = outs[0].shape[0]
    if own:
        live = lax.broadcasted_iota(jnp.int32, (rows, TXT), 1) < pos_ref[2]
    first = lax.broadcasted_iota(jnp.int32, (rows, 128), 1) < HEAD_DIM
    where = [0] if own else [lax.rem(pos_ref[1] + i, 4) for i in (1, 2, 3)]
    lane = lax.broadcasted_iota(jnp.int32, (rows, 128), 1)
    stats = jnp.zeros((rows, 128), F32)
    for g in range(3):
        cols = slice(g * 128, g * 128 + 128)
        if own:
            q = q_ref[:, cols]
        else:
            q = state_ref[:, 512 + g * 128 : 640 + g * 128].astype(BF)
        accs = []
        scales = []
        for side in range(2):
            head = 2 * g + side
            here = first if side == 0 else jnp.logical_not(first)
            qh = jnp.where(here, q, jnp.zeros_like(q))
            parts = []
            for i in where:
                s = (
                    lax.dot_general(qh, kv_ref[i, 0, :, cols], NT, preferred_element_type=F32)
                    * 0.125
                )
                parts.append((s, kv_ref[i, 1, :, cols]))
            if own:
                s = (
                    lax.dot_general(qh, text_ref[0, :, cols], NT, preferred_element_type=F32)
                    * 0.125
                )
                parts.append((jnp.where(live, s, -jnp.inf), text_ref[1, :, cols]))
            top = None
            for s, _ in parts:
                peak = jnp.max(s, axis=1, keepdims=True)
                top = peak if top is None else jnp.maximum(top, peak)
            if not own:
                old = state_ref[:, 384 + head : 385 + head]
                top = jnp.maximum(top, old)
            total = None
            acc = None
            for s, values in parts:
                p = jnp.exp(s - top)
                amount = jnp.sum(p, axis=1, keepdims=True)
                part = lax.dot_general(p.astype(BF), values, NN, preferred_element_type=F32)
                total = amount if total is None else total + amount
                acc = part if acc is None else acc + part
            if own:
                stats = jnp.where(lane == head, top, stats)
                stats = jnp.where(lane == HEAD_DIM + head, total, stats)
            else:
                factor = jnp.exp(old - top)
                total = total + state_ref[:, 448 + head : 449 + head] * factor
                scales.append((factor, total))
            accs.append(acc)
        acc = jnp.where(first, accs[0], accs[1])
        if own:
            outs[0][:, cols] = acc
        else:
            factor = jnp.where(first, scales[0][0], scales[1][0])
            total = jnp.where(first, scales[0][1], scales[1][1])
            outs[0][:, cols] = ((acc + state_ref[:, cols] * factor) / total).astype(BF)
    if own:
        outs[0][:, 384:512] = stats


def attention(pos, kv, query=None, text=None, state=None):
    own = state is None
    args = [kv, query, text] if own else [kv, state]
    rows = kv.shape[2]
    if own:
        out = jax.ShapeDtypeStruct((rows, 896), F32)
    else:
        out = jax.ShapeDtypeStruct((rows, 384), BF)
    return pl.pallas_call(
        functools.partial(attention_kernel, own),
        out_shape=out,
        in_specs=[pl.BlockSpec(memory_space=pltpu.SMEM)]
        + [pl.BlockSpec(memory_space=pltpu.VMEM)] * len(args),
        compiler_params=params(16),
        name="attention",
    )(pos, *args)


def out_kernel(pos_ref, a_ref, own_ref, near_ref, far_ref, out_ref, w_ref):
    def store(source, half, ref, index):
        if ref is own_ref:
            value = ref[index * 48 : index * 48 + 48, :]
        else:
            value = ref[index, 1]
        w_ref[source, half] = value

    assemble(pos_ref, own_ref, near_ref, far_ref, store)
    w = w_ref[...].reshape(384, out_ref.shape[1])
    out_ref[...] = lax.dot_general(
        a_ref[...], w, NN, preferred_element_type=F32
    ).astype(BF)


def out_projection(pos, a, own, near, far):
    width = own.shape[1]
    return pl.pallas_call(
        out_kernel,
        out_shape=jax.ShapeDtypeStruct((a.shape[0], width), BF),
        in_specs=[pl.BlockSpec(memory_space=pltpu.SMEM)]
        + [pl.BlockSpec(memory_space=pltpu.VMEM)] * 4,
        scratch_shapes=[pltpu.VMEM((4, 2, 48, width), BF)],
        compiler_params=params(8),
        name="out_projection",
    )(pos, a, own, near, far)


def second_norm_kernel(x_ref, part_ref, mod_ref, second_ref, out_ref):
    proj = part_ref[0].astype(F32)
    for i in range(1, part_ref.shape[0]):
        proj += part_ref[i].astype(F32)
    second = (x_ref[...].astype(F32) + mod_ref[2:3, :] * proj).astype(BF)
    second_ref[...] = second
    h = layer_norm(second.astype(F32), mod_ref[3:4, :], mod_ref[4:5, :]).astype(BF)
    for i in range(out_ref.shape[0]):
        out_ref[i] = h


def second_norm(tokens, parts, mods):
    return pl.pallas_call(
        second_norm_kernel,
        out_shape=[
            jax.ShapeDtypeStruct(tokens.shape, BF),
            jax.ShapeDtypeStruct(parts.shape, BF),
        ],
        compiler_params=params(6),
        name="second_norm",
    )(tokens, parts, mods)


def ffn_kernel(h_ref, up_ref, down_ref, out_ref, hidden_ref):
    step = pl.program_id(0)
    part = up_ref.shape[-1]

    @pl.when(step < 2)
    def _():
        up = jnp.concatenate([up_ref[0, 0], up_ref[0, 1]], axis=1)
        hidden_ref[lax.rem(step, 2)] = jax.nn.gelu(
            lax.dot_general(h_ref[...], up, NN, preferred_element_type=F32),
            approximate=True,
        ).astype(BF)

    @pl.when(step >= 2)
    def _():
        hidden = jnp.concatenate([hidden_ref[0], hidden_ref[1]], axis=1)
        down = jnp.concatenate(
            [
                jnp.concatenate([down_ref[0, y, :part], down_ref[0, y, part:]], axis=1)
                for y in range(4)
            ],
            axis=0,
        )
        out_ref[...] = lax.dot_general(
            hidden, down, NN, preferred_element_type=F32
        ).astype(BF)


def feed_forward(h, weights):
    rows, width = h.shape
    part = weights.shape[3]
    return pl.pallas_call(
        ffn_kernel,
        grid=(4,),
        out_shape=jax.ShapeDtypeStruct((rows, width), BF),
        in_specs=[
            pl.BlockSpec((rows, width), lambda i: (0, 0)),
            pl.BlockSpec((1, 2, width, part), lambda i: (0, jnp.minimum(i, 1), 0, 0)),
            pl.BlockSpec((1, 4, 2 * part, part), lambda i: (1, 0, jnp.maximum(i - 2, 0), 0)),
        ],
        out_specs=pl.BlockSpec((rows, 2 * part), lambda i: (0, jnp.maximum(i - 2, 0))),
        scratch_shapes=[pltpu.VMEM((2, rows, 2 * part), BF)],
        compiler_params=params(58),
        name="feed_forward",
    )(h, weights, weights)


def last_kernel(second_ref, part_ref, mod_ref, w_ref, state_ref, vel_ref):
    ffn = part_ref[0].astype(F32)
    for i in range(1, part_ref.shape[0]):
        ffn += part_ref[i].astype(F32)
    state = (second_ref[...].astype(F32) + mod_ref[5:6, :] * ffn).astype(BF)
    state_ref[...] = state
    h = layer_norm(state.astype(F32), mod_ref[6:7, :], mod_ref[7:8, :]).astype(BF)
    vel_ref[...] = lax.dot_general(h, w_ref[...], NN, preferred_element_type=F32)


def last_stage(second, parts, mods, w_final):
    return pl.pallas_call(
        last_kernel,
        out_shape=[
            jax.ShapeDtypeStruct(second.shape, BF),
            jax.ShapeDtypeStruct((second.shape[0], w_final.shape[1]), F32),
        ],
        compiler_params=params(6),
        name="last_stage",
    )(second, parts, mods, w_final)


def on_device(
    image_tokens,
    latent,
    modulation,
    text_kv,
    text_len,
    timestep,
    w_qkv,
    w_out,
    w_up,
    w_down,
    w_final,
):
    tokens = image_tokens[0]
    mods = modulation[0]
    rows, width = tokens.shape
    core = lax.axis_index("core")
    pos = jnp.concatenate([jnp.stack([core, lax.axis_index("ty")]).astype(jnp.int32), text_len])
    swap2 = [(0, 1), (1, 0)]

    def to_lines(value, step):
        return lax.ppermute(value, "ty", [(i, (i + step) % 4) for i in range(4)])

    own_qkv = jnp.transpose(w_qkv, (1, 2, 0))
    half_kv = lax.dynamic_slice(own_qkv, (1, core * 48, 0), (2, 48, width))
    near_kv = [to_lines(half_kv, step) for step in STRIDES]
    place = jnp.stack([core, lax.axis_index("zp")]).astype(jnp.int32)
    h1, quarter = first_norm_and_pack(place, tokens, mods, w_up, w_down, 4)
    ffn_full = lax.all_gather(quarter, ("core", "tx", "zp"), axis=0, tiled=False)
    ffn_full = ffn_full.reshape(2, 4, width, w_up.shape[1])
    h1 = lax.all_to_all(h1, "tx", split_axis=0, concat_axis=0, tiled=True)

    half_q = lax.dynamic_slice(own_qkv, (0, core * 48, 0), (1, 48, width))
    half_out = lax.dynamic_slice(w_out, (core * 48, 0), (48, width))
    half_qo = jnp.concatenate([half_q, half_out[None]])
    near_qo = [to_lines(half_qo, step) for step in STRIDES[:2]]
    *near, h1, half_qo = lax.optimization_barrier((*near_kv, *near_qo, h1, half_qo))
    stacked, half_qo = lax.optimization_barrier((jnp.stack(near[:3]), half_qo))
    far_kv = lax.ppermute(stacked, "core", swap2)
    near_qo = [*near[3:], to_lines(half_qo, STRIDES[2])]
    h1 = h1.reshape(4 * rows, width)
    own_kv = project(pos, h1, own_qkv, 1, 2, 4, stacked, far_kv)
    all_kv = lax.all_to_all(own_kv, "ty", split_axis=0, concat_axis=0, tiled=True)
    *near_qo, own_kv, text_kv = lax.optimization_barrier((*near_qo, own_kv, text_kv))
    text = lax.dynamic_slice_in_dim(text_kv[0], lax.axis_index("tx") * 384, 384, 2)
    text = jnp.transpose(text, (1, 0, 2))
    near_qo = jnp.stack(near_qo)
    far_qo = lax.ppermute(near_qo, "core", swap2)
    query = project(pos, h1, own_qkv, 0, 1, 1, near_qo, far_qo)[0, 0]

    state = attention(pos, own_kv, query=query, text=text)
    attended = attention(pos, all_kv, state=state)

    partial = out_projection(pos, attended, w_out, near_qo, far_qo)
    partial = partial.reshape(4, rows, width)
    partial = lax.all_to_all(partial, "tx", split_axis=0, concat_axis=0, tiled=True)
    second, h2 = second_norm(tokens, partial, mods)
    h2 = lax.all_to_all(h2, "ty", split_axis=0, concat_axis=0, tiled=True)
    partial = feed_forward(h2.reshape(4 * rows, width), ffn_full).reshape(4, rows, width)
    partial = lax.all_to_all(partial, "ty", split_axis=0, concat_axis=0, tiled=True)
    state, velocity = last_stage(second, partial, mods, w_final)

    step_index = timestep[0]
    delta = sigma_at(step_index + 1) - sigma_at(step_index)
    moved = latent[0] + delta * velocity.reshape(rows // 2, 2 * velocity.shape[1])
    return (state[None], moved[None])


def solution(mesh):
    fine = Mesh(
        mesh.devices.reshape(mesh.shape["req"] // 4, 2, 2, 4, 4, mesh.shape["blk"]),
        ("zl", "zp", "core", "tx", "ty", "blk"),
    )
    group = ("zl", "zp", "core", "blk")
    tile = ("tx", "ty")
    in_specs = (
        P(group, tile, None),
        P(group, tile, None),
        P(group, None, None),
        P(group, None, None, None),
        P(group),
        P(group),
        P(None, None, tile),
        P(tile, None),
        P(None, tile),
        P(tile, None),
        P(),
    )
    out_specs = (P(group, tile, None), P(group, tile, None))
    return jax.shard_map(
        on_device, mesh=fine, in_specs=in_specs, out_specs=out_specs, check_vma=False
    )
```

```python
import functools

import jax
import jax.numpy as jnp
from jax import lax
from jax.experimental import pallas as pl
from jax.experimental.pallas import tpu as pltpu
from jax.sharding import Mesh, PartitionSpec as P

HEAD_DIM = 64
TXT = 154
STEPS = 8
BF = jnp.bfloat16
F32 = jnp.float32
NT = (((1,), (1,)), ((), ()))
NN = (((1,), (0,)), ((), ()))
STRIDES = (1, 3, 2)


def params(mebibytes):
    return pltpu.CompilerParams(vmem_limit_bytes=mebibytes * 1024 * 1024)


def layer_norm(full, shift, scale):
    mean = jnp.mean(full, axis=-1, keepdims=True)
    cent = full - mean
    spread = jnp.mean(jnp.square(cent), axis=-1, keepdims=True)
    return cent * lax.rsqrt(spread + 1e-06) * (1.0 + scale) + shift


def sigma_at(index):
    frac = 1.0 - index.astype(F32) / STEPS
    return 3.0 * frac / (1.0 + 2.0 * frac)


def first_kernel(
    copies, pos_ref, x_ref, mod_ref, up_ref, down_ref, out_ref, pack_ref, held, load_sem, store_sem
):
    core = pos_ref[0]
    zone = pos_ref[1]
    part = down_ref.shape[0]

    def move(sources):
        loads = []
        stores = []
        for i, source in enumerate(sources):
            rows = pl.ds(i * part, part)
            loads.append(pltpu.make_async_copy(source, held.at[rows, :], load_sem.at[i]))
            stores.append(
                pltpu.make_async_copy(held.at[rows, :], pack_ref.at[rows, :], store_sem.at[i])
            )
        for load in loads:
            load.start()
        h = layer_norm(x_ref[...].astype(F32), mod_ref[0:1, :], mod_ref[1:2, :]).astype(BF)
        for i in range(copies):
            out_ref[i] = h
        for load, store in zip(loads, stores):
            load.wait()
            store.start()
        for store in stores:
            store.wait()

    for half in range(2):

        @pl.when(jnp.logical_and(core == 0, zone == half))
        def _():
            move([up_ref.at[pl.ds((2 * half + i) * part, part), :] for i in range(2)])

        @pl.when(jnp.logical_and(core == 1, zone == half))
        def _():
            move([down_ref.at[:, pl.ds((2 * half + i) * part, part)] for i in range(2)])


def first_norm_and_pack(pos, tokens, mods, w_up, w_down, copies):
    rows, width = tokens.shape
    part = w_down.shape[0]
    return pl.pallas_call(
        functools.partial(first_kernel, copies),
        out_shape=[
            jax.ShapeDtypeStruct((copies, rows, width), BF),
            jax.ShapeDtypeStruct((2 * part, part), BF),
        ],
        in_specs=[pl.BlockSpec(memory_space=pltpu.SMEM)]
        + [pl.BlockSpec(memory_space=pltpu.VMEM)] * 2
        + [pl.BlockSpec(memory_space=pltpu.HBM)] * 2,
        out_specs=[
            pl.BlockSpec(memory_space=pltpu.VMEM),
            pl.BlockSpec(memory_space=pltpu.HBM),
        ],
        scratch_shapes=[
            pltpu.VMEM((2 * part, part), BF),
            pltpu.SemaphoreType.DMA((2,)),
            pltpu.SemaphoreType.DMA((2,)),
        ],
        compiler_params=params(58),
        name="first_norm_and_pack",
    )(pos, tokens, mods, w_up, w_down)


def assemble(pos_ref, own_ref, near_refs, far_ref, store):
    core = pos_ref[0]
    row = pos_ref[1]
    store(row, 0, own_ref, 0)
    store(row, 1, own_ref, 1)
    for i, (near_ref, step) in enumerate(zip(near_refs, STRIDES)):
        source = lax.rem(row + 4 - step, 4)
        store(source, core, near_ref, None)
        store(source, 1 - core, far_ref, i)


def project_kernel(first, pos_ref, h_ref, own_ref, n0_ref, n1_ref, n2_ref, far_ref, out_ref, w_ref):
    count = out_ref.shape[1]

    def store(source, half, ref, index):
        for k in range(count):
            if ref is own_ref:
                value = ref[first + k, index * 48 : index * 48 + 48, :]
            elif index is None:
                value = ref[k]
            else:
                value = ref[index, k]
            w_ref[k, source, half] = value

    assemble(pos_ref, own_ref, (n0_ref, n1_ref, n2_ref), far_ref, store)
    h = h_ref[...]
    for k in range(count):
        w = w_ref[k].reshape(384, h.shape[1])
        value = lax.dot_general(h, w, NT, preferred_element_type=F32).astype(BF)
        for i in range(out_ref.shape[0]):
            out_ref[i, k] = value


def project(pos, h, own, first, count, copies, near, far):
    rows, width = h.shape
    return pl.pallas_call(
        functools.partial(project_kernel, first),
        out_shape=jax.ShapeDtypeStruct((copies, count, rows, 384), BF),
        in_specs=[pl.BlockSpec(memory_space=pltpu.SMEM)]
        + [pl.BlockSpec(memory_space=pltpu.VMEM)] * 6,
        scratch_shapes=[pltpu.VMEM((count, 4, 2, 48, width), BF)],
        compiler_params=params(14),
        name="project",
    )(pos, h, own, *near, far)


def attention_kernel(own, *refs):
    refs = list(refs)
    pos_ref, q_ref, kv_ref = refs[:3]
    if own:
        text_ref = refs[3]
        outs = refs[4:]
    else:
        state_ref = refs[3]
        outs = refs[4:]
    rows = q_ref.shape[0]
    if own:
        live = lax.broadcasted_iota(jnp.int32, (rows, TXT), 1) < pos_ref[2]
    first = lax.broadcasted_iota(jnp.int32, (rows, 128), 1) < HEAD_DIM
    where = [0] if own else [lax.rem(pos_ref[1] + i, 4) for i in (1, 2, 3)]
    lane = lax.broadcasted_iota(jnp.int32, (rows, 128), 1)
    stats = jnp.zeros((rows, 128), F32)
    for g in range(q_ref.shape[1] // 128):
        cols = slice(g * 128, g * 128 + 128)
        q = q_ref[:, cols]
        accs = []
        scales = []
        for side in range(2):
            head = 2 * g + side
            here = first if side == 0 else jnp.logical_not(first)
            qh = jnp.where(here, q, jnp.zeros_like(q))
            parts = []
            for i in where:
                s = (
                    lax.dot_general(qh, kv_ref[i, 0, :, cols], NT, preferred_element_type=F32)
                    * 0.125
                )
                parts.append((s, kv_ref[i, 1, :, cols]))
            if own:
                s = (
                    lax.dot_general(qh, text_ref[0, :, cols], NT, preferred_element_type=F32)
                    * 0.125
                )
                parts.append((jnp.where(live, s, -jnp.inf), text_ref[1, :, cols]))
            top = None
            for s, _ in parts:
                peak = jnp.max(s, axis=1, keepdims=True)
                top = peak if top is None else jnp.maximum(top, peak)
            if not own:
                old = state_ref[:, 384 + head : 385 + head]
                top = jnp.maximum(top, old)
            total = None
            acc = None
            for s, values in parts:
                p = jnp.exp(s - top)
                amount = jnp.sum(p, axis=1, keepdims=True)
                part = lax.dot_general(p.astype(BF), values, NN, preferred_element_type=F32)
                total = amount if total is None else total + amount
                acc = part if acc is None else acc + part
            if own:
                stats = jnp.where(lane == head, top, stats)
                stats = jnp.where(lane == HEAD_DIM + head, total, stats)
            else:
                factor = jnp.exp(old - top)
                total = total + state_ref[:, 448 + head : 449 + head] * factor
                scales.append((factor, total))
            accs.append(acc)
        acc = jnp.where(first, accs[0], accs[1])
        if own:
            outs[0][:, cols] = acc
        else:
            factor = jnp.where(first, scales[0][0], scales[1][0])
            total = jnp.where(first, scales[0][1], scales[1][1])
            outs[0][:, cols] = ((acc + state_ref[:, cols] * factor) / total).astype(BF)
    if own:
        outs[0][:, 384:] = stats


def attention(pos, q, kv, text=None, state=None):
    own = text is not None
    args = [q, kv, text if own else state]
    if own:
        out = jax.ShapeDtypeStruct((q.shape[0], 512), F32)
    else:
        out = jax.ShapeDtypeStruct(q.shape, BF)
    return pl.pallas_call(
        functools.partial(attention_kernel, own),
        out_shape=out,
        in_specs=[pl.BlockSpec(memory_space=pltpu.SMEM)]
        + [pl.BlockSpec(memory_space=pltpu.VMEM)] * len(args),
        compiler_params=params(16),
        name="attention",
    )(pos, *args)


def out_kernel(pos_ref, a_ref, own_ref, n0_ref, n1_ref, n2_ref, far_ref, out_ref, w_ref):
    def store(source, half, ref, index):
        if ref is own_ref:
            value = ref[index * 48 : index * 48 + 48, :]
        elif index is None:
            value = ref[1]
        else:
            value = ref[index, 1]
        w_ref[source, half] = value

    assemble(pos_ref, own_ref, (n0_ref, n1_ref, n2_ref), far_ref, store)
    w = w_ref[...].reshape(384, out_ref.shape[1])
    out_ref[...] = lax.dot_general(
        a_ref[...], w, NN, preferred_element_type=F32
    ).astype(BF)


def out_projection(pos, a, own, near, far):
    width = own.shape[1]
    return pl.pallas_call(
        out_kernel,
        out_shape=jax.ShapeDtypeStruct((a.shape[0], width), BF),
        in_specs=[pl.BlockSpec(memory_space=pltpu.SMEM)]
        + [pl.BlockSpec(memory_space=pltpu.VMEM)] * 6,
        scratch_shapes=[pltpu.VMEM((4, 2, 48, width), BF)],
        compiler_params=params(8),
        name="out_projection",
    )(pos, a, own, *near, far)


def second_norm_kernel(x_ref, part_ref, mod_ref, second_ref, out_ref):
    proj = part_ref[0].astype(F32)
    for i in range(1, part_ref.shape[0]):
        proj += part_ref[i].astype(F32)
    second = (x_ref[...].astype(F32) + mod_ref[2:3, :] * proj).astype(BF)
    second_ref[...] = second
    h = layer_norm(second.astype(F32), mod_ref[3:4, :], mod_ref[4:5, :]).astype(BF)
    for i in range(out_ref.shape[0]):
        out_ref[i] = h


def second_norm(tokens, parts, mods):
    return pl.pallas_call(
        second_norm_kernel,
        out_shape=[
            jax.ShapeDtypeStruct(tokens.shape, BF),
            jax.ShapeDtypeStruct(parts.shape, BF),
        ],
        compiler_params=params(6),
        name="second_norm",
    )(tokens, parts, mods)


def ffn_kernel(h_ref, up_ref, down_ref, out_ref, hidden_ref):
    step = pl.program_id(0)
    part = up_ref.shape[-1]

    @pl.when(step < 2)
    def _():
        up = jnp.concatenate([up_ref[0, 0], up_ref[0, 1]], axis=1)
        hidden_ref[lax.rem(step, 2)] = jax.nn.gelu(
            lax.dot_general(h_ref[...], up, NN, preferred_element_type=F32),
            approximate=True,
        ).astype(BF)

    @pl.when(step >= 2)
    def _():
        hidden = jnp.concatenate([hidden_ref[0], hidden_ref[1]], axis=1)
        down = jnp.concatenate(
            [
                jnp.concatenate([down_ref[0, y, :part], down_ref[0, y, part:]], axis=1)
                for y in range(4)
            ],
            axis=0,
        )
        out_ref[...] = lax.dot_general(
            hidden, down, NN, preferred_element_type=F32
        ).astype(BF)


def feed_forward(h, weights):
    rows, width = h.shape
    part = weights.shape[3]
    return pl.pallas_call(
        ffn_kernel,
        grid=(4,),
        out_shape=jax.ShapeDtypeStruct((rows, width), BF),
        in_specs=[
            pl.BlockSpec((rows, width), lambda i: (0, 0)),
            pl.BlockSpec((1, 2, width, part), lambda i: (0, jnp.minimum(i, 1), 0, 0)),
            pl.BlockSpec((1, 4, 2 * part, part), lambda i: (1, 0, jnp.maximum(i - 2, 0), 0)),
        ],
        out_specs=pl.BlockSpec((rows, 2 * part), lambda i: (0, jnp.maximum(i - 2, 0))),
        scratch_shapes=[pltpu.VMEM((2, rows, 2 * part), BF)],
        compiler_params=params(58),
        name="feed_forward",
    )(h, weights, weights)


def last_kernel(second_ref, part_ref, mod_ref, w_ref, state_ref, vel_ref):
    ffn = part_ref[0].astype(F32)
    for i in range(1, part_ref.shape[0]):
        ffn += part_ref[i].astype(F32)
    state = (second_ref[...].astype(F32) + mod_ref[5:6, :] * ffn).astype(BF)
    state_ref[...] = state
    h = layer_norm(state.astype(F32), mod_ref[6:7, :], mod_ref[7:8, :]).astype(BF)
    vel_ref[...] = lax.dot_general(h, w_ref[...], NN, preferred_element_type=F32)


def last_stage(second, parts, mods, w_final):
    return pl.pallas_call(
        last_kernel,
        out_shape=[
            jax.ShapeDtypeStruct(second.shape, BF),
            jax.ShapeDtypeStruct((second.shape[0], w_final.shape[1]), F32),
        ],
        compiler_params=params(6),
        name="last_stage",
    )(second, parts, mods, w_final)


def on_device(
    image_tokens,
    latent,
    modulation,
    text_kv,
    text_len,
    timestep,
    w_qkv,
    w_out,
    w_up,
    w_down,
    w_final,
):
    tokens = image_tokens[0]
    mods = modulation[0]
    rows, width = tokens.shape
    core = lax.axis_index("core")
    pos = jnp.concatenate([jnp.stack([core, lax.axis_index("ty")]).astype(jnp.int32), text_len])
    swap2 = [(0, 1), (1, 0)]

    def to_lines(value, step):
        return lax.ppermute(value, "ty", [(i, (i + step) % 4) for i in range(4)])

    own_qkv = jnp.transpose(w_qkv, (1, 2, 0))
    half_kv = lax.dynamic_slice(own_qkv, (1, core * 48, 0), (2, 48, width))
    place = jnp.stack([core, lax.axis_index("zp")]).astype(jnp.int32)
    h1, quarter = first_norm_and_pack(place, tokens, mods, w_up, w_down, 4)
    ffn_full = lax.all_gather(quarter, ("core", "tx", "zp"), axis=0, tiled=False)
    ffn_full = ffn_full.reshape(2, 4, width, w_up.shape[1])
    h1, half_kv = lax.optimization_barrier((h1, half_kv))
    h1 = lax.all_to_all(h1, "tx", split_axis=0, concat_axis=0, tiled=True)
    near_kv = [to_lines(half_kv, step) for step in STRIDES]

    half_q = lax.dynamic_slice(own_qkv, (0, core * 48, 0), (1, 48, width))
    half_out = lax.dynamic_slice(w_out, (core * 48, 0), (48, width))
    half_qo = jnp.concatenate([half_q, half_out[None]])
    text = lax.dynamic_slice_in_dim(text_kv[0], lax.axis_index("tx") * 384, 384, 2)
    text = jnp.transpose(text, (1, 0, 2))
    far_kv = lax.ppermute(jnp.stack(near_kv), "core", swap2)
    h1, half_qo, text = lax.optimization_barrier((h1, half_qo, text))
    near_qo = [to_lines(half_qo, step) for step in STRIDES]
    h1 = h1.reshape(4 * rows, width)
    own_kv = project(pos, h1, own_qkv, 1, 2, 4, near_kv, far_kv)
    all_kv = lax.all_to_all(own_kv, "ty", split_axis=0, concat_axis=0, tiled=True)
    *near_qo, own_kv = lax.optimization_barrier((*near_qo, own_kv))
    far_qo = lax.ppermute(jnp.stack(near_qo), "core", swap2)
    query = project(pos, h1, own_qkv, 0, 1, 1, near_qo, far_qo)[0, 0]

    state = attention(pos, query, own_kv, text=text)
    attended = attention(pos, query, all_kv, state=state)

    partial = out_projection(pos, attended, w_out, near_qo, far_qo)
    partial = partial.reshape(4, rows, width)
    partial = lax.all_to_all(partial, "tx", split_axis=0, concat_axis=0, tiled=True)
    second, h2 = second_norm(tokens, partial, mods)
    h2 = lax.all_to_all(h2, "ty", split_axis=0, concat_axis=0, tiled=True)
    partial = feed_forward(h2.reshape(4 * rows, width), ffn_full).reshape(4, rows, width)
    partial = lax.all_to_all(partial, "ty", split_axis=0, concat_axis=0, tiled=True)
    state, velocity = last_stage(second, partial, mods, w_final)

    step_index = timestep[0]
    delta = sigma_at(step_index + 1) - sigma_at(step_index)
    moved = latent[0] + delta * velocity.reshape(rows // 2, 2 * velocity.shape[1])
    return (state[None], moved[None])


def solution(mesh):
    fine = Mesh(
        mesh.devices.reshape(mesh.shape["req"] // 4, 2, 2, 4, 4, mesh.shape["blk"]),
        ("zl", "zp", "core", "tx", "ty", "blk"),
    )
    group = ("zl", "zp", "core", "blk")
    tile = ("tx", "ty")
    in_specs = (
        P(group, tile, None),
        P(group, tile, None),
        P(group, None, None),
        P(group, None, None, None),
        P(group),
        P(group),
        P(None, None, tile),
        P(tile, None),
        P(None, tile),
        P(tile, None),
        P(),
    )
    out_specs = (P(group, tile, None), P(group, tile, None))
    return jax.shard_map(
        on_device, mesh=fine, in_specs=in_specs, out_specs=out_specs, check_vma=False
    )
```

```python
import functools

import jax
import jax.numpy as jnp
from jax import lax
from jax.experimental import pallas as pl
from jax.experimental.pallas import tpu as pltpu
from jax.sharding import Mesh, PartitionSpec as P

HEAD_DIM = 64
TXT = 154
STEPS = 8
BF = jnp.bfloat16
F32 = jnp.float32
NT = (((1,), (1,)), ((), ()))
NN = (((1,), (0,)), ((), ()))
STRIDES = (1, 3, 2)


def params(mebibytes):
    return pltpu.CompilerParams(vmem_limit_bytes=mebibytes * 1024 * 1024)


def layer_norm(full, shift, scale):
    mean = jnp.mean(full, axis=-1, keepdims=True)
    cent = full - mean
    spread = jnp.mean(jnp.square(cent), axis=-1, keepdims=True)
    return cent * lax.rsqrt(spread + 1e-06) * (1.0 + scale) + shift


def sigma_at(index):
    frac = 1.0 - index.astype(F32) / STEPS
    return 3.0 * frac / (1.0 + 2.0 * frac)


def first_kernel(
    copies, pos_ref, x_ref, mod_ref, up_ref, down_ref, out_ref, pack_ref, held, load_sem, store_sem
):
    core = pos_ref[0]
    zone = pos_ref[1]
    part = down_ref.shape[0]

    def move(sources):
        loads = []
        stores = []
        for i, source in enumerate(sources):
            rows = pl.ds(i * part, part)
            loads.append(pltpu.make_async_copy(source, held.at[rows, :], load_sem.at[i]))
            stores.append(
                pltpu.make_async_copy(held.at[rows, :], pack_ref.at[rows, :], store_sem.at[i])
            )
        for load in loads:
            load.start()
        h = layer_norm(x_ref[...].astype(F32), mod_ref[0:1, :], mod_ref[1:2, :]).astype(BF)
        for i in range(copies):
            out_ref[i] = h
        for load, store in zip(loads, stores):
            load.wait()
            store.start()
        for store in stores:
            store.wait()

    for half in range(2):

        @pl.when(jnp.logical_and(core == 0, zone == half))
        def _():
            move([up_ref.at[pl.ds((2 * half + i) * part, part), :] for i in range(2)])

        @pl.when(jnp.logical_and(core == 1, zone == half))
        def _():
            move([down_ref.at[:, pl.ds((2 * half + i) * part, part)] for i in range(2)])


def first_norm_and_pack(pos, tokens, mods, w_up, w_down, copies):
    rows, width = tokens.shape
    part = w_down.shape[0]
    return pl.pallas_call(
        functools.partial(first_kernel, copies),
        out_shape=[
            jax.ShapeDtypeStruct((copies, rows, width), BF),
            jax.ShapeDtypeStruct((2 * part, part), BF),
        ],
        in_specs=[pl.BlockSpec(memory_space=pltpu.SMEM)]
        + [pl.BlockSpec(memory_space=pltpu.VMEM)] * 2
        + [pl.BlockSpec(memory_space=pltpu.HBM)] * 2,
        out_specs=[
            pl.BlockSpec(memory_space=pltpu.VMEM),
            pl.BlockSpec(memory_space=pltpu.HBM),
        ],
        scratch_shapes=[
            pltpu.VMEM((2 * part, part), BF),
            pltpu.SemaphoreType.DMA((2,)),
            pltpu.SemaphoreType.DMA((2,)),
        ],
        compiler_params=params(58),
        name="first_norm_and_pack",
    )(pos, tokens, mods, w_up, w_down)


def assemble(pos_ref, own_ref, near_refs, far_ref, store):
    core = pos_ref[0]
    row = pos_ref[1]
    store(row, 0, own_ref, 0)
    store(row, 1, own_ref, 1)
    for i, (near_ref, step) in enumerate(zip(near_refs, STRIDES)):
        source = lax.rem(row + 4 - step, 4)
        store(source, core, near_ref, None)
        store(source, 1 - core, far_ref, i)


def project_kernel(first, pos_ref, h_ref, own_ref, n0_ref, n1_ref, n2_ref, far_ref, out_ref, w_ref):
    count = out_ref.shape[1]

    def store(source, half, ref, index):
        for k in range(count):
            if ref is own_ref:
                value = ref[first + k, index * 48 : index * 48 + 48, :]
            elif index is None:
                value = ref[k]
            else:
                value = ref[index, k]
            w_ref[k, source, half] = value

    assemble(pos_ref, own_ref, (n0_ref, n1_ref, n2_ref), far_ref, store)
    h = h_ref[...]
    for k in range(count):
        w = w_ref[k].reshape(384, h.shape[1])
        value = lax.dot_general(h, w, NT, preferred_element_type=F32).astype(BF)
        for i in range(out_ref.shape[0]):
            out_ref[i, k] = value


def project(pos, h, own, first, count, copies, near, far):
    rows, width = h.shape
    return pl.pallas_call(
        functools.partial(project_kernel, first),
        out_shape=jax.ShapeDtypeStruct((copies, count, rows, 384), BF),
        in_specs=[pl.BlockSpec(memory_space=pltpu.SMEM)]
        + [pl.BlockSpec(memory_space=pltpu.VMEM)] * 6,
        scratch_shapes=[pltpu.VMEM((count, 4, 2, 48, width), BF)],
        compiler_params=params(14),
        name="project",
    )(pos, h, own, *near, far)


def attention_kernel(own, *refs):
    refs = list(refs)
    pos_ref, q_ref, kv_ref = refs[:3]
    if own:
        text_ref = refs[3]
        outs = refs[4:]
    else:
        state_ref = refs[3]
        outs = refs[4:]
    rows = q_ref.shape[0]
    if own:
        live = lax.broadcasted_iota(jnp.int32, (rows, TXT), 1) < pos_ref[2]
    first = lax.broadcasted_iota(jnp.int32, (rows, 128), 1) < HEAD_DIM
    where = [0] if own else [lax.rem(pos_ref[1] + i, 4) for i in (1, 2, 3)]
    lane = lax.broadcasted_iota(jnp.int32, (rows, 128), 1)
    stats = jnp.zeros((rows, 128), F32)
    for g in range(q_ref.shape[1] // 128):
        cols = slice(g * 128, g * 128 + 128)
        q = q_ref[:, cols]
        accs = []
        scales = []
        for side in range(2):
            head = 2 * g + side
            here = first if side == 0 else jnp.logical_not(first)
            qh = jnp.where(here, q, jnp.zeros_like(q))
            parts = []
            for i in where:
                s = (
                    lax.dot_general(qh, kv_ref[i, 0, :, cols], NT, preferred_element_type=F32)
                    * 0.125
                )
                parts.append((s, kv_ref[i, 1, :, cols]))
            if own:
                s = (
                    lax.dot_general(qh, text_ref[0, :, cols], NT, preferred_element_type=F32)
                    * 0.125
                )
                parts.append((jnp.where(live, s, -jnp.inf), text_ref[1, :, cols]))
            top = None
            for s, _ in parts:
                peak = jnp.max(s, axis=1, keepdims=True)
                top = peak if top is None else jnp.maximum(top, peak)
            if not own:
                old = state_ref[:, 384 + head : 385 + head]
                top = jnp.maximum(top, old)
            total = None
            acc = None
            for s, values in parts:
                p = jnp.exp(s - top)
                amount = jnp.sum(p, axis=1, keepdims=True)
                part = lax.dot_general(p.astype(BF), values, NN, preferred_element_type=F32)
                total = amount if total is None else total + amount
                acc = part if acc is None else acc + part
            if own:
                stats = jnp.where(lane == head, top, stats)
                stats = jnp.where(lane == HEAD_DIM + head, total, stats)
            else:
                factor = jnp.exp(old - top)
                total = total + state_ref[:, 448 + head : 449 + head] * factor
                scales.append((factor, total))
            accs.append(acc)
        acc = jnp.where(first, accs[0], accs[1])
        if own:
            outs[0][:, cols] = acc
        else:
            factor = jnp.where(first, scales[0][0], scales[1][0])
            total = jnp.where(first, scales[0][1], scales[1][1])
            outs[0][:, cols] = ((acc + state_ref[:, cols] * factor) / total).astype(BF)
    if own:
        outs[0][:, 384:] = stats


def attention(pos, q, kv, text=None, state=None):
    own = text is not None
    args = [q, kv, text if own else state]
    if own:
        out = jax.ShapeDtypeStruct((q.shape[0], 512), F32)
    else:
        out = jax.ShapeDtypeStruct(q.shape, BF)
    return pl.pallas_call(
        functools.partial(attention_kernel, own),
        out_shape=out,
        in_specs=[pl.BlockSpec(memory_space=pltpu.SMEM)]
        + [pl.BlockSpec(memory_space=pltpu.VMEM)] * len(args),
        compiler_params=params(16),
        name="attention",
    )(pos, *args)


def out_kernel(pos_ref, a_ref, own_ref, n0_ref, n1_ref, n2_ref, far_ref, out_ref, w_ref):
    def store(source, half, ref, index):
        if ref is own_ref:
            value = ref[index * 48 : index * 48 + 48, :]
        elif index is None:
            value = ref[1]
        else:
            value = ref[index, 1]
        w_ref[source, half] = value

    assemble(pos_ref, own_ref, (n0_ref, n1_ref, n2_ref), far_ref, store)
    w = w_ref[...].reshape(384, out_ref.shape[1])
    out_ref[...] = lax.dot_general(
        a_ref[...], w, NN, preferred_element_type=F32
    ).astype(BF)


def out_projection(pos, a, own, near, far):
    width = own.shape[1]
    return pl.pallas_call(
        out_kernel,
        out_shape=jax.ShapeDtypeStruct((a.shape[0], width), BF),
        in_specs=[pl.BlockSpec(memory_space=pltpu.SMEM)]
        + [pl.BlockSpec(memory_space=pltpu.VMEM)] * 6,
        scratch_shapes=[pltpu.VMEM((4, 2, 48, width), BF)],
        compiler_params=params(8),
        name="out_projection",
    )(pos, a, own, *near, far)


def second_norm_kernel(x_ref, part_ref, mod_ref, second_ref, out_ref):
    proj = part_ref[0].astype(F32)
    for i in range(1, part_ref.shape[0]):
        proj += part_ref[i].astype(F32)
    second = (x_ref[...].astype(F32) + mod_ref[2:3, :] * proj).astype(BF)
    second_ref[...] = second
    h = layer_norm(second.astype(F32), mod_ref[3:4, :], mod_ref[4:5, :]).astype(BF)
    for i in range(out_ref.shape[0]):
        out_ref[i] = h


def second_norm(tokens, parts, mods):
    return pl.pallas_call(
        second_norm_kernel,
        out_shape=[
            jax.ShapeDtypeStruct(tokens.shape, BF),
            jax.ShapeDtypeStruct(parts.shape, BF),
        ],
        compiler_params=params(6),
        name="second_norm",
    )(tokens, parts, mods)


def ffn_kernel(h_ref, up_ref, down_ref, out_ref, hidden_ref):
    step = pl.program_id(0)
    part = up_ref.shape[-1]

    @pl.when(step < 2)
    def _():
        up = jnp.concatenate([up_ref[0, 0], up_ref[0, 1]], axis=1)
        hidden_ref[lax.rem(step, 2)] = jax.nn.gelu(
            lax.dot_general(h_ref[...], up, NN, preferred_element_type=F32),
            approximate=True,
        ).astype(BF)

    @pl.when(step >= 2)
    def _():
        hidden = jnp.concatenate([hidden_ref[0], hidden_ref[1]], axis=1)
        down = jnp.concatenate(
            [
                jnp.concatenate([down_ref[0, y, :part], down_ref[0, y, part:]], axis=1)
                for y in range(4)
            ],
            axis=0,
        )
        out_ref[...] = lax.dot_general(
            hidden, down, NN, preferred_element_type=F32
        ).astype(BF)


def feed_forward(h, weights):
    rows, width = h.shape
    part = weights.shape[3]
    return pl.pallas_call(
        ffn_kernel,
        grid=(4,),
        out_shape=jax.ShapeDtypeStruct((rows, width), BF),
        in_specs=[
            pl.BlockSpec((rows, width), lambda i: (0, 0)),
            pl.BlockSpec((1, 2, width, part), lambda i: (0, jnp.minimum(i, 1), 0, 0)),
            pl.BlockSpec((1, 4, 2 * part, part), lambda i: (1, 0, jnp.maximum(i - 2, 0), 0)),
        ],
        out_specs=pl.BlockSpec((rows, 2 * part), lambda i: (0, jnp.maximum(i - 2, 0))),
        scratch_shapes=[pltpu.VMEM((2, rows, 2 * part), BF)],
        compiler_params=params(58),
        name="feed_forward",
    )(h, weights, weights)


def last_kernel(second_ref, part_ref, mod_ref, w_ref, state_ref, vel_ref):
    ffn = part_ref[0].astype(F32)
    for i in range(1, part_ref.shape[0]):
        ffn += part_ref[i].astype(F32)
    state = (second_ref[...].astype(F32) + mod_ref[5:6, :] * ffn).astype(BF)
    state_ref[...] = state
    h = layer_norm(state.astype(F32), mod_ref[6:7, :], mod_ref[7:8, :]).astype(BF)
    vel_ref[...] = lax.dot_general(h, w_ref[...], NN, preferred_element_type=F32)


def last_stage(second, parts, mods, w_final):
    return pl.pallas_call(
        last_kernel,
        out_shape=[
            jax.ShapeDtypeStruct(second.shape, BF),
            jax.ShapeDtypeStruct((second.shape[0], w_final.shape[1]), F32),
        ],
        compiler_params=params(6),
        name="last_stage",
    )(second, parts, mods, w_final)


def on_device(
    image_tokens,
    latent,
    modulation,
    text_kv,
    text_len,
    timestep,
    w_qkv,
    w_out,
    w_up,
    w_down,
    w_final,
):
    tokens = image_tokens[0]
    mods = modulation[0]
    rows, width = tokens.shape
    core = lax.axis_index("core")
    pos = jnp.concatenate([jnp.stack([core, lax.axis_index("ty")]).astype(jnp.int32), text_len])
    swap2 = [(0, 1), (1, 0)]

    def to_lines(value, step):
        return lax.ppermute(value, "ty", [(i, (i + step) % 4) for i in range(4)])

    own_qkv = jnp.transpose(w_qkv, (1, 2, 0))
    half_kv = lax.dynamic_slice(own_qkv, (1, core * 48, 0), (2, 48, width))
    place = jnp.stack([core, lax.axis_index("zp")]).astype(jnp.int32)
    h1, quarter = first_norm_and_pack(place, tokens, mods, w_up, w_down, 4)
    ffn_full = lax.all_gather(quarter, ("core", "tx", "zp"), axis=0, tiled=False)
    ffn_full = ffn_full.reshape(2, 4, width, w_up.shape[1])
    h1, half_kv = lax.optimization_barrier((h1, half_kv))
    h1 = lax.all_to_all(h1, "tx", split_axis=0, concat_axis=0, tiled=True)
    near_kv = [to_lines(half_kv, step) for step in STRIDES]

    half_q = lax.dynamic_slice(own_qkv, (0, core * 48, 0), (1, 48, width))
    half_out = lax.dynamic_slice(w_out, (core * 48, 0), (48, width))
    half_qo = jnp.concatenate([half_q, half_out[None]])
    text = lax.dynamic_slice_in_dim(text_kv[0], lax.axis_index("tx") * 384, 384, 2)
    text = jnp.transpose(text, (1, 0, 2))
    *near_kv, h1 = lax.optimization_barrier((*near_kv, h1))
    far_kv = lax.ppermute(jnp.stack(near_kv), "core", swap2)
    h1, half_qo, text = lax.optimization_barrier((h1, half_qo, text))
    near_qo = [to_lines(half_qo, step) for step in STRIDES]
    h1 = h1.reshape(4 * rows, width)
    own_kv = project(pos, h1, own_qkv, 1, 2, 4, near_kv, far_kv)
    all_kv = lax.all_to_all(own_kv, "ty", split_axis=0, concat_axis=0, tiled=True)
    *near_qo, own_kv = lax.optimization_barrier((*near_qo, own_kv))
    far_qo = lax.ppermute(jnp.stack(near_qo), "core", swap2)
    query = project(pos, h1, own_qkv, 0, 1, 1, near_qo, far_qo)[0, 0]

    state = attention(pos, query, own_kv, text=text)
    attended = attention(pos, query, all_kv, state=state)

    partial = out_projection(pos, attended, w_out, near_qo, far_qo)
    partial = partial.reshape(4, rows, width)
    partial = lax.all_to_all(partial, "tx", split_axis=0, concat_axis=0, tiled=True)
    second, h2 = second_norm(tokens, partial, mods)
    h2 = lax.all_to_all(h2, "ty", split_axis=0, concat_axis=0, tiled=True)
    partial = feed_forward(h2.reshape(4 * rows, width), ffn_full).reshape(4, rows, width)
    partial = lax.all_to_all(partial, "ty", split_axis=0, concat_axis=0, tiled=True)
    state, velocity = last_stage(second, partial, mods, w_final)

    step_index = timestep[0]
    delta = sigma_at(step_index + 1) - sigma_at(step_index)
    moved = latent[0] + delta * velocity.reshape(rows // 2, 2 * velocity.shape[1])
    return (state[None], moved[None])


def solution(mesh):
    fine = Mesh(
        mesh.devices.reshape(mesh.shape["req"] // 4, 2, 2, 4, 4, mesh.shape["blk"]),
        ("zl", "zp", "core", "tx", "ty", "blk"),
    )
    group = ("zl", "zp", "core", "blk")
    tile = ("tx", "ty")
    in_specs = (
        P(group, tile, None),
        P(group, tile, None),
        P(group, None, None),
        P(group, None, None, None),
        P(group),
        P(group),
        P(None, None, tile),
        P(tile, None),
        P(None, tile),
        P(tile, None),
        P(),
    )
    out_specs = (P(group, tile, None), P(group, tile, None))
    return jax.shard_map(
        on_device, mesh=fine, in_specs=in_specs, out_specs=out_specs, check_vma=False
    )
```

```python
import functools

import jax
import jax.numpy as jnp
from jax import lax
from jax.experimental import pallas as pl
from jax.experimental.pallas import tpu as pltpu
from jax.sharding import Mesh, PartitionSpec as P

HEAD_DIM = 64
TXT = 154
STEPS = 8
BF = jnp.bfloat16
F32 = jnp.float32
NT = (((1,), (1,)), ((), ()))
NN = (((1,), (0,)), ((), ()))
STRIDES = (1, 3, 2)


def params(mebibytes):
    return pltpu.CompilerParams(vmem_limit_bytes=mebibytes * 1024 * 1024)


def layer_norm(full, shift, scale):
    mean = jnp.mean(full, axis=-1, keepdims=True)
    cent = full - mean
    spread = jnp.mean(jnp.square(cent), axis=-1, keepdims=True)
    return cent * lax.rsqrt(spread + 1e-06) * (1.0 + scale) + shift


def sigma_at(index):
    frac = 1.0 - index.astype(F32) / STEPS
    return 3.0 * frac / (1.0 + 2.0 * frac)


def first_kernel(
    copies, pos_ref, x_ref, mod_ref, up_ref, down_ref, out_ref, pack_ref, held, load_sem, store_sem
):
    core = pos_ref[0]
    zone = pos_ref[1]
    part = down_ref.shape[0]

    def move(sources):
        loads = []
        stores = []
        for i, source in enumerate(sources):
            rows = pl.ds(i * part, part)
            loads.append(pltpu.make_async_copy(source, held.at[rows, :], load_sem.at[i]))
            stores.append(
                pltpu.make_async_copy(held.at[rows, :], pack_ref.at[rows, :], store_sem.at[i])
            )
        for load in loads:
            load.start()
        h = layer_norm(x_ref[...].astype(F32), mod_ref[0:1, :], mod_ref[1:2, :]).astype(BF)
        for i in range(copies):
            out_ref[i] = h
        for load, store in zip(loads, stores):
            load.wait()
            store.start()
        for store in stores:
            store.wait()

    for half in range(2):

        @pl.when(jnp.logical_and(core == 0, zone == half))
        def _():
            move([up_ref.at[pl.ds((2 * half + i) * part, part), :] for i in range(2)])

        @pl.when(jnp.logical_and(core == 1, zone == half))
        def _():
            move([down_ref.at[:, pl.ds((2 * half + i) * part, part)] for i in range(2)])


def first_norm_and_pack(pos, tokens, mods, w_up, w_down, copies):
    rows, width = tokens.shape
    part = w_down.shape[0]
    return pl.pallas_call(
        functools.partial(first_kernel, copies),
        out_shape=[
            jax.ShapeDtypeStruct((copies, rows, width), BF),
            jax.ShapeDtypeStruct((2 * part, part), BF),
        ],
        in_specs=[pl.BlockSpec(memory_space=pltpu.SMEM)]
        + [pl.BlockSpec(memory_space=pltpu.VMEM)] * 2
        + [pl.BlockSpec(memory_space=pltpu.HBM)] * 2,
        out_specs=[
            pl.BlockSpec(memory_space=pltpu.VMEM),
            pl.BlockSpec(memory_space=pltpu.HBM),
        ],
        scratch_shapes=[
            pltpu.VMEM((2 * part, part), BF),
            pltpu.SemaphoreType.DMA((2,)),
            pltpu.SemaphoreType.DMA((2,)),
        ],
        compiler_params=params(58),
        name="first_norm_and_pack",
    )(pos, tokens, mods, w_up, w_down)


def assemble(pos_ref, own_ref, near_refs, far_ref, store):
    core = pos_ref[0]
    row = pos_ref[1]
    store(row, 0, own_ref, 0)
    store(row, 1, own_ref, 1)
    for i, (near_ref, step) in enumerate(zip(near_refs, STRIDES)):
        source = lax.rem(row + 4 - step, 4)
        store(source, core, near_ref, None)
        store(source, 1 - core, far_ref, i)


def project_kernel(first, pos_ref, h_ref, own_ref, n0_ref, n1_ref, n2_ref, far_ref, out_ref, w_ref):
    k = pl.program_id(0)

    def store(source, half, ref, index):
        if ref is own_ref:
            value = ref[first + k, index * 48 : index * 48 + 48, :]
        elif index is None:
            value = ref[k]
        else:
            value = ref[index, k]
        w_ref[source, half] = value

    assemble(pos_ref, own_ref, (n0_ref, n1_ref, n2_ref), far_ref, store)
    w = w_ref[...].reshape(384, h_ref.shape[1])
    value = lax.dot_general(h_ref[...], w, NT, preferred_element_type=F32).astype(BF)
    for i in range(out_ref.shape[0]):
        out_ref[i, 0] = value


def project(pos, h, own, first, count, copies, near, far):
    rows, width = h.shape
    return pl.pallas_call(
        functools.partial(project_kernel, first),
        grid=(count,),
        out_shape=jax.ShapeDtypeStruct((copies, count, rows, 384), BF),
        in_specs=[pl.BlockSpec(memory_space=pltpu.SMEM)]
        + [pl.BlockSpec(memory_space=pltpu.VMEM)] * 6,
        out_specs=pl.BlockSpec((copies, 1, rows, 384), lambda k: (0, k, 0, 0)),
        scratch_shapes=[pltpu.VMEM((4, 2, 48, width), BF)],
        compiler_params=params(14),
        name="project",
    )(pos, h, own, *near, far)


def attention_kernel(own, *refs):
    refs = list(refs)
    pos_ref, q_ref, kv_ref = refs[:3]
    if own:
        text_ref = refs[3]
        outs = refs[4:]
    else:
        state_ref = refs[3]
        outs = refs[4:]
    rows = q_ref.shape[0]
    if own:
        live = lax.broadcasted_iota(jnp.int32, (rows, TXT), 1) < pos_ref[2]
    first = lax.broadcasted_iota(jnp.int32, (rows, 128), 1) < HEAD_DIM
    where = [0] if own else [lax.rem(pos_ref[1] + i, 4) for i in (1, 2, 3)]
    lane = lax.broadcasted_iota(jnp.int32, (rows, 128), 1)
    stats = jnp.zeros((rows, 128), F32)
    for g in range(q_ref.shape[1] // 128):
        cols = slice(g * 128, g * 128 + 128)
        q = q_ref[:, cols]
        accs = []
        scales = []
        for side in range(2):
            head = 2 * g + side
            here = first if side == 0 else jnp.logical_not(first)
            qh = jnp.where(here, q, jnp.zeros_like(q))
            parts = []
            for i in where:
                s = (
                    lax.dot_general(qh, kv_ref[i, 0, :, cols], NT, preferred_element_type=F32)
                    * 0.125
                )
                parts.append((s, kv_ref[i, 1, :, cols]))
            if own:
                s = (
                    lax.dot_general(qh, text_ref[0, :, cols], NT, preferred_element_type=F32)
                    * 0.125
                )
                parts.append((jnp.where(live, s, -jnp.inf), text_ref[1, :, cols]))
            top = None
            for s, _ in parts:
                peak = jnp.max(s, axis=1, keepdims=True)
                top = peak if top is None else jnp.maximum(top, peak)
            if not own:
                old = state_ref[:, 384 + head : 385 + head]
                top = jnp.maximum(top, old)
            total = None
            acc = None
            for s, values in parts:
                p = jnp.exp(s - top)
                amount = jnp.sum(p, axis=1, keepdims=True)
                part = lax.dot_general(p.astype(BF), values, NN, preferred_element_type=F32)
                total = amount if total is None else total + amount
                acc = part if acc is None else acc + part
            if own:
                stats = jnp.where(lane == head, top, stats)
                stats = jnp.where(lane == HEAD_DIM + head, total, stats)
            else:
                factor = jnp.exp(old - top)
                total = total + state_ref[:, 448 + head : 449 + head] * factor
                scales.append((factor, total))
            accs.append(acc)
        acc = jnp.where(first, accs[0], accs[1])
        if own:
            outs[0][:, cols] = acc
        else:
            factor = jnp.where(first, scales[0][0], scales[1][0])
            total = jnp.where(first, scales[0][1], scales[1][1])
            outs[0][:, cols] = ((acc + state_ref[:, cols] * factor) / total).astype(BF)
    if own:
        outs[0][:, 384:] = stats


def attention(pos, q, kv, text=None, state=None):
    own = text is not None
    args = [q, kv, text if own else state]
    if own:
        out = jax.ShapeDtypeStruct((q.shape[0], 512), F32)
    else:
        out = jax.ShapeDtypeStruct(q.shape, BF)
    return pl.pallas_call(
        functools.partial(attention_kernel, own),
        out_shape=out,
        in_specs=[pl.BlockSpec(memory_space=pltpu.SMEM)]
        + [pl.BlockSpec(memory_space=pltpu.VMEM)] * len(args),
        compiler_params=params(16),
        name="attention",
    )(pos, *args)


def out_kernel(pos_ref, a_ref, own_ref, n0_ref, n1_ref, n2_ref, far_ref, out_ref, w_ref):
    def store(source, half, ref, index):
        if ref is own_ref:
            value = ref[index * 48 : index * 48 + 48, :]
        elif index is None:
            value = ref[1]
        else:
            value = ref[index, 1]
        w_ref[source, half] = value

    assemble(pos_ref, own_ref, (n0_ref, n1_ref, n2_ref), far_ref, store)
    w = w_ref[...].reshape(384, out_ref.shape[1])
    out_ref[...] = lax.dot_general(
        a_ref[...], w, NN, preferred_element_type=F32
    ).astype(BF)


def out_projection(pos, a, own, near, far):
    width = own.shape[1]
    return pl.pallas_call(
        out_kernel,
        out_shape=jax.ShapeDtypeStruct((a.shape[0], width), BF),
        in_specs=[pl.BlockSpec(memory_space=pltpu.SMEM)]
        + [pl.BlockSpec(memory_space=pltpu.VMEM)] * 6,
        scratch_shapes=[pltpu.VMEM((4, 2, 48, width), BF)],
        compiler_params=params(8),
        name="out_projection",
    )(pos, a, own, *near, far)


def second_norm_kernel(x_ref, part_ref, mod_ref, second_ref, out_ref):
    proj = part_ref[0].astype(F32)
    for i in range(1, part_ref.shape[0]):
        proj += part_ref[i].astype(F32)
    second = (x_ref[...].astype(F32) + mod_ref[2:3, :] * proj).astype(BF)
    second_ref[...] = second
    h = layer_norm(second.astype(F32), mod_ref[3:4, :], mod_ref[4:5, :]).astype(BF)
    for i in range(out_ref.shape[0]):
        out_ref[i] = h


def second_norm(tokens, parts, mods):
    return pl.pallas_call(
        second_norm_kernel,
        out_shape=[
            jax.ShapeDtypeStruct(tokens.shape, BF),
            jax.ShapeDtypeStruct(parts.shape, BF),
        ],
        compiler_params=params(6),
        name="second_norm",
    )(tokens, parts, mods)


def ffn_kernel(h_ref, up_ref, down_ref, out_ref, hidden_ref):
    step = pl.program_id(0)
    part = up_ref.shape[-1]

    @pl.when(step < 2)
    def _():
        up = jnp.concatenate([up_ref[0, 0], up_ref[0, 1]], axis=1)
        hidden_ref[lax.rem(step, 2)] = jax.nn.gelu(
            lax.dot_general(h_ref[...], up, NN, preferred_element_type=F32),
            approximate=True,
        ).astype(BF)

    @pl.when(step >= 2)
    def _():
        hidden = jnp.concatenate([hidden_ref[0], hidden_ref[1]], axis=1)
        down = jnp.concatenate(
            [
                jnp.concatenate([down_ref[0, y, :part], down_ref[0, y, part:]], axis=1)
                for y in range(4)
            ],
            axis=0,
        )
        out_ref[...] = lax.dot_general(
            hidden, down, NN, preferred_element_type=F32
        ).astype(BF)


def feed_forward(h, weights):
    rows, width = h.shape
    part = weights.shape[3]
    return pl.pallas_call(
        ffn_kernel,
        grid=(4,),
        out_shape=jax.ShapeDtypeStruct((rows, width), BF),
        in_specs=[
            pl.BlockSpec((rows, width), lambda i: (0, 0)),
            pl.BlockSpec((1, 2, width, part), lambda i: (0, jnp.minimum(i, 1), 0, 0)),
            pl.BlockSpec((1, 4, 2 * part, part), lambda i: (1, 0, jnp.maximum(i - 2, 0), 0)),
        ],
        out_specs=pl.BlockSpec((rows, 2 * part), lambda i: (0, jnp.maximum(i - 2, 0))),
        scratch_shapes=[pltpu.VMEM((2, rows, 2 * part), BF)],
        compiler_params=params(58),
        name="feed_forward",
    )(h, weights, weights)


def last_kernel(second_ref, part_ref, mod_ref, w_ref, state_ref, vel_ref):
    ffn = part_ref[0].astype(F32)
    for i in range(1, part_ref.shape[0]):
        ffn += part_ref[i].astype(F32)
    state = (second_ref[...].astype(F32) + mod_ref[5:6, :] * ffn).astype(BF)
    state_ref[...] = state
    h = layer_norm(state.astype(F32), mod_ref[6:7, :], mod_ref[7:8, :]).astype(BF)
    vel_ref[...] = lax.dot_general(h, w_ref[...], NN, preferred_element_type=F32)


def last_stage(second, parts, mods, w_final):
    return pl.pallas_call(
        last_kernel,
        out_shape=[
            jax.ShapeDtypeStruct(second.shape, BF),
            jax.ShapeDtypeStruct((second.shape[0], w_final.shape[1]), F32),
        ],
        compiler_params=params(6),
        name="last_stage",
    )(second, parts, mods, w_final)


def on_device(
    image_tokens,
    latent,
    modulation,
    text_kv,
    text_len,
    timestep,
    w_qkv,
    w_out,
    w_up,
    w_down,
    w_final,
):
    tokens = image_tokens[0]
    mods = modulation[0]
    rows, width = tokens.shape
    core = lax.axis_index("core")
    pos = jnp.concatenate([jnp.stack([core, lax.axis_index("ty")]).astype(jnp.int32), text_len])
    swap2 = [(0, 1), (1, 0)]

    def to_lines(value, step):
        return lax.ppermute(value, "ty", [(i, (i + step) % 4) for i in range(4)])

    own_qkv = jnp.transpose(w_qkv, (1, 2, 0))
    half_kv = lax.dynamic_slice(own_qkv, (1, core * 48, 0), (2, 48, width))
    place = jnp.stack([core, lax.axis_index("zp")]).astype(jnp.int32)
    h1, quarter = first_norm_and_pack(place, tokens, mods, w_up, w_down, 4)
    ffn_full = lax.all_gather(quarter, ("core", "tx", "zp"), axis=0, tiled=False)
    ffn_full = ffn_full.reshape(2, 4, width, w_up.shape[1])
    h1, half_kv = lax.optimization_barrier((h1, half_kv))
    h1 = lax.all_to_all(h1, "tx", split_axis=0, concat_axis=0, tiled=True)
    near_kv = [to_lines(half_kv, step) for step in STRIDES]

    half_q = lax.dynamic_slice(own_qkv, (0, core * 48, 0), (1, 48, width))
    half_out = lax.dynamic_slice(w_out, (core * 48, 0), (48, width))
    half_qo = jnp.concatenate([half_q, half_out[None]])
    text = lax.dynamic_slice_in_dim(text_kv[0], lax.axis_index("tx") * 384, 384, 2)
    text = jnp.transpose(text, (1, 0, 2))
    far_kv = lax.ppermute(jnp.stack(near_kv), "core", swap2)
    h1, half_qo, text = lax.optimization_barrier((h1, half_qo, text))
    near_qo = [to_lines(half_qo, step) for step in STRIDES]
    h1 = h1.reshape(4 * rows, width)
    own_kv = project(pos, h1, own_qkv, 1, 2, 4, near_kv, far_kv)
    all_kv = lax.all_to_all(own_kv, "ty", split_axis=0, concat_axis=0, tiled=True)
    *near_qo, own_kv = lax.optimization_barrier((*near_qo, own_kv))
    far_qo = lax.ppermute(jnp.stack(near_qo), "core", swap2)
    query = project(pos, h1, own_qkv, 0, 1, 1, near_qo, far_qo)[0, 0]

    state = attention(pos, query, own_kv, text=text)
    attended = attention(pos, query, all_kv, state=state)

    partial = out_projection(pos, attended, w_out, near_qo, far_qo)
    partial = partial.reshape(4, rows, width)
    partial = lax.all_to_all(partial, "tx", split_axis=0, concat_axis=0, tiled=True)
    second, h2 = second_norm(tokens, partial, mods)
    h2 = lax.all_to_all(h2, "ty", split_axis=0, concat_axis=0, tiled=True)
    partial = feed_forward(h2.reshape(4 * rows, width), ffn_full).reshape(4, rows, width)
    partial = lax.all_to_all(partial, "ty", split_axis=0, concat_axis=0, tiled=True)
    state, velocity = last_stage(second, partial, mods, w_final)

    step_index = timestep[0]
    delta = sigma_at(step_index + 1) - sigma_at(step_index)
    moved = latent[0] + delta * velocity.reshape(rows // 2, 2 * velocity.shape[1])
    return (state[None], moved[None])


def solution(mesh):
    fine = Mesh(
        mesh.devices.reshape(mesh.shape["req"] // 4, 2, 2, 4, 4, mesh.shape["blk"]),
        ("zl", "zp", "core", "tx", "ty", "blk"),
    )
    group = ("zl", "zp", "core", "blk")
    tile = ("tx", "ty")
    in_specs = (
        P(group, tile, None),
        P(group, tile, None),
        P(group, None, None),
        P(group, None, None, None),
        P(group),
        P(group),
        P(None, None, tile),
        P(tile, None),
        P(None, tile),
        P(tile, None),
        P(),
    )
    out_specs = (P(group, tile, None), P(group, tile, None))
    return jax.shard_map(
        on_device, mesh=fine, in_specs=in_specs, out_specs=out_specs, check_vma=False
    )
```

```python
import functools

import jax
import jax.numpy as jnp
from jax import lax
from jax.experimental import pallas as pl
from jax.experimental.pallas import tpu as pltpu
from jax.sharding import Mesh, PartitionSpec as P

HEAD_DIM = 64
TXT = 154
STEPS = 8
BF = jnp.bfloat16
F32 = jnp.float32
NT = (((1,), (1,)), ((), ()))
NN = (((1,), (0,)), ((), ()))
STRIDES = (2, 1, 3)


def params(mebibytes):
    return pltpu.CompilerParams(vmem_limit_bytes=mebibytes * 1024 * 1024)


def layer_norm(full, shift, scale):
    mean = jnp.mean(full, axis=-1, keepdims=True)
    cent = full - mean
    spread = jnp.mean(jnp.square(cent), axis=-1, keepdims=True)
    return cent * lax.rsqrt(spread + 1e-06) * (1.0 + scale) + shift


def sigma_at(index):
    frac = 1.0 - index.astype(F32) / STEPS
    return 3.0 * frac / (1.0 + 2.0 * frac)


def first_kernel(
    copies, pos_ref, x_ref, mod_ref, up_ref, down_ref, out_ref, pack_ref, held, load_sem, store_sem
):
    core = pos_ref[0]
    zone = pos_ref[1]
    part = down_ref.shape[0]

    def move(sources):
        loads = []
        stores = []
        for i, source in enumerate(sources):
            rows = pl.ds(i * part, part)
            loads.append(pltpu.make_async_copy(source, held.at[rows, :], load_sem.at[i]))
            stores.append(
                pltpu.make_async_copy(held.at[rows, :], pack_ref.at[rows, :], store_sem.at[i])
            )
        for load in loads:
            load.start()
        h = layer_norm(x_ref[...].astype(F32), mod_ref[0:1, :], mod_ref[1:2, :]).astype(BF)
        for i in range(copies):
            out_ref[i] = h
        for load, store in zip(loads, stores):
            load.wait()
            store.start()
        for store in stores:
            store.wait()

    for half in range(2):

        @pl.when(jnp.logical_and(core == 0, zone == half))
        def _():
            move([up_ref.at[pl.ds((2 * half + i) * part, part), :] for i in range(2)])

        @pl.when(jnp.logical_and(core == 1, zone == half))
        def _():
            move([down_ref.at[:, pl.ds((2 * half + i) * part, part)] for i in range(2)])


def first_norm_and_pack(pos, tokens, mods, w_up, w_down, copies):
    rows, width = tokens.shape
    part = w_down.shape[0]
    return pl.pallas_call(
        functools.partial(first_kernel, copies),
        out_shape=[
            jax.ShapeDtypeStruct((copies, rows, width), BF),
            jax.ShapeDtypeStruct((2 * part, part), BF),
        ],
        in_specs=[pl.BlockSpec(memory_space=pltpu.SMEM)]
        + [pl.BlockSpec(memory_space=pltpu.VMEM)] * 2
        + [pl.BlockSpec(memory_space=pltpu.HBM)] * 2,
        out_specs=[
            pl.BlockSpec(memory_space=pltpu.VMEM),
            pl.BlockSpec(memory_space=pltpu.HBM),
        ],
        scratch_shapes=[
            pltpu.VMEM((2 * part, part), BF),
            pltpu.SemaphoreType.DMA((2,)),
            pltpu.SemaphoreType.DMA((2,)),
        ],
        compiler_params=params(58),
        name="first_norm_and_pack",
    )(pos, tokens, mods, w_up, w_down)


def assemble(pos_ref, own_ref, near_refs, far_ref, store):
    core = pos_ref[0]
    row = pos_ref[1]
    store(row, 0, own_ref, 0)
    store(row, 1, own_ref, 1)
    for i, (near_ref, step) in enumerate(zip(near_refs, STRIDES)):
        source = lax.rem(row + 4 - step, 4)
        store(source, core, near_ref, None)
        store(source, 1 - core, far_ref, i)


def project_kernel(first, pos_ref, h_ref, own_ref, n0_ref, n1_ref, n2_ref, far_ref, out_ref, w_ref):
    count = out_ref.shape[1]

    def store(source, half, ref, index):
        for k in range(count):
            if ref is own_ref:
                value = ref[first + k, index * 48 : index * 48 + 48, :]
            elif index is None:
                value = ref[k]
            else:
                value = ref[index, k]
            w_ref[k, source, half] = value

    assemble(pos_ref, own_ref, (n0_ref, n1_ref, n2_ref), far_ref, store)
    h = h_ref[...]
    for k in range(count):
        w = w_ref[k].reshape(384, h.shape[1])
        value = lax.dot_general(h, w, NT, preferred_element_type=F32).astype(BF)
        for i in range(out_ref.shape[0]):
            out_ref[i, k] = value


def project(pos, h, own, first, count, copies, near, far):
    rows, width = h.shape
    return pl.pallas_call(
        functools.partial(project_kernel, first),
        out_shape=jax.ShapeDtypeStruct((copies, count, rows, 384), BF),
        in_specs=[pl.BlockSpec(memory_space=pltpu.SMEM)]
        + [pl.BlockSpec(memory_space=pltpu.VMEM)] * 6,
        scratch_shapes=[pltpu.VMEM((count, 4, 2, 48, width), BF)],
        compiler_params=params(14),
        name="project",
    )(pos, h, own, *near, far)


def attention_kernel(own, *refs):
    refs = list(refs)
    pos_ref, q_ref, kv_ref = refs[:3]
    if own:
        text_ref = refs[3]
        outs = refs[4:]
    else:
        state_ref = refs[3]
        outs = refs[4:]
    rows = q_ref.shape[0]
    if own:
        live = lax.broadcasted_iota(jnp.int32, (rows, TXT), 1) < pos_ref[2]
    first = lax.broadcasted_iota(jnp.int32, (rows, 128), 1) < HEAD_DIM
    where = [0] if own else [lax.rem(pos_ref[1] + i, 4) for i in (1, 2, 3)]
    lane = lax.broadcasted_iota(jnp.int32, (rows, 128), 1)
    stats = jnp.zeros((rows, 128), F32)
    for g in range(q_ref.shape[1] // 128):
        cols = slice(g * 128, g * 128 + 128)
        q = q_ref[:, cols]
        accs = []
        scales = []
        for side in range(2):
            head = 2 * g + side
            here = first if side == 0 else jnp.logical_not(first)
            qh = jnp.where(here, q, jnp.zeros_like(q))
            parts = []
            for i in where:
                s = (
                    lax.dot_general(qh, kv_ref[i, 0, :, cols], NT, preferred_element_type=F32)
                    * 0.125
                )
                parts.append((s, kv_ref[i, 1, :, cols]))
            if own:
                s = (
                    lax.dot_general(qh, text_ref[0, :, cols], NT, preferred_element_type=F32)
                    * 0.125
                )
                parts.append((jnp.where(live, s, -jnp.inf), text_ref[1, :, cols]))
            top = None
            for s, _ in parts:
                peak = jnp.max(s, axis=1, keepdims=True)
                top = peak if top is None else jnp.maximum(top, peak)
            if not own:
                old = state_ref[:, 384 + head : 385 + head]
                top = jnp.maximum(top, old)
            total = None
            acc = None
            for s, values in parts:
                p = jnp.exp(s - top)
                amount = jnp.sum(p, axis=1, keepdims=True)
                part = lax.dot_general(p.astype(BF), values, NN, preferred_element_type=F32)
                total = amount if total is None else total + amount
                acc = part if acc is None else acc + part
            if own:
                stats = jnp.where(lane == head, top, stats)
                stats = jnp.where(lane == HEAD_DIM + head, total, stats)
            else:
                factor = jnp.exp(old - top)
                total = total + state_ref[:, 448 + head : 449 + head] * factor
                scales.append((factor, total))
            accs.append(acc)
        acc = jnp.where(first, accs[0], accs[1])
        if own:
            outs[0][:, cols] = acc
        else:
            factor = jnp.where(first, scales[0][0], scales[1][0])
            total = jnp.where(first, scales[0][1], scales[1][1])
            outs[0][:, cols] = ((acc + state_ref[:, cols] * factor) / total).astype(BF)
    if own:
        outs[0][:, 384:] = stats


def attention(pos, q, kv, text=None, state=None):
    own = text is not None
    args = [q, kv, text if own else state]
    if own:
        out = jax.ShapeDtypeStruct((q.shape[0], 512), F32)
    else:
        out = jax.ShapeDtypeStruct(q.shape, BF)
    return pl.pallas_call(
        functools.partial(attention_kernel, own),
        out_shape=out,
        in_specs=[pl.BlockSpec(memory_space=pltpu.SMEM)]
        + [pl.BlockSpec(memory_space=pltpu.VMEM)] * len(args),
        compiler_params=params(16),
        name="attention",
    )(pos, *args)


def out_kernel(pos_ref, a_ref, own_ref, n0_ref, n1_ref, n2_ref, far_ref, out_ref, w_ref):
    def store(source, half, ref, index):
        if ref is own_ref:
            value = ref[index * 48 : index * 48 + 48, :]
        elif index is None:
            value = ref[1]
        else:
            value = ref[index, 1]
        w_ref[source, half] = value

    assemble(pos_ref, own_ref, (n0_ref, n1_ref, n2_ref), far_ref, store)
    w = w_ref[...].reshape(384, out_ref.shape[1])
    out_ref[...] = lax.dot_general(
        a_ref[...], w, NN, preferred_element_type=F32
    ).astype(BF)


def out_projection(pos, a, own, near, far):
    width = own.shape[1]
    return pl.pallas_call(
        out_kernel,
        out_shape=jax.ShapeDtypeStruct((a.shape[0], width), BF),
        in_specs=[pl.BlockSpec(memory_space=pltpu.SMEM)]
        + [pl.BlockSpec(memory_space=pltpu.VMEM)] * 6,
        scratch_shapes=[pltpu.VMEM((4, 2, 48, width), BF)],
        compiler_params=params(8),
        name="out_projection",
    )(pos, a, own, *near, far)


def second_norm_kernel(x_ref, part_ref, mod_ref, second_ref, out_ref):
    proj = part_ref[0].astype(F32)
    for i in range(1, part_ref.shape[0]):
        proj += part_ref[i].astype(F32)
    second = (x_ref[...].astype(F32) + mod_ref[2:3, :] * proj).astype(BF)
    second_ref[...] = second
    h = layer_norm(second.astype(F32), mod_ref[3:4, :], mod_ref[4:5, :]).astype(BF)
    for i in range(out_ref.shape[0]):
        out_ref[i] = h


def second_norm(tokens, parts, mods):
    return pl.pallas_call(
        second_norm_kernel,
        out_shape=[
            jax.ShapeDtypeStruct(tokens.shape, BF),
            jax.ShapeDtypeStruct(parts.shape, BF),
        ],
        compiler_params=params(6),
        name="second_norm",
    )(tokens, parts, mods)


def ffn_kernel(h_ref, up_ref, down_ref, out_ref, hidden_ref):
    step = pl.program_id(0)
    part = up_ref.shape[-1]

    @pl.when(step < 2)
    def _():
        up = jnp.concatenate([up_ref[0, 0], up_ref[0, 1]], axis=1)
        hidden_ref[lax.rem(step, 2)] = jax.nn.gelu(
            lax.dot_general(h_ref[...], up, NN, preferred_element_type=F32),
            approximate=True,
        ).astype(BF)

    @pl.when(step >= 2)
    def _():
        hidden = jnp.concatenate([hidden_ref[0], hidden_ref[1]], axis=1)
        down = jnp.concatenate(
            [
                jnp.concatenate([down_ref[0, y, :part], down_ref[0, y, part:]], axis=1)
                for y in range(4)
            ],
            axis=0,
        )
        out_ref[...] = lax.dot_general(
            hidden, down, NN, preferred_element_type=F32
        ).astype(BF)


def feed_forward(h, weights):
    rows, width = h.shape
    part = weights.shape[3]
    return pl.pallas_call(
        ffn_kernel,
        grid=(4,),
        out_shape=jax.ShapeDtypeStruct((rows, width), BF),
        in_specs=[
            pl.BlockSpec((rows, width), lambda i: (0, 0)),
            pl.BlockSpec((1, 2, width, part), lambda i: (0, jnp.minimum(i, 1), 0, 0)),
            pl.BlockSpec((1, 4, 2 * part, part), lambda i: (1, 0, jnp.maximum(i - 2, 0), 0)),
        ],
        out_specs=pl.BlockSpec((rows, 2 * part), lambda i: (0, jnp.maximum(i - 2, 0))),
        scratch_shapes=[pltpu.VMEM((2, rows, 2 * part), BF)],
        compiler_params=params(58),
        name="feed_forward",
    )(h, weights, weights)


def last_kernel(second_ref, part_ref, mod_ref, w_ref, state_ref, vel_ref):
    ffn = part_ref[0].astype(F32)
    for i in range(1, part_ref.shape[0]):
        ffn += part_ref[i].astype(F32)
    state = (second_ref[...].astype(F32) + mod_ref[5:6, :] * ffn).astype(BF)
    state_ref[...] = state
    h = layer_norm(state.astype(F32), mod_ref[6:7, :], mod_ref[7:8, :]).astype(BF)
    vel_ref[...] = lax.dot_general(h, w_ref[...], NN, preferred_element_type=F32)


def last_stage(second, parts, mods, w_final):
    return pl.pallas_call(
        last_kernel,
        out_shape=[
            jax.ShapeDtypeStruct(second.shape, BF),
            jax.ShapeDtypeStruct((second.shape[0], w_final.shape[1]), F32),
        ],
        compiler_params=params(6),
        name="last_stage",
    )(second, parts, mods, w_final)


def on_device(
    image_tokens,
    latent,
    modulation,
    text_kv,
    text_len,
    timestep,
    w_qkv,
    w_out,
    w_up,
    w_down,
    w_final,
):
    tokens = image_tokens[0]
    mods = modulation[0]
    rows, width = tokens.shape
    core = lax.axis_index("core")
    pos = jnp.concatenate([jnp.stack([core, lax.axis_index("ty")]).astype(jnp.int32), text_len])
    swap2 = [(0, 1), (1, 0)]

    def to_lines(value, step):
        return lax.ppermute(value, "ty", [(i, (i + step) % 4) for i in range(4)])

    own_qkv = jnp.transpose(w_qkv, (1, 2, 0))
    half_kv = lax.dynamic_slice(own_qkv, (1, core * 48, 0), (2, 48, width))
    place = jnp.stack([core, lax.axis_index("zp")]).astype(jnp.int32)
    h1, quarter = first_norm_and_pack(place, tokens, mods, w_up, w_down, 4)
    ffn_full = lax.all_gather(quarter, ("core", "tx", "zp"), axis=0, tiled=False)
    ffn_full = ffn_full.reshape(2, 4, width, w_up.shape[1])
    h1, half_kv = lax.optimization_barrier((h1, half_kv))
    h1 = lax.all_to_all(h1, "tx", split_axis=0, concat_axis=0, tiled=True)
    near_kv = [to_lines(half_kv, step) for step in STRIDES]

    half_q = lax.dynamic_slice(own_qkv, (0, core * 48, 0), (1, 48, width))
    half_out = lax.dynamic_slice(w_out, (core * 48, 0), (48, width))
    half_qo = jnp.concatenate([half_q, half_out[None]])
    text = lax.dynamic_slice_in_dim(text_kv[0], lax.axis_index("tx") * 384, 384, 2)
    text = jnp.transpose(text, (1, 0, 2))
    far_kv = lax.ppermute(jnp.stack(near_kv), "core", swap2)
    h1, half_qo, text = lax.optimization_barrier((h1, half_qo, text))
    near_qo = [to_lines(half_qo, step) for step in STRIDES]
    h1 = h1.reshape(4 * rows, width)
    own_kv = project(pos, h1, own_qkv, 1, 2, 4, near_kv, far_kv)
    all_kv = lax.all_to_all(own_kv, "ty", split_axis=0, concat_axis=0, tiled=True)
    *near_qo, own_kv = lax.optimization_barrier((*near_qo, own_kv))
    far_qo = lax.ppermute(jnp.stack(near_qo), "core", swap2)
    query = project(pos, h1, own_qkv, 0, 1, 1, near_qo, far_qo)[0, 0]

    state = attention(pos, query, own_kv, text=text)
    attended = attention(pos, query, all_kv, state=state)

    partial = out_projection(pos, attended, w_out, near_qo, far_qo)
    partial = partial.reshape(4, rows, width)
    partial = lax.all_to_all(partial, "tx", split_axis=0, concat_axis=0, tiled=True)
    second, h2 = second_norm(tokens, partial, mods)
    h2 = lax.all_to_all(h2, "ty", split_axis=0, concat_axis=0, tiled=True)
    partial = feed_forward(h2.reshape(4 * rows, width), ffn_full).reshape(4, rows, width)
    partial = lax.all_to_all(partial, "ty", split_axis=0, concat_axis=0, tiled=True)
    state, velocity = last_stage(second, partial, mods, w_final)

    step_index = timestep[0]
    delta = sigma_at(step_index + 1) - sigma_at(step_index)
    moved = latent[0] + delta * velocity.reshape(rows // 2, 2 * velocity.shape[1])
    return (state[None], moved[None])


def solution(mesh):
    fine = Mesh(
        mesh.devices.reshape(mesh.shape["req"] // 4, 2, 2, 4, 4, mesh.shape["blk"]),
        ("zl", "zp", "core", "tx", "ty", "blk"),
    )
    group = ("zl", "zp", "core", "blk")
    tile = ("tx", "ty")
    in_specs = (
        P(group, tile, None),
        P(group, tile, None),
        P(group, None, None),
        P(group, None, None, None),
        P(group),
        P(group),
        P(None, None, tile),
        P(tile, None),
        P(None, tile),
        P(tile, None),
        P(),
    )
    out_specs = (P(group, tile, None), P(group, tile, None))
    return jax.shard_map(
        on_device, mesh=fine, in_specs=in_specs, out_specs=out_specs, check_vma=False
    )
```
